32 devices in a mesh: brick: 8 (over y, x, core), kvec: 4 (over z).
Axes of the slice: x: 2, y: 2, z: 4, core: 2. Of those that a mesh axis runs over, the one named last changes fastest.
Arguments:
- positions: float32 [2, 3, 1024], P(None, None, 'brick'), may hold values from -20 to 20
- moments: float32 [1024, 640], P('brick'), may hold values from -4 to 4
- adj_pos: float32 [3, 1024], P(None, 'brick'), may hold values from -1.8 to 1.8
- final_momentum_adjoint: float32 [3, 1024], P(None, 'brick'), may hold values from -6 to 6
- species: int32 [1024], P('brick'), may hold values from 0 to 5
- masses: float32 [6], replicated, may hold values from 1 to 16
- kint: int32 [1536, 3], P('kvec'), may hold values from -5 to 5
Outputs:
- pos_adjoint: float32 [3, 1024], P(None, 'brick')
- initial_momentum_adjoint: float32 [3, 1024], P(None, 'brick')
The draws below stay inside these ranges and needn't reach their ends.
All inputs are finite; a program needn't handle non-finite values.
Results may differ from the reference program's by a relative error of at most 0.0003.
Values sent between devices are 32-bit elements; how exact they have to be, the bound alone decides.
A program may use at most 64 MiB of HBM per device.

```python
import math
import jax
import jax.numpy as jnp
from jax import lax

C = 64
K = 1536
MOM = 10
NSPEC = 6
STEPS = 2
A_DEV = 128
ATOMS = 1024
N_BRICK = 8


def set_ends(values, key, low, top_value):
    dims = values.shape
    place = [jax.random.randint(jax.random.fold_in(key, axis), (), 0, dims[axis]) for axis in range(len(dims))]
    values = values.at[tuple(place)].set(low)
    longest = dims.index(max(dims))
    place[longest] = (place[longest] + 1) % dims[longest]
    return values.at[tuple(place)].set(top_value)


def levels(own_key, extent, pieces, smallest, high):
    def one(dim, parts):
        steps = jax.random.uniform(jax.random.fold_in(jax.random.fold_in(own_key, 6), dim), (parts,), jnp.float32, smallest / len(pieces), high / len(pieces))
        return jnp.repeat(jnp.exp(steps), extent[dim] // parts).reshape((-1,) + (1,) * (len(extent) - dim - 1))

    loudness = one(*pieces[0])
    for cut in pieces[1:]:
        loudness = loudness * one(*cut)
    return loudness


def noise(stream_key, dims, scale, limit, shards=(), kind=jnp.bfloat16):
    values = jax.random.normal(stream_key, dims, jnp.float32) * scale
    if len(shards) > 0:
        values = levels(stream_key, dims, shards, -0.22, 0.18) * values
    return jnp.clip(values, min=-limit, max=limit).astype(kind)


def setup_inputs(seed: int = 0) -> dict:
    key_list = jax.random.split(jax.random.key(seed), 8)
    positions = jnp.clip(jax.random.uniform(key_list[0], (STEPS, 3, ATOMS), jnp.float32, -20.0, 20.0) * levels(key_list[0], (STEPS, 3, ATOMS), ((2, 8),), -0.4, 0.0), -20.0, 20.0)
    moments = noise(key_list[1], (ATOMS, MOM * C), 0.3, 4.0, ((0, 8),), jnp.float32)
    adj_pos = noise(key_list[2], (3, ATOMS), 0.3, 1.8, ((1, 8),), jnp.float32)
    final_momentum_adjoint = noise(key_list[3], (3, ATOMS), 1.0, 6.0, ((1, 8),), jnp.float32)
    species = set_ends(jax.random.randint(key_list[4], (ATOMS,), 0, NSPEC), jax.random.fold_in(key_list[4], 1), 0, NSPEC - 1).astype(jnp.int32)
    masses = jnp.clip(jnp.exp(jax.random.uniform(key_list[5], (NSPEC,), jnp.float32, math.log(1.0), math.log(16.0))), 1.0, 16.0)
    kint = set_ends(jax.random.randint(key_list[6], (K, 3), -5, 6), jax.random.fold_in(key_list[6], 1), -5, 5).astype(jnp.int32)
    return {"positions": positions, "moments": moments, "adj_pos": adj_pos, "final_momentum_adjoint": final_momentum_adjoint, "species": species, "masses": masses, "kint": kint}


exact = lax.Precision.HIGHEST
wavevector_scale = 0.5
time_step = 0.5
energy_scale = 0.125

def coef_arrays(wavevector_phase):
    kx, ky, kz = (wavevector_phase[:, 0], wavevector_phase[:, 1], wavevector_phase[:, 2])
    ones = jnp.ones_like(kx)
    zeros = jnp.zeros_like(kx)
    acoef = jnp.stack([ones, zeros, zeros, zeros, -0.5 * kx * kx, -0.5 * ky * ky, -0.5 * kz * kz, -kx * ky, -kx * kz, -ky * kz], 1)
    bcoef = jnp.stack([zeros, kx, ky, kz, zeros, zeros, zeros, zeros, zeros, zeros], 1)
    return (acoef, bcoef)

def moment_sums(cos_w, sin_w, moments, acoef, bcoef):
    channels = moments.shape[1] // 10
    cos_part = jnp.dot(cos_w, moments, precision=exact).reshape(cos_w.shape[0], 10, channels)
    sine_component = jnp.dot(sin_w, moments, precision=exact).reshape(cos_w.shape[0], 10, channels)
    real_sum = jnp.einsum('km,kmc->kc', acoef, cos_part, precision=exact) - jnp.einsum('km,kmc->kc', bcoef, sine_component, precision=exact)
    imag_sum = jnp.einsum('km,kmc->kc', acoef, sine_component, precision=exact) + jnp.einsum('km,kmc->kc', bcoef, cos_part, precision=exact)
    return (real_sum, imag_sum)

def weave_terms(leading_dimension, trailing, acoef, bcoef):
    woven = leading_dimension[:, None, :] * acoef[:, :, None] + trailing[:, None, :] * bcoef[:, :, None]
    return woven.reshape(leading_dimension.shape[0], -1)

def tangent_force(wavevector_phase, k_weight, acoef, bcoef, factor, tangent, cosines, sines, k_dot_dir, moments, prefactor):
    factor_re, factor_im = factor
    tangent_re, tangent_im = tangent
    stacked = jnp.stack([weave_terms(tangent_im, -tangent_re, acoef, bcoef), weave_terms(tangent_re, tangent_im, acoef, bcoef), weave_terms(factor_re, factor_im, acoef, bcoef), weave_terms(factor_im, -factor_re, acoef, bcoef)])
    projected = jnp.einsum('jkf,af->jka', stacked, moments, precision=exact)
    inner_sum = cosines * projected[0] - sines * projected[1] - k_dot_dir * (cosines * projected[2] + sines * projected[3])
    return jnp.dot((k_weight[:, None] * wavevector_phase).T, inner_sum, precision=exact) * prefactor

def reference(positions, moments, adj_pos, final_momentum_adjoint, species, masses, kint):
    wavevector_phase = kint.astype(jnp.float32) * wavevector_scale
    ksq = lax.optimization_barrier(jnp.sum(wavevector_phase * wavevector_phase, 1))
    k_weight = jnp.exp(-ksq / 4.0) / jnp.maximum(ksq, 1.0)
    acoef, bcoef = coef_arrays(wavevector_phase)
    prefactor = energy_scale / math.sqrt(ATOMS)
    onehot = (species[None, :] == jnp.arange(NSPEC, dtype=jnp.int32)[:, None]).astype(jnp.float32)
    inv_mass = jnp.dot(1.0 / masses, onehot, precision=exact)
    mom_blocks = moments.reshape(N_BRICK, A_DEV, MOM * C)
    for step_index in reversed(range(STEPS)):
        pos_blocks = positions[step_index].reshape(3, N_BRICK, A_DEV).transpose(1, 0, 2)
        direction = final_momentum_adjoint * inv_mass
        dir_blocks = direction.reshape(3, N_BRICK, A_DEV).transpose(1, 0, 2)

        def block_phases(pos_b, dir_b):
            phase = jnp.dot(wavevector_phase, pos_b, precision=exact)
            return (jnp.cos(phase), jnp.sin(phase), jnp.dot(wavevector_phase, dir_b, precision=exact))

        def add_block(carry, item):
            pos_b, mom_b, dir_b = item
            cosines, sines, k_dot_dir = block_phases(pos_b, dir_b)
            f_re, f_im = moment_sums(cosines, sines, mom_b, acoef, bcoef)
            t_re, t_im = moment_sums(k_dot_dir * cosines, k_dot_dir * sines, mom_b, acoef, bcoef)
            return ((carry[0] + f_re, carry[1] + f_im, carry[2] - t_im, carry[3] + t_re), None)
        zeros = jnp.zeros((K, C), jnp.float32)
        totals, _ = lax.scan(add_block, (zeros, zeros, zeros, zeros), (pos_blocks, mom_blocks, dir_blocks))

        def block_force(item):
            pos_b, mom_b, dir_b = item
            cosines, sines, k_dot_dir = block_phases(pos_b, dir_b)
            return tangent_force(wavevector_phase, k_weight, acoef, bcoef, (totals[0], totals[1]), (totals[2], totals[3]), cosines, sines, k_dot_dir, mom_b, prefactor)
        forces = lax.map(block_force, (pos_blocks, mom_blocks, dir_blocks))
        force = forces.transpose(1, 0, 2).reshape(3, ATOMS)
        adj_pos = adj_pos - time_step * force
        final_momentum_adjoint = final_momentum_adjoint + time_step * adj_pos
    return (adj_pos, final_momentum_adjoint)
```

```python
import functools
import math

import jax
import jax.numpy as jnp
import numpy as np
from jax import lax
from jax.experimental import pallas as pl
from jax.experimental.pallas import tpu as pltpu
from jax.sharding import PartitionSpec as P

exact = lax.Precision.HIGHEST
wavevector_scale = 0.5
time_step = 0.5
energy_scale = 0.125


def coef_arrays(wavevector_phase):
    kx, ky, kz = (wavevector_phase[:, 0], wavevector_phase[:, 1], wavevector_phase[:, 2])
    ones = jnp.ones_like(kx)
    zeros = jnp.zeros_like(kx)
    acoef = jnp.stack(
        [
            ones,
            zeros,
            zeros,
            zeros,
            -0.5 * kx * kx,
            -0.5 * ky * ky,
            -0.5 * kz * kz,
            -kx * ky,
            -kx * kz,
            -ky * kz,
        ],
        1,
    )
    bcoef = jnp.stack([zeros, kx, ky, kz, zeros, zeros, zeros, zeros, zeros, zeros], 1)
    return (acoef, bcoef)


def moment_sums(cos_w, sin_w, moments, acoef, bcoef):
    channels = moments.shape[1] // 10
    cos_part = jnp.dot(cos_w, moments, precision=exact).reshape(cos_w.shape[0], 10, channels)
    sine_component = jnp.dot(sin_w, moments, precision=exact).reshape(cos_w.shape[0], 10, channels)
    real_sum = jnp.einsum("km,kmc->kc", acoef, cos_part, precision=exact) - jnp.einsum(
        "km,kmc->kc", bcoef, sine_component, precision=exact
    )
    imag_sum = jnp.einsum("km,kmc->kc", acoef, sine_component, precision=exact) + jnp.einsum(
        "km,kmc->kc", bcoef, cos_part, precision=exact
    )
    return (real_sum, imag_sum)


def weave_terms(leading_dimension, trailing, acoef, bcoef):
    woven = (
        leading_dimension[:, None, :] * acoef[:, :, None] + trailing[:, None, :] * bcoef[:, :, None]
    )
    return woven.reshape(leading_dimension.shape[0], -1)


def tangent_force(
    wavevector_phase,
    k_weight,
    acoef,
    bcoef,
    factor,
    tangent,
    cosines,
    sines,
    k_dot_dir,
    moments,
    prefactor,
):
    factor_re, factor_im = factor
    tangent_re, tangent_im = tangent
    stacked = jnp.stack(
        [
            weave_terms(tangent_im, -tangent_re, acoef, bcoef),
            weave_terms(tangent_re, tangent_im, acoef, bcoef),
            weave_terms(factor_re, factor_im, acoef, bcoef),
            weave_terms(factor_im, -factor_re, acoef, bcoef),
        ]
    )
    projected = jnp.einsum("jkf,af->jka", stacked, moments, precision=exact)
    inner_sum = (
        cosines * projected[0]
        - sines * projected[1]
        - k_dot_dir * (cosines * projected[2] + sines * projected[3])
    )
    return jnp.dot((k_weight[:, None] * wavevector_phase).T, inner_sum, precision=exact) * prefactor


def plain_local(positions, moments, adj_pos, final_momentum_adjoint, species, masses, kint):
    wavevector_phase = kint.astype(jnp.float32) * wavevector_scale
    ksq = jnp.sum(wavevector_phase * wavevector_phase, 1)
    k_weight = jnp.exp(-ksq / 4.0) / jnp.maximum(ksq, 1.0)
    acoef, bcoef = coef_arrays(wavevector_phase)
    prefactor = energy_scale / math.sqrt(positions.shape[2] * lax.axis_size("brick"))
    onehot = (species[None, :] == jnp.arange(masses.shape[0], dtype=jnp.int32)[:, None]).astype(
        jnp.float32
    )
    inv_mass = jnp.dot(1.0 / masses, onehot, precision=exact)
    num_steps = positions.shape[0]

    def step_phases(step_index):
        phase = jnp.dot(wavevector_phase, positions[step_index], precision=exact)
        return (jnp.cos(phase), jnp.sin(phase))

    phase_list = [step_phases(step_index) for step_index in range(num_steps)]
    for step_index in reversed(range(num_steps)):
        cosines, sines = phase_list[step_index]
        direction = final_momentum_adjoint * inv_mass
        k_dot_dir = jnp.dot(wavevector_phase, direction, precision=exact)
        tangent_real_part, tan_im = moment_sums(
            k_dot_dir * cosines, k_dot_dir * sines, moments, acoef, bcoef
        )
        fac_re, fac_im = moment_sums(cosines, sines, moments, acoef, bcoef)
        summed_terms = lax.psum((fac_re, fac_im, -tan_im, tangent_real_part), "brick")
        factor = (summed_terms[0], summed_terms[1])
        tangent = (summed_terms[2], summed_terms[3])
        partial_force = tangent_force(
            wavevector_phase,
            k_weight,
            acoef,
            bcoef,
            factor,
            tangent,
            cosines,
            sines,
            k_dot_dir,
            moments,
            prefactor,
        )
        force = lax.psum(partial_force, "kvec")
        adj_pos = adj_pos - time_step * force
        final_momentum_adjoint = final_momentum_adjoint + time_step * adj_pos
    return (adj_pos, final_momentum_adjoint)


def plain(mesh):
    placed = (
        P(None, None, "brick"),
        P("brick", None),
        P(None, "brick"),
        P(None, "brick"),
        P("brick"),
        P(),
        P("kvec", None),
    )
    return jax.shard_map(
        plain_local,
        mesh=mesh,
        in_specs=placed,
        out_specs=(P(None, "brick"), P(None, "brick")),
        check_vma=False,
    )


MESH = pl.DeviceIdType.MESH
GROUP = 8
MOM = 10
LANES = 128
USED = MOM * 8
F32, BF16 = jnp.float32, jnp.bfloat16
two_over_pi = 2.0 / math.pi
half_pi_parts = (1.5703125, 4.837512969970703125e-4, 7.549789948768648e-8)

TOP = 5
PAIRS = [(0, b) for b in range(TOP + 1)] + [
    (a, b) for a in range(1, TOP + 1) for b in range(-TOP, TOP + 1)
]
HALF = 64
ALONG_Z = [0] + [c for top in range(1, TOP + 1) for c in (top, -top)]
SLOTS = len(ALONG_Z)
OPS = 6
SUMS = SLOTS * OPS * 8
CHUNK = 256


def grid_tables(prefactor):
    scale = wavevector_scale
    a = np.zeros(HALF)
    b = np.zeros(HALF)
    a[: len(PAIRS)] = [pair[0] for pair in PAIRS]
    b[: len(PAIRS)] = [pair[1] for pair in PAIRS]
    kx, ky = scale * a, scale * b
    along = np.broadcast_to(np.stack([kx, ky])[:, :, None], (2, HALF, LANES))
    lane_x, lane_y = np.tile(kx, 2), np.tile(ky, 2)
    sign = np.where(np.arange(LANES) < HALF, -1.0, 1.0)
    lanes = np.zeros((8, LANES))
    lanes[:6] = [
        lane_x,
        lane_y,
        -0.5 * lane_x**2,
        -0.5 * lane_y**2,
        -lane_x * lane_y,
        sign,
    ]
    weights = np.zeros((16, LANES))
    maps = np.zeros((4, SLOTS, HALF, LANES))
    lane = np.arange(LANES)
    room = (LANES - USED) // 8
    one = np.where(lane < USED, lane // 8, (lane - USED) // 8)
    two = np.where(
        lane < USED,
        lane // 8,
        np.where(lane < USED + (MOM - room) * 8, room + (lane - USED) // 8, MOM),
    )
    for slot, c in enumerate(ALONG_Z):
        kz = scale * c + 0.0 * kx
        ksq = kx**2 + ky**2 + kz**2
        weights[slot] = np.tile(np.exp(-ksq / 4.0) / np.maximum(ksq, 1.0), 2) * prefactor
        zero = 0.0 * kx
        acoef = np.stack(
            [zero + 1, zero, zero, zero]
            + [-0.5 * kx**2, -0.5 * ky**2, -0.5 * kz**2, -kx * ky, -kx * kz, -ky * kz]
            + [zero],
            1,
        )
        bcoef = np.stack([zero, kx, ky, kz] + [zero] * 7, 1)
        maps[0, slot], maps[1, slot] = acoef[:, one], bcoef[:, one]
        maps[2, slot], maps[3, slot] = acoef[:, two], bcoef[:, two]
    small = np.concatenate([along.reshape(2 * HALF, LANES), lanes, weights])
    return small.astype(np.float32), maps.reshape(4, SLOTS * HALF, LANES).astype(np.float32)


def sin_cos(phase):
    n = jnp.round(phase * two_over_pi)
    r = phase - n * half_pi_parts[0]
    r = r - n * half_pi_parts[1]
    r = r - n * half_pi_parts[2]
    q = n.astype(jnp.int32)
    z = r * r
    s = r + r * z * (-1.6666654611e-1 + z * (8.3321608736e-3 + z * -1.9515295891e-4))
    c = 1.0 - 0.5 * z + z * z * (
        4.166664568298827e-2 + z * (-1.388731625493765e-3 + z * 2.443315711809948e-5)
    )
    odd = (q & 1) == 1
    sine = jnp.where(odd, c, s)
    cosine = jnp.where(odd, s, c)
    sine = jnp.where((q & 2) == 2, -sine, sine)
    cosine = jnp.where(((q + 1) & 2) == 2, -cosine, cosine)
    return sine, cosine


def split(x):
    high = x.astype(BF16)
    return high, (x - high.astype(F32)).astype(BF16)


def wide(x, copies):
    return jnp.concatenate([x] * copies, axis=1)


def dot_rows(x, y):
    return lax.dot_general(x, y, (((1,), (1,)), ((), ())), preferred_element_type=F32)


def kernel(
    kvecs,
    pos_hbm,
    mom_hbm,
    adj_hbm,
    fma_hbm,
    spec_hbm,
    mass_hbm,
    kint_hbm,
    small_hbm,
    maps_hbm,
    out_adj,
    out_fma,
    pos_ref,
    mom_ref,
    adj_ref,
    fma_ref,
    spec_ref,
    mass_ref,
    kint_ref,
    small,
    maps,
    pack,
    rows,
    sent,
    moments,
    counts,
    counted,
    xy,
    ztab,
    lmat,
    rhigh,
    rlow,
    sums,
    opr,
    w2,
    proj,
    acc,
    hess,
    dirs,
    gather,
    gathered,
    total,
    part,
    bricks,
    load_sem,
    send_sem,
    recv_sem,
    zsend_sem,
    zrecv_sem,
):
    me = lax.axis_index("brick")
    mev = lax.axis_index("kvec")
    atoms = LANES * GROUP

    def flip(off):
        other = me
        for bit in (1, 2, 4):
            if off & bit:
                other = other + bit - 2 * bit * lax.rem(lax.div(me, bit), 2)
        return other

    loads = []
    for at, (src, dst) in enumerate(
        (
            (mom_hbm, mom_ref),
            (pos_hbm, pos_ref),
            (fma_hbm, fma_ref),
            (adj_hbm, adj_ref),
            (spec_hbm, spec_ref),
            (mass_hbm, mass_ref),
            (kint_hbm, kint_ref),
            (small_hbm, small),
            (maps_hbm, maps),
        )
    ):
        loads.append(pltpu.make_async_copy(src, dst, load_sem.at[at]))
        loads[-1].start()

    barrier = pltpu.get_barrier_semaphore()
    for off in range(1, GROUP):
        pl.semaphore_signal(barrier, inc=1, device_id=(flip(off), mev), device_id_type=MESH)
    for over in range(1, kvecs):
        pl.semaphore_signal(
            barrier, inc=1, device_id=(me, lax.rem(mev + over, kvecs)), device_id_type=MESH
        )

    for load in loads[1:6]:
        load.wait()
    species = spec_ref[...]
    mass = jnp.ones(species.shape, F32)
    for kind in range(mass_ref.shape[0]):
        mass = jnp.where(species == kind, mass_ref[kind], mass)
    pack[...] = jnp.zeros_like(pack)
    for axis in range(3):
        pack[axis : axis + 1, :] = pos_ref[axis, 0:1]
        pack[3 + axis : 4 + axis, :] = pos_ref[axis, 1:2]
    pack[6:9, :] = fma_ref[...]
    pack[9:12, :] = adj_ref[...]
    pack[12:13, :] = 1.0 / mass
    rows[:, 0:LANES] = pack[...]

    loads[0].wait()
    for piece in range(mom_ref.shape[1] // LANES):
        turned = mom_ref[:, piece * LANES : (piece + 1) * LANES].T
        sent[2 * piece : 2 * piece + 2] = turned.reshape(2, GROUP, 8, LANES)

    loads[6].wait()
    ka, kb, kc = kint_ref[0:1, :], kint_ref[1:2, :], kint_ref[2:3, :]
    turn = (ka < 0) | ((ka == 0) & (kb < 0))
    ka, kb, kc = (jnp.where(turn, -k, k) for k in (ka, kb, kc))
    pair = jnp.where(ka == 0, kb, (TOP + 1) + (ka - 1) * (2 * TOP + 1) + kb + TOP)
    slot = jnp.where(kc > 0, 2 * kc - 1, -2 * kc)
    here = kint_ref.shape[1]
    pair_row = lax.broadcasted_iota(jnp.int32, (LANES, here), 0)
    pair_row = jnp.where(pair_row < HALF, pair_row, pair_row - HALF)
    slot_row = lax.broadcasted_iota(jnp.int32, (16, here), 0)
    counts[...] = dot_rows(
        (slot_row == slot).astype(F32).astype(BF16), (pair_row == pair).astype(F32).astype(BF16)
    )

    pl.semaphore_wait(barrier, GROUP - 1 + kvecs - 1)
    copies = {}
    for off in range(1, GROUP):
        copies[0, off] = pltpu.make_async_remote_copy(
            src_ref=pack,
            dst_ref=rows.at[:, pl.ds(off * LANES, LANES)],
            send_sem=send_sem.at[0, off],
            recv_sem=recv_sem.at[0, off],
            device_id=(flip(off), mev),
            device_id_type=MESH,
        )
        copies[0, off].start()
    for off in (6, 7, 2, 3, 4, 5, 1):
        copies[1, off] = pltpu.make_async_remote_copy(
            src_ref=sent.at[:, flip(off)],
            dst_ref=moments.at[:, :, pl.ds(off * LANES, LANES)],
            send_sem=send_sem.at[1, off],
            recv_sem=recv_sem.at[1, off],
            device_id=(flip(off), mev),
            device_id_type=MESH,
        )
        copies[1, off].start()
    zcopies = []
    for over in range(1, kvecs):
        zcopies.append(
            pltpu.make_async_remote_copy(
                src_ref=counts,
                dst_ref=counted.at[over],
                send_sem=zsend_sem.at[over],
                recv_sem=zrecv_sem.at[over],
                device_id=(me, lax.rem(mev + over, kvecs)),
                device_id_type=MESH,
            )
        )
        zcopies[-1].start()
    moments[:, :, 0:LANES] = sent[:, pl.ds(me, 1)].reshape(MOM, 8, LANES)

    loads[7].wait()
    loads[8].wait()
    for off in range(1, GROUP):
        copies[0, off].wait_recv()
    lane_x, lane_y = small[128:129], small[129:130]
    lane_xx, lane_yy, lane_xy = small[130:131], small[131:132], small[132:133]
    sign = small[133:134]

    def along_x(at, size, copies_wide):
        return wide(small[pl.ds(at, size)], copies_wide)

    def along_y(at, size, copies_wide):
        return wide(small[pl.ds(HALF + at, size)], copies_wide)

    def make_phases(step):
        turns = lax.broadcasted_iota(jnp.int32, (8, atoms), 0).astype(F32) * wavevector_scale
        sine, cosine = sin_cos(turns * rows[3 * step + 2 : 3 * step + 3, :])
        ztab[step, 0:8] = cosine
        ztab[step, 8:16] = sine

        @pl.loop(0, HALF // 16)
        def _(chunk):
            at = pl.multiple_of(chunk * 16, 16)
            phase = along_x(at, 16, GROUP) * rows[3 * step : 3 * step + 1, :] + along_y(
                at, 16, GROUP
            ) * rows[3 * step + 1 : 3 * step + 2, :]
            sine, cosine = sin_cos(phase)
            xy[step, 0, pl.ds(at, 16)] = cosine
            xy[step, 1, pl.ds(at, 16)] = sine
            store_split(step, 0, at, cosine, sine)

    def store_split(step, block, at, real, imag):
        base = block * 256
        for which, part_here in enumerate((real, imag)):
            high, low = split(part_here)
            lmat[step, pl.ds(base + which * HALF + at, 16)] = high
            lmat[step, pl.ds(base + LANES + which * HALF + at, 16)] = low

    def make_tangents(step, direction):
        @pl.loop(0, HALF // 16)
        def _(chunk):
            at = pl.multiple_of(chunk * 16, 16)
            real, imag = xy[step, 0, pl.ds(at, 16)], xy[step, 1, pl.ds(at, 16)]
            k_dot = along_x(at, 16, GROUP) * direction(0) + along_y(at, 16, GROUP) * direction(1)
            store_split(step, 1, at, -k_dot * imag, k_dot * real)
            store_split(step, 2, at, direction(2) * real, direction(2) * imag)

    def make_terms(step, first, width):
        here = pl.ds(first, width)
        q = [moments[m, :, here] for m in range(MOM)]

        def store(group, ops):
            for two in range(OPS // 2):
                both = jnp.concatenate([ops[2 * two], ops[2 * two + 1]], axis=0)
                at = group * OPS * 8 + two * 16
                rhigh[step, at : at + 16, here], rlow[step, at : at + 16, here] = split(both)

        store(0, [q[0], q[1], q[2], q[4], q[5], q[7]])
        for turn in range(1, TOP + 1):
            kz = turn * wavevector_scale
            c, s = ztab[step, turn : turn + 1, here], ztab[step, 8 + turn : 9 + turn, here]
            kc, ks = kz * c, kz * s
            charge = q[0] - (0.5 * kz * kz) * q[6]
            store(
                2 * turn - 1,
                [
                    charge * c - q[3] * ks,
                    q[1] * c - q[8] * ks,
                    q[2] * c - q[9] * ks,
                    q[4] * c,
                    q[5] * c,
                    q[7] * c,
                ],
            )
            store(
                2 * turn,
                [
                    charge * s + q[3] * kc,
                    q[1] * s + q[8] * kc,
                    q[2] * s + q[9] * kc,
                    q[4] * s,
                    q[5] * s,
                    q[7] * s,
                ],
            )

    def dots(step, first, width, low_row, high_row):
        here = pl.ds(first, width)
        across = lmat[step, low_row:high_row, here]
        return dot_rows(rhigh[step, :, here], across) + dot_rows(rlow[step, :, here], across)

    def combine(block):
        base = block * 256
        out = []
        for group in range(SLOTS):
            op = []
            for which in range(OPS):
                at = (group * OPS + which) * 8
                op.append(
                    sums[at : at + 8, base : base + LANES]
                    + sums[at : at + 8, base + LANES : base + 2 * LANES]
                )
            turned = pltpu.roll(lane_x * op[1] + lane_y * op[2], HALF, 1) * sign
            out.append(op[0] + turned + lane_xx * op[3] + lane_yy * op[4] + lane_xy * op[5])
        return out

    def tangent_sums():
        t1, g = combine(1), combine(2)
        out = [t1[0]]
        for turn in range(1, TOP + 1):
            kz = turn * wavevector_scale
            out.append(t1[2 * turn - 1] - kz * g[2 * turn])
            out.append(t1[2 * turn] + kz * g[2 * turn - 1])
        return out

    lane = lax.broadcasted_iota(jnp.int32, (1, LANES), 1)

    def operand(slot, real, imag):
        here = slice(slot * HALF, (slot + 1) * HALF)
        one = real * maps[0, here] + imag * maps[1, here]
        two = real * maps[2, here] + imag * maps[3, here]
        top = one.astype(BF16)
        rest = jnp.where(lane < USED, one - top.astype(F32), two).astype(BF16)
        return jnp.concatenate([top, rest], axis=1)

    def project(place, parts, weights):
        for slot, c in enumerate(ALONG_Z):
            if c == 0:
                value = parts[0]
            else:
                turn = abs(c)
                turned = pltpu.roll(parts[2 * turn], HALF, 1) * sign
                value = parts[2 * turn - 1] + (turned if c > 0 else -turned)
            value = value * weights[slot : slot + 1]
            tile = jnp.concatenate([value] * 16, axis=0).T
            real, imag = tile[0:HALF], tile[HALF:]
            at = slot * 2 * HALF
            opr[place, at : at + HALF] = operand(slot, real, imag)
            opr[place, at + HALF : at + 2 * HALF] = operand(slot, imag, -real)
        proj[place] = jnp.dot(opr[place], w2[...], preferred_element_type=F32)

    def around(step, at, here):
        real, imag = xy[step, 0, pl.ds(at, 8), here], xy[step, 1, pl.ds(at, 8), here]
        yield 0, real, imag
        for turn in range(1, TOP + 1):
            c, s = ztab[step, turn : turn + 1, here], ztab[step, 8 + turn : 9 + turn, here]
            rc, is_, ic, rs = real * c, imag * s, imag * c, real * s
            yield turn, (rc - is_, ic + rs), (rc + is_, ic - rs)

    def projected(place, slot, at, here):
        base = slot * 2 * HALF
        return (
            proj[place, pl.ds(pl.multiple_of(base + at, 8), 8), here],
            proj[place, pl.ds(pl.multiple_of(base + HALF + at, 8), 8), here],
        )

    def tangent_value(wave, place, slot, at, here):
        first, second = projected(place, slot, at, here)
        return wave[0] * second - wave[1] * first

    def factor_value(wave, place, slot, at, here):
        first, second = projected(place, slot, at, here)
        return wave[0] * first + wave[1] * second

    pieces = CHUNK // LANES

    def each_chunk(body):
        @pl.loop(0, (HALF // 8) * (atoms // CHUNK))
        def _(index):
            at = pl.multiple_of(lax.rem(index, HALF // 8) * 8, 8)
            here = pl.ds(pl.multiple_of(lax.div(index, HALF // 8) * CHUNK, CHUNK), CHUNK)
            body(at, here)

    def force_sums(step, direction, with_factor):
        acc[...] = jnp.zeros_like(acc)

        def body(at, here):
            kx, ky = along_x(at, 8, pieces), along_y(at, 8, pieces)
            if with_factor:
                dz = direction(2, here)
                k_dot = kx * direction(0, here) + ky * direction(1, here)
            waves = around(step, at, here)
            _, real, imag = next(waves)
            flat = tangent_value((real, imag), 1, 0, at, here)
            if with_factor:
                flat = flat - k_dot * factor_value((real, imag), 0, 0, at, here)
            tilt = 0.0
            for turn, plus, minus in waves:
                kz = turn * wavevector_scale
                up = tangent_value(plus, 1, 2 * turn - 1, at, here)
                down = tangent_value(minus, 1, 2 * turn, at, here)
                if with_factor:
                    kdz = kz * dz
                    up = up - (k_dot + kdz) * factor_value(plus, 0, 2 * turn - 1, at, here)
                    down = down - (k_dot - kdz) * factor_value(minus, 0, 2 * turn, at, here)
                flat = flat + (up + down)
                tilt = tilt + kz * (up - down)
            acc[0, :, here] += kx * flat
            acc[1, :, here] += ky * flat
            acc[2, :, here] += tilt

        each_chunk(body)

    def hessian_sums(step):
        hess[...] = jnp.zeros_like(hess)

        def body(at, here):
            kx, ky = along_x(at, 8, pieces), along_y(at, 8, pieces)
            waves = around(step, at, here)
            _, real, imag = next(waves)
            flat = factor_value((real, imag), 0, 0, at, here)
            tilt, bend = 0.0, 0.0
            for turn, plus, minus in waves:
                kz = turn * wavevector_scale
                up = factor_value(plus, 0, 2 * turn - 1, at, here)
                down = factor_value(minus, 0, 2 * turn, at, here)
                both = up + down
                flat = flat + both
                tilt = tilt + kz * (up - down)
                bend = bend + (kz * kz) * both
            fx, fy = kx * flat, ky * flat
            hess[0, :, here] += kx * fx
            hess[1, :, here] += kx * fy
            hess[2, :, here] += kx * tilt
            hess[3, :, here] += ky * fy
            hess[4, :, here] += ky * tilt
            hess[5, :, here] += bend

        each_chunk(body)

    last = 1
    inv_mass = rows[12:13, :]
    dirs[0:3, :] = rows[6:9, :] * inv_mass
    make_phases(last)
    make_tangents(last, lambda axis: dirs[axis : axis + 1, :])
    make_phases(0)

    order = (0, 2, 4, 6)
    for place, off in enumerate(order):
        for one in (off, off + 1):
            if one > 0:
                copies[1, one].wait_recv()
        make_terms(last, off * LANES, 2 * LANES)
        piece = dots(last, off * LANES, 2 * LANES, 0, 768)
        sums[...] = piece if place == 0 else sums[...] + piece
        here = pl.ds(off * LANES, 2 * LANES)
        q_high, q_low = split(moments[:, :, here].reshape(USED, 2 * LANES))
        fits = LANES - USED
        w2[0:USED, here] = q_high
        w2[USED:LANES, here] = q_low[0:fits]
        w2[LANES : LANES + USED, here] = q_high
        w2[LANES + USED : LANES + 2 * USED - fits, here] = q_low[fits:]
        w2[LANES + 2 * USED - fits :, here] = jnp.zeros((16, 2 * LANES), BF16)

    for copy in zcopies:
        copy.wait_recv()
    count = counts[...]
    for over in range(1, kvecs):
        count = count + counted[over]
    weights = count * small[136:152]

    project(0, combine(0), weights)
    project(1, tangent_sums(), weights)
    force_sums(last, lambda axis, here: dirs[axis : axis + 1, here], True)

    for axis in range(3):
        out = jnp.sum(acc[axis], axis=0, keepdims=True)
        for off in range(GROUP):
            gather[pl.ds(axis * GROUP + flip(off), 1), :] = out[:, off * LANES : (off + 1) * LANES]
    for off in range(1, GROUP):
        copies[2, off] = pltpu.make_async_remote_copy(
            src_ref=gather,
            dst_ref=gathered.at[off],
            send_sem=send_sem.at[2, off],
            recv_sem=recv_sem.at[2, off],
            device_id=(flip(off), mev),
            device_id_type=MESH,
        )
        copies[2, off].start()

    for off in order:
        make_terms(0, off * LANES, 2 * LANES)
    sums[:, 0:256] = dots(0, 0, atoms, 0, 256)
    project(0, combine(0), weights)
    hessian_sums(0)
    second = [jnp.sum(hess[row], axis=0, keepdims=True) for row in range(6)]

    out = gather[...]
    for off in range(1, GROUP):
        copies[2, off].wait_recv()
        out = out + gathered[off]
    total[...] = out
    forces = []
    for axis in range(3):
        forces.append(
            jnp.concatenate(
                [total[pl.ds(axis * GROUP + flip(off), 1), :] for off in range(GROUP)], axis=1
            )
        )
    adj = [rows[9 + axis : 10 + axis, :] - time_step * forces[axis] for axis in range(3)]
    fma = [rows[6 + axis : 7 + axis, :] + time_step * adj[axis] for axis in range(3)]
    for axis in range(3):
        dirs[axis : axis + 1, :] = fma[axis] * inv_mass

    make_tangents(0, lambda axis: dirs[axis : axis + 1, :])
    sums[:, 256:768] = dots(0, 0, atoms, 256, 768)
    project(1, tangent_sums(), weights)
    force_sums(0, None, False)
    direction = [dirs[axis : axis + 1, :] for axis in range(3)]
    places = ((0, 1, 2), (1, 3, 4), (2, 4, 5))
    part[...] = jnp.zeros_like(part)
    for axis in range(3):
        out = jnp.sum(acc[axis], axis=0, keepdims=True)
        for other in range(3):
            out = out - second[places[axis][other]] * direction[other]
        for off in range(GROUP):
            part[off, axis : axis + 1, :] = out[:, off * LANES : (off + 1) * LANES]
    for off in range(1, GROUP):
        copies[3, off] = pltpu.make_async_remote_copy(
            src_ref=part.at[off],
            dst_ref=bricks.at[off],
            send_sem=send_sem.at[3, off],
            recv_sem=recv_sem.at[3, off],
            device_id=(flip(off), mev),
            device_id_type=MESH,
        )
        copies[3, off].start()
    out = part[0]
    for off in range(1, GROUP):
        copies[3, off].wait_recv()
        out = out + bricks[off]
    for axis in range(3):
        adj_here = adj[axis][:, 0:LANES] - time_step * out[axis : axis + 1]
        out_adj[axis : axis + 1, :] = adj_here
        out_fma[axis : axis + 1, :] = fma[axis][:, 0:LANES] + time_step * adj_here
    for copy in copies.values():
        copy.wait_send()
    for copy in zcopies:
        copy.wait_send()


def fused(kvecs, positions, moments, adj_pos, final_momentum_adjoint, species, masses, kint):
    steps, _, here = positions.shape
    kdev = kint.shape[0]
    atoms = here * GROUP
    small, maps = grid_tables(energy_scale / math.sqrt(atoms))
    vmem = pl.BlockSpec(memory_space=pltpu.VMEM)
    hbm = pl.BlockSpec(memory_space=pltpu.HBM)
    result = jax.ShapeDtypeStruct((3, here), F32)
    points = SLOTS * HALF
    return pl.pallas_call(
        functools.partial(kernel, kvecs),
        out_shape=(result, result),
        in_specs=[hbm] * 9,
        out_specs=(vmem, vmem),
        scratch_shapes=[
            pltpu.VMEM((3, steps, here), F32),
            pltpu.VMEM(moments.shape, F32),
            pltpu.VMEM((3, here), F32),
            pltpu.VMEM((3, here), F32),
            pltpu.VMEM((1, here), jnp.int32),
            pltpu.SMEM(masses.shape, F32),
            pltpu.VMEM((3, kdev), jnp.int32),
            pltpu.VMEM(small.shape, F32),
            pltpu.VMEM(maps.shape, F32),
            pltpu.VMEM((16, here), F32),
            pltpu.VMEM((16, atoms), F32),
            pltpu.VMEM((MOM, GROUP, 8, here), F32),
            pltpu.VMEM((MOM, 8, atoms), F32),
            pltpu.VMEM((16, LANES), F32),
            pltpu.VMEM((kvecs, 16, LANES), F32),
            pltpu.VMEM((steps, 2, HALF, atoms), F32),
            pltpu.VMEM((steps, 16, atoms), F32),
            pltpu.VMEM((steps, 768, atoms), BF16),
            pltpu.VMEM((steps, SUMS, atoms), BF16),
            pltpu.VMEM((steps, SUMS, atoms), BF16),
            pltpu.VMEM((SUMS, 768), F32),
            pltpu.VMEM((2, 2 * points, 2 * LANES), BF16),
            pltpu.VMEM((2 * LANES, atoms), BF16),
            pltpu.VMEM((2, 2 * points, atoms), F32),
            pltpu.VMEM((3, 8, atoms), F32),
            pltpu.VMEM((6, 8, atoms), F32),
            pltpu.VMEM((8, atoms), F32),
            pltpu.VMEM((3 * GROUP, here), F32),
            pltpu.VMEM((GROUP, 3 * GROUP, here), F32),
            pltpu.VMEM((3 * GROUP, here), F32),
            pltpu.VMEM((GROUP, 4, here), F32),
            pltpu.VMEM((GROUP, 4, here), F32),
            pltpu.SemaphoreType.DMA((9,)),
            pltpu.SemaphoreType.DMA((4, GROUP)),
            pltpu.SemaphoreType.DMA((4, GROUP)),
            pltpu.SemaphoreType.DMA((kvecs,)),
            pltpu.SemaphoreType.DMA((kvecs,)),
        ],
        compiler_params=pltpu.CompilerParams(
            collective_id=0, has_side_effects=True, vmem_limit_bytes=48 << 20
        ),
    )(
        positions.transpose(1, 0, 2),
        moments,
        adj_pos,
        final_momentum_adjoint,
        species.reshape(1, here),
        masses,
        kint.T,
        small,
        maps,
    )


def solution(mesh):
    bricks, kvecs = mesh.shape["brick"], mesh.shape["kvec"]
    if bricks != GROUP:
        return plain(mesh)
    placed = (
        P(None, None, "brick"),
        P("brick", None),
        P(None, "brick"),
        P(None, "brick"),
        P("brick"),
        P(),
        P("kvec", None),
    )
    return jax.shard_map(
        functools.partial(fused, kvecs),
        mesh=mesh,
        in_specs=placed,
        out_specs=(P(None, "brick"), P(None, "brick")),
        check_vma=False,
    )
```

```python
import functools
import math

import jax
import jax.numpy as jnp
import numpy as np
from jax import lax
from jax.experimental import pallas as pl
from jax.experimental.pallas import tpu as pltpu
from jax.sharding import PartitionSpec as P

exact = lax.Precision.HIGHEST
wavevector_scale = 0.5
time_step = 0.5
energy_scale = 0.125


def coef_arrays(wavevector_phase):
    kx, ky, kz = (wavevector_phase[:, 0], wavevector_phase[:, 1], wavevector_phase[:, 2])
    ones = jnp.ones_like(kx)
    zeros = jnp.zeros_like(kx)
    acoef = jnp.stack(
        [
            ones,
            zeros,
            zeros,
            zeros,
            -0.5 * kx * kx,
            -0.5 * ky * ky,
            -0.5 * kz * kz,
            -kx * ky,
            -kx * kz,
            -ky * kz,
        ],
        1,
    )
    bcoef = jnp.stack([zeros, kx, ky, kz, zeros, zeros, zeros, zeros, zeros, zeros], 1)
    return (acoef, bcoef)


def moment_sums(cos_w, sin_w, moments, acoef, bcoef):
    channels = moments.shape[1] // 10
    cos_part = jnp.dot(cos_w, moments, precision=exact).reshape(cos_w.shape[0], 10, channels)
    sine_component = jnp.dot(sin_w, moments, precision=exact).reshape(cos_w.shape[0], 10, channels)
    real_sum = jnp.einsum("km,kmc->kc", acoef, cos_part, precision=exact) - jnp.einsum(
        "km,kmc->kc", bcoef, sine_component, precision=exact
    )
    imag_sum = jnp.einsum("km,kmc->kc", acoef, sine_component, precision=exact) + jnp.einsum(
        "km,kmc->kc", bcoef, cos_part, precision=exact
    )
    return (real_sum, imag_sum)


def weave_terms(leading_dimension, trailing, acoef, bcoef):
    woven = (
        leading_dimension[:, None, :] * acoef[:, :, None] + trailing[:, None, :] * bcoef[:, :, None]
    )
    return woven.reshape(leading_dimension.shape[0], -1)


def tangent_force(
    wavevector_phase,
    k_weight,
    acoef,
    bcoef,
    factor,
    tangent,
    cosines,
    sines,
    k_dot_dir,
    moments,
    prefactor,
):
    factor_re, factor_im = factor
    tangent_re, tangent_im = tangent
    stacked = jnp.stack(
        [
            weave_terms(tangent_im, -tangent_re, acoef, bcoef),
            weave_terms(tangent_re, tangent_im, acoef, bcoef),
            weave_terms(factor_re, factor_im, acoef, bcoef),
            weave_terms(factor_im, -factor_re, acoef, bcoef),
        ]
    )
    projected = jnp.einsum("jkf,af->jka", stacked, moments, precision=exact)
    inner_sum = (
        cosines * projected[0]
        - sines * projected[1]
        - k_dot_dir * (cosines * projected[2] + sines * projected[3])
    )
    return jnp.dot((k_weight[:, None] * wavevector_phase).T, inner_sum, precision=exact) * prefactor


def plain_local(positions, moments, adj_pos, final_momentum_adjoint, species, masses, kint):
    wavevector_phase = kint.astype(jnp.float32) * wavevector_scale
    ksq = jnp.sum(wavevector_phase * wavevector_phase, 1)
    k_weight = jnp.exp(-ksq / 4.0) / jnp.maximum(ksq, 1.0)
    acoef, bcoef = coef_arrays(wavevector_phase)
    prefactor = energy_scale / math.sqrt(positions.shape[2] * lax.axis_size("brick"))
    onehot = (species[None, :] == jnp.arange(masses.shape[0], dtype=jnp.int32)[:, None]).astype(
        jnp.float32
    )
    inv_mass = jnp.dot(1.0 / masses, onehot, precision=exact)
    num_steps = positions.shape[0]

    def step_phases(step_index):
        phase = jnp.dot(wavevector_phase, positions[step_index], precision=exact)
        return (jnp.cos(phase), jnp.sin(phase))

    phase_list = [step_phases(step_index) for step_index in range(num_steps)]
    for step_index in reversed(range(num_steps)):
        cosines, sines = phase_list[step_index]
        direction = final_momentum_adjoint * inv_mass
        k_dot_dir = jnp.dot(wavevector_phase, direction, precision=exact)
        tangent_real_part, tan_im = moment_sums(
            k_dot_dir * cosines, k_dot_dir * sines, moments, acoef, bcoef
        )
        fac_re, fac_im = moment_sums(cosines, sines, moments, acoef, bcoef)
        summed_terms = lax.psum((fac_re, fac_im, -tan_im, tangent_real_part), "brick")
        factor = (summed_terms[0], summed_terms[1])
        tangent = (summed_terms[2], summed_terms[3])
        partial_force = tangent_force(
            wavevector_phase,
            k_weight,
            acoef,
            bcoef,
            factor,
            tangent,
            cosines,
            sines,
            k_dot_dir,
            moments,
            prefactor,
        )
        force = lax.psum(partial_force, "kvec")
        adj_pos = adj_pos - time_step * force
        final_momentum_adjoint = final_momentum_adjoint + time_step * adj_pos
    return (adj_pos, final_momentum_adjoint)


def plain(mesh):
    placed = (
        P(None, None, "brick"),
        P("brick", None),
        P(None, "brick"),
        P(None, "brick"),
        P("brick"),
        P(),
        P("kvec", None),
    )
    return jax.shard_map(
        plain_local,
        mesh=mesh,
        in_specs=placed,
        out_specs=(P(None, "brick"), P(None, "brick")),
        check_vma=False,
    )


MESH = pl.DeviceIdType.MESH
GROUP = 8
MOM = 10
LANES = 128
USED = MOM * 8
F32, BF16 = jnp.float32, jnp.bfloat16
two_over_pi = 2.0 / math.pi
half_pi_parts = (1.5703125, 4.837512969970703125e-4, 7.549789948768648e-8)

TOP = 5
PAIRS = [(0, b) for b in range(TOP + 1)] + [
    (a, b) for a in range(1, TOP + 1) for b in range(-TOP, TOP + 1)
]
HALF = 64
SIDE = HALF // 2
ALONG_Z = [0] + [c for top in range(1, TOP + 1) for c in (top, -top)]
SLOTS = len(ALONG_Z)
OPS = 6
SUMS = SLOTS * OPS * 8
CHUNK = 256
HIGH, LOW = (128, 256, 384), (0, 512, 640)


def grid_tables(prefactor):
    scale = wavevector_scale
    a = np.zeros(HALF)
    b = np.zeros(HALF)
    a[: len(PAIRS)] = [pair[0] for pair in PAIRS]
    b[: len(PAIRS)] = [pair[1] for pair in PAIRS]
    kx, ky = scale * a, scale * b
    along = np.broadcast_to(np.stack([kx, ky])[:, :, None], (2, HALF, LANES))
    lane_x, lane_y = np.tile(kx, 2), np.tile(ky, 2)
    sign = np.where(np.arange(LANES) < HALF, -1.0, 1.0)
    lanes = np.zeros((8, LANES))
    lanes[:6] = [
        lane_x,
        lane_y,
        -0.5 * lane_x**2,
        -0.5 * lane_y**2,
        -lane_x * lane_y,
        sign,
    ]
    weights = np.zeros((16, LANES))
    maps = np.zeros((4, SLOTS, HALF, LANES))
    lane = np.arange(LANES)
    room = (LANES - USED) // 8
    one = np.where(lane < USED, lane // 8, (lane - USED) // 8)
    two = np.where(
        lane < USED,
        lane // 8,
        np.where(lane < USED + (MOM - room) * 8, room + (lane - USED) // 8, MOM),
    )
    for slot, c in enumerate(ALONG_Z):
        kz = scale * c + 0.0 * kx
        ksq = kx**2 + ky**2 + kz**2
        weights[slot] = np.tile(np.exp(-ksq / 4.0) / np.maximum(ksq, 1.0), 2) * prefactor
        zero = 0.0 * kx
        acoef = np.stack(
            [zero + 1, zero, zero, zero]
            + [-0.5 * kx**2, -0.5 * ky**2, -0.5 * kz**2, -kx * ky, -kx * kz, -ky * kz]
            + [zero],
            1,
        )
        bcoef = np.stack([zero, kx, ky, kz] + [zero] * 7, 1)
        maps[0, slot], maps[1, slot] = acoef[:, one], bcoef[:, one]
        maps[2, slot], maps[3, slot] = acoef[:, two], bcoef[:, two]
    small = np.concatenate([along.reshape(2 * HALF, LANES), lanes, weights])
    return small.astype(np.float32), maps.reshape(4, SLOTS * HALF, LANES).astype(np.float32)


def sin_cos(phase):
    n = jnp.round(phase * two_over_pi)
    r = phase - n * half_pi_parts[0]
    r = r - n * half_pi_parts[1]
    r = r - n * half_pi_parts[2]
    q = n.astype(jnp.int32)
    z = r * r
    s = r + r * z * (-1.6666654611e-1 + z * (8.3321608736e-3 + z * -1.9515295891e-4))
    c = 1.0 - 0.5 * z + z * z * (
        4.166664568298827e-2 + z * (-1.388731625493765e-3 + z * 2.443315711809948e-5)
    )
    odd = (q & 1) == 1
    sine = jnp.where(odd, c, s)
    cosine = jnp.where(odd, s, c)
    sine = jnp.where((q & 2) == 2, -sine, sine)
    cosine = jnp.where(((q + 1) & 2) == 2, -cosine, cosine)
    return sine, cosine


def split(x):
    high = x.astype(BF16)
    return high, (x - high.astype(F32)).astype(BF16)


def wide(x, copies):
    return jnp.concatenate([x] * copies, axis=1)


def dot_rows(x, y):
    return lax.dot_general(x, y, (((1,), (1,)), ((), ())), preferred_element_type=F32)


def kernel(
    kvecs,
    pos_hbm,
    mom_hbm,
    adj_hbm,
    fma_hbm,
    spec_hbm,
    mass_hbm,
    kint_hbm,
    small_hbm,
    maps_hbm,
    out_ref,
    pos_ref,
    mom_ref,
    adj_ref,
    fma_ref,
    spec_ref,
    mass_ref,
    kint_ref,
    small,
    maps,
    pack,
    rows,
    sent,
    moments,
    counts,
    counted,
    tally,
    xy,
    ztab,
    lmat,
    rhigh,
    rlow,
    sums,
    opr,
    w2,
    proj_a,
    proj_b,
    acc,
    hess,
    dirs,
    gather,
    gathered,
    total,
    part,
    bricks,
    load_sem,
    send_sem,
    recv_sem,
    zsend_sem,
    zrecv_sem,
):
    me = lax.axis_index("brick")
    mev = lax.axis_index("kvec")
    atoms = LANES * GROUP

    def flip(off):
        other = me
        for bit in (1, 2, 4):
            if off & bit:
                other = other + bit - 2 * bit * lax.rem(lax.div(me, bit), 2)
        return other

    loads = []
    for at, (src, dst) in enumerate(
        (
            (mom_hbm, mom_ref),
            (pos_hbm, pos_ref),
            (fma_hbm, fma_ref),
            (adj_hbm, adj_ref),
            (spec_hbm, spec_ref),
            (mass_hbm, mass_ref),
            (kint_hbm, kint_ref),
            (small_hbm, small),
            (maps_hbm, maps),
        )
    ):
        loads.append(pltpu.make_async_copy(src, dst, load_sem.at[at]))
        loads[-1].start()

    barrier = pltpu.get_barrier_semaphore()
    for off in range(1, GROUP):
        pl.semaphore_signal(barrier, inc=1, device_id=(flip(off), mev), device_id_type=MESH)
    leader = me == 0
    beyond = kvecs - 1

    @pl.when(leader)
    def _():
        for over in range(1, kvecs):
            pl.semaphore_signal(
                barrier, inc=1, device_id=(me, lax.rem(mev + over, kvecs)), device_id_type=MESH
            )

    for load in loads[1:6]:
        load.wait()
    species = spec_ref[...]
    mass = jnp.ones(species.shape, F32)
    for kind in range(mass_ref.shape[0]):
        mass = jnp.where(species == kind, mass_ref[kind], mass)
    pack[...] = jnp.zeros_like(pack)
    for axis in range(3):
        pack[axis : axis + 1, :] = pos_ref[axis, 0:1]
        pack[3 + axis : 4 + axis, :] = pos_ref[axis, 1:2]
    pack[6:9, :] = fma_ref[...]
    pack[9:12, :] = adj_ref[...]
    pack[12:13, :] = 1.0 / mass
    rows[:, 0:LANES] = pack[...]

    loads[0].wait()
    for piece in range(mom_ref.shape[1] // LANES):
        turned = mom_ref[:, piece * LANES : (piece + 1) * LANES].T
        sent[2 * piece : 2 * piece + 2] = turned.reshape(2, GROUP, 8, LANES)

    loads[6].wait()
    ka, kb, kc = kint_ref[0:1, :], kint_ref[1:2, :], kint_ref[2:3, :]
    turn = (ka < 0) | ((ka == 0) & (kb < 0))
    ka, kb, kc = (jnp.where(turn, -k, k) for k in (ka, kb, kc))
    pair = jnp.where(ka == 0, kb, (TOP + 1) + (ka - 1) * (2 * TOP + 1) + kb + TOP)
    slot = jnp.where(kc > 0, 2 * kc - 1, -2 * kc)
    here = kint_ref.shape[1]
    pair_row = lax.broadcasted_iota(jnp.int32, (LANES, here), 0)
    pair_row = jnp.where(pair_row < HALF, pair_row, pair_row - HALF)
    slot_row = lax.broadcasted_iota(jnp.int32, (16, here), 0)
    counts[...] = dot_rows(
        (slot_row == slot).astype(F32).astype(BF16), (pair_row == pair).astype(F32).astype(BF16)
    )

    pl.semaphore_wait(barrier, GROUP - 1 + jnp.where(leader, beyond, 0))
    copies = {}
    for off in range(1, GROUP):
        copies[0, off] = pltpu.make_async_remote_copy(
            src_ref=pack,
            dst_ref=rows.at[:, pl.ds(off * LANES, LANES)],
            send_sem=send_sem.at[0, off],
            recv_sem=recv_sem.at[0, off],
            device_id=(flip(off), mev),
            device_id_type=MESH,
        )
        copies[0, off].start()
    for off in (6, 7, 2, 3, 4, 5, 1):
        copies[1, off] = pltpu.make_async_remote_copy(
            src_ref=sent.at[:, flip(off)],
            dst_ref=moments.at[:, :, pl.ds(off * LANES, LANES)],
            send_sem=send_sem.at[1, off],
            recv_sem=recv_sem.at[1, off],
            device_id=(flip(off), mev),
            device_id_type=MESH,
        )
        copies[1, off].start()

    def count_copy(over):
        return pltpu.make_async_remote_copy(
            src_ref=counts,
            dst_ref=counted.at[over],
            send_sem=zsend_sem.at[over],
            recv_sem=zrecv_sem.at[over],
            device_id=(me, lax.rem(mev + over, kvecs)),
            device_id_type=MESH,
        )

    def tally_copy(off):
        return pltpu.make_async_remote_copy(
            src_ref=tally,
            dst_ref=tally,
            send_sem=send_sem.at[4, off],
            recv_sem=recv_sem.at[4, 0],
            device_id=(flip(off), mev),
            device_id_type=MESH,
        )

    @pl.when(leader)
    def _():
        for over in range(1, kvecs):
            count_copy(over).start()

    moments[:, :, 0:LANES] = sent[:, pl.ds(me, 1)].reshape(MOM, 8, LANES)

    loads[7].wait()
    loads[8].wait()
    for off in range(1, GROUP):
        copies[0, off].wait_recv()
    lane_x, lane_y = small[128:129], small[129:130]
    lane_xx, lane_yy, lane_xy = small[130:131], small[131:132], small[132:133]
    sign = small[133:134]

    def along_x(at, size, copies_wide):
        return wide(small[pl.ds(at, size)], copies_wide)

    def along_y(at, size, copies_wide):
        return wide(small[pl.ds(HALF + at, size)], copies_wide)

    def make_phases(step):
        turns = lax.broadcasted_iota(jnp.int32, (8, atoms), 0).astype(F32) * wavevector_scale
        sine, cosine = sin_cos(turns * rows[3 * step + 2 : 3 * step + 3, :])
        ztab[step, 0:8] = cosine
        ztab[step, 8:16] = sine

        @pl.loop(0, HALF // 16)
        def _(chunk):
            at = pl.multiple_of(chunk * 16, 16)
            phase = along_x(at, 16, GROUP) * rows[3 * step : 3 * step + 1, :] + along_y(
                at, 16, GROUP
            ) * rows[3 * step + 1 : 3 * step + 2, :]
            sine, cosine = sin_cos(phase)
            xy[step, 0, pl.ds(at, 16)] = cosine
            xy[step, 1, pl.ds(at, 16)] = sine
            store_split(step, 0, at, cosine, sine)

    def store_split(step, block, at, real, imag):
        for which, part_here in enumerate((real, imag)):
            high, low = split(part_here)
            lmat[step, pl.ds(HIGH[block] + which * HALF + at, 16)] = high
            lmat[step, pl.ds(LOW[block] + which * HALF + at, 16)] = low

    def make_tangents(step, direction):
        @pl.loop(0, HALF // 16)
        def _(chunk):
            at = pl.multiple_of(chunk * 16, 16)
            real, imag = xy[step, 0, pl.ds(at, 16)], xy[step, 1, pl.ds(at, 16)]
            k_dot = along_x(at, 16, GROUP) * direction(0) + along_y(at, 16, GROUP) * direction(1)
            store_split(step, 1, at, -k_dot * imag, k_dot * real)
            store_split(step, 2, at, direction(2) * real, direction(2) * imag)

    def make_terms(step, first, width):
        here = pl.ds(first, width)
        q = [moments[m, :, here] for m in range(MOM)]

        def store(group, ops):
            for two in range(OPS // 2):
                both = jnp.concatenate([ops[2 * two], ops[2 * two + 1]], axis=0)
                at = group * OPS * 8 + two * 16
                rhigh[step, at : at + 16, here], rlow[step, at : at + 16, here] = split(both)

        store(0, [q[0], q[1], q[2], q[4], q[5], q[7]])
        for turn in range(1, TOP + 1):
            kz = turn * wavevector_scale
            c, s = ztab[step, turn : turn + 1, here], ztab[step, 8 + turn : 9 + turn, here]
            kc, ks = kz * c, kz * s
            charge = q[0] - (0.5 * kz * kz) * q[6]
            store(
                2 * turn - 1,
                [
                    charge * c - q[3] * ks,
                    q[1] * c - q[8] * ks,
                    q[2] * c - q[9] * ks,
                    q[4] * c,
                    q[5] * c,
                    q[7] * c,
                ],
            )
            store(
                2 * turn,
                [
                    charge * s + q[3] * kc,
                    q[1] * s + q[8] * kc,
                    q[2] * s + q[9] * kc,
                    q[4] * s,
                    q[5] * s,
                    q[7] * s,
                ],
            )

    def dots(step, first, width, begin, end, add):
        here = pl.ds(first, width)
        value = dot_rows(rhigh[step, :, here], lmat[step, begin:end, here])
        sums[:, begin:end] = sums[:, begin:end] + value if add else value
        begin, end = max(begin, HIGH[0]), min(end, LOW[1])
        sums[:, begin:end] += dot_rows(rlow[step, :, here], lmat[step, begin:end, here])

    def combine(block):
        high, low = HIGH[block], LOW[block]
        out = []
        for group in range(SLOTS):
            op = []
            for which in range(OPS):
                at = (group * OPS + which) * 8
                op.append(
                    sums[at : at + 8, high : high + LANES] + sums[at : at + 8, low : low + LANES]
                )
            turned = pltpu.roll(lane_x * op[1] + lane_y * op[2], HALF, 1) * sign
            out.append(op[0] + turned + lane_xx * op[3] + lane_yy * op[4] + lane_xy * op[5])
        return out

    def tangent_sums():
        t1, g = combine(1), combine(2)
        out = [t1[0]]
        for turn in range(1, TOP + 1):
            kz = turn * wavevector_scale
            out.append(t1[2 * turn - 1] - kz * g[2 * turn])
            out.append(t1[2 * turn] + kz * g[2 * turn - 1])
        return out

    lane = lax.broadcasted_iota(jnp.int32, (1, LANES), 1)

    def operand(slot, real, imag):
        here = slice(slot * HALF, (slot + 1) * HALF)
        one = real * maps[0, here] + imag * maps[1, here]
        two = real * maps[2, here] + imag * maps[3, here]
        top = one.astype(BF16)
        rest = jnp.where(lane < USED, one - top.astype(F32), two).astype(BF16)
        return jnp.concatenate([top, rest], axis=1)

    def project(place, parts, weights):
        for slot, c in enumerate(ALONG_Z):
            if c == 0:
                value = parts[0]
            else:
                turn = abs(c)
                turned = pltpu.roll(parts[2 * turn], HALF, 1) * sign
                value = parts[2 * turn - 1] + (turned if c > 0 else -turned)
            value = value * weights[slot : slot + 1]
            tile = jnp.concatenate([value] * 16, axis=0).T
            real, imag = tile[0:HALF], tile[HALF:]
            first, second = operand(slot, real, imag), operand(slot, imag, -real)
            at = slot * 2 * SIDE
            for side in range(2):
                here = slice(side * SIDE, (side + 1) * SIDE)
                opr[side, place, at : at + SIDE] = first[here]
                opr[side, place, at + SIDE : at + 2 * SIDE] = second[here]

    def around(step, at, here):
        real, imag = xy[step, 0, at : at + 8, here], xy[step, 1, at : at + 8, here]
        yield 0, real, imag
        for turn in range(1, TOP + 1):
            c, s = ztab[step, turn : turn + 1, here], ztab[step, 8 + turn : 9 + turn, here]
            rc, is_, ic, rs = real * c, imag * s, imag * c, real * s
            yield turn, (rc - is_, ic + rs), (rc + is_, ic - rs)

    def projected(buffer, place, slot, row):
        at = (place * SLOTS + slot) * 2 * SIDE + row
        return buffer[at : at + 8], buffer[at + SIDE : at + SIDE + 8]

    def tangent_value(wave, buffer, place, slot, row):
        first, second = projected(buffer, place, slot, row)
        return wave[0] * second - wave[1] * first

    def factor_value(wave, buffer, place, slot, row):
        first, second = projected(buffer, place, slot, row)
        return wave[0] * first + wave[1] * second

    pieces = CHUNK // LANES

    def force_terms(step, buffer, side, here, direction, with_factor):
        place = 1 if with_factor else 0
        total_x, total_y, total_z = 0.0, 0.0, 0.0
        if with_factor:
            dx, dy, dz = (direction(axis, here) for axis in range(3))
        for row in range(0, SIDE, 8):
            at = side * SIDE + row
            kx, ky = along_x(at, 8, pieces), along_y(at, 8, pieces)
            waves = around(step, at, here)
            _, real, imag = next(waves)
            flat = tangent_value((real, imag), buffer, place, 0, row)
            if with_factor:
                k_dot = kx * dx + ky * dy
                flat = flat - k_dot * factor_value((real, imag), buffer, 0, 0, row)
            tilt = 0.0
            for turn, plus, minus in waves:
                kz = turn * wavevector_scale
                up = tangent_value(plus, buffer, place, 2 * turn - 1, row)
                down = tangent_value(minus, buffer, place, 2 * turn, row)
                if with_factor:
                    kdz = kz * dz
                    up = up - (k_dot + kdz) * factor_value(plus, buffer, 0, 2 * turn - 1, row)
                    down = down - (k_dot - kdz) * factor_value(minus, buffer, 0, 2 * turn, row)
                flat = flat + (up + down)
                tilt = tilt + kz * (up - down)
            total_x, total_y, total_z = total_x + kx * flat, total_y + ky * flat, total_z + tilt
        acc[0, :, here] += total_x
        acc[1, :, here] += total_y
        acc[2, :, here] += total_z

    def hessian_terms(step, buffer, side, here):
        totals = [0.0] * 6
        for row in range(0, SIDE, 8):
            at = side * SIDE + row
            kx, ky = along_x(at, 8, pieces), along_y(at, 8, pieces)
            waves = around(step, at, here)
            _, real, imag = next(waves)
            flat = factor_value((real, imag), buffer, 0, 0, row)
            tilt, bend = 0.0, 0.0
            for turn, plus, minus in waves:
                kz = turn * wavevector_scale
                up = factor_value(plus, buffer, 0, 2 * turn - 1, row)
                down = factor_value(minus, buffer, 0, 2 * turn, row)
                both = up + down
                flat = flat + both
                tilt = tilt + kz * (up - down)
                bend = bend + (kz * kz) * both
            fx, fy = kx * flat, ky * flat
            for entry, value in enumerate((kx * fx, kx * fy, kx * tilt, ky * fy, ky * tilt, bend)):
                totals[entry] = totals[entry] + value
        for entry in range(6):
            hess[entry, :, here] += totals[entry]

    def sweep(places, terms):
        count = len(places) * SLOTS * 2 * SIDE
        buffers = (proj_a.at[0:count], proj_b.at[0:count])

        def fill(side, first):
            left = opr[side, places[0] : places[-1] + 1].reshape(count, 2 * LANES)
            buffers[side][...] = jnp.dot(
                left, w2[:, pl.ds(first, CHUNK)], preferred_element_type=F32
            )

        fill(0, 0)

        @pl.loop(0, atoms // CHUNK)
        def _(index):
            first = pl.multiple_of(index * CHUNK, CHUNK)
            after = pl.multiple_of(lax.rem(index + 1, atoms // CHUNK) * CHUNK, CHUNK)
            here = pl.ds(first, CHUNK)
            fill(1, first)
            terms(buffers[0], 0, here)
            fill(0, after)
            terms(buffers[1], 1, here)

    last = 1
    inv_mass = rows[12:13, :]
    dirs[0:3, :] = rows[6:9, :] * inv_mass
    make_phases(last)
    make_tangents(last, lambda axis: dirs[axis : axis + 1, :])
    make_phases(0)

    order = (0, 2, 4, 6)
    for place, off in enumerate(order):
        if place == 1:

            @pl.when(leader)
            def _():
                count = counts[...]
                for over in range(1, kvecs):
                    count_copy(over).wait_recv()
                    count = count + counted[over]
                tally[...] = count
                for other in range(1, GROUP):
                    tally_copy(other).start()

        for one in (off, off + 1):
            if one > 0:
                copies[1, one].wait_recv()
        make_terms(last, off * LANES, 2 * LANES)
        dots(last, off * LANES, 2 * LANES, 0, 768, place > 0)
        here = pl.ds(off * LANES, 2 * LANES)
        q_high, q_low = split(moments[:, :, here].reshape(USED, 2 * LANES))
        fits = LANES - USED
        w2[0:USED, here] = q_high
        w2[USED:LANES, here] = q_low[0:fits]
        w2[LANES : LANES + USED, here] = q_high
        w2[LANES + USED : LANES + 2 * USED - fits, here] = q_low[fits:]
        w2[LANES + 2 * USED - fits :, here] = jnp.zeros((16, 2 * LANES), BF16)

    @pl.when(me != 0)
    def _():
        tally_copy(1).wait_recv()

    weights = tally[...] * small[136:152]

    project(0, combine(0), weights)
    project(1, tangent_sums(), weights)
    acc[...] = jnp.zeros_like(acc)
    sweep(
        (0, 1),
        lambda buffer, side, here: force_terms(
            last, buffer, side, here, lambda axis, here: dirs[axis : axis + 1, here], True
        ),
    )

    for axis in range(3):
        out = jnp.sum(acc[axis], axis=0, keepdims=True)
        for off in range(GROUP):
            gather[pl.ds(axis * GROUP + flip(off), 1), :] = out[:, off * LANES : (off + 1) * LANES]
    for off in range(1, GROUP):
        copies[2, off] = pltpu.make_async_remote_copy(
            src_ref=gather,
            dst_ref=gathered.at[off],
            send_sem=send_sem.at[2, off],
            recv_sem=recv_sem.at[2, off],
            device_id=(flip(off), mev),
            device_id_type=MESH,
        )
        copies[2, off].start()

    for off in order:
        make_terms(0, off * LANES, 2 * LANES)
    dots(0, 0, atoms, 0, 256, False)
    project(0, combine(0), weights)
    hess[...] = jnp.zeros_like(hess)
    sweep((0,), lambda buffer, side, here: hessian_terms(0, buffer, side, here))
    second = [jnp.sum(hess[row], axis=0, keepdims=True) for row in range(6)]

    out = gather[...]
    for off in range(1, GROUP):
        copies[2, off].wait_recv()
        out = out + gathered[off]
    total[...] = out
    forces = []
    for axis in range(3):
        forces.append(
            jnp.concatenate(
                [total[pl.ds(axis * GROUP + flip(off), 1), :] for off in range(GROUP)], axis=1
            )
        )
    adj = [rows[9 + axis : 10 + axis, :] - time_step * forces[axis] for axis in range(3)]
    fma = [rows[6 + axis : 7 + axis, :] + time_step * adj[axis] for axis in range(3)]
    for axis in range(3):
        dirs[axis : axis + 1, :] = fma[axis] * inv_mass

    make_tangents(0, lambda axis: dirs[axis : axis + 1, :])
    dots(0, 0, atoms, 256, 768, False)
    project(1, tangent_sums(), weights)
    acc[...] = jnp.zeros_like(acc)
    sweep((1,), lambda buffer, side, here: force_terms(0, buffer, side, here, None, False))
    direction = [dirs[axis : axis + 1, :] for axis in range(3)]
    places = ((0, 1, 2), (1, 3, 4), (2, 4, 5))
    part[...] = jnp.zeros_like(part)
    for axis in range(3):
        out = jnp.sum(acc[axis], axis=0, keepdims=True)
        for other in range(3):
            out = out - second[places[axis][other]] * direction[other]
        for off in range(GROUP):
            part[off, axis : axis + 1, :] = out[:, off * LANES : (off + 1) * LANES]
    for off in range(1, GROUP):
        copies[3, off] = pltpu.make_async_remote_copy(
            src_ref=part.at[off],
            dst_ref=bricks.at[off],
            send_sem=send_sem.at[3, off],
            recv_sem=recv_sem.at[3, off],
            device_id=(flip(off), mev),
            device_id_type=MESH,
        )
        copies[3, off].start()
    out = part[0]
    for off in range(1, GROUP):
        copies[3, off].wait_recv()
        out = out + bricks[off]
    out_ref[0:4, :] = out
    for axis in range(3):
        out_ref[4 + axis : 5 + axis, :] = adj[axis][:, 0:LANES]
        out_ref[8 + axis : 9 + axis, :] = fma[axis][:, 0:LANES]
    for copy in copies.values():
        copy.wait_send()

    @pl.when(leader)
    def _():
        for over in range(1, kvecs):
            count_copy(over).wait_send()
        for off in range(1, GROUP):
            tally_copy(off).wait_send()


def fused(kvecs, positions, moments, adj_pos, final_momentum_adjoint, species, masses, kint):
    steps, _, here = positions.shape
    kdev = kint.shape[0]
    atoms = here * GROUP
    small, maps = grid_tables(energy_scale / math.sqrt(atoms))
    vmem = pl.BlockSpec(memory_space=pltpu.VMEM)
    hbm = pl.BlockSpec(memory_space=pltpu.HBM)
    points = SLOTS * HALF
    last = pl.pallas_call(
        functools.partial(kernel, kvecs),
        out_shape=jax.ShapeDtypeStruct((16, here), F32),
        in_specs=[hbm] * 9,
        out_specs=vmem,
        scratch_shapes=[
            pltpu.VMEM((3, steps, here), F32),
            pltpu.VMEM(moments.shape, F32),
            pltpu.VMEM((3, here), F32),
            pltpu.VMEM((3, here), F32),
            pltpu.VMEM((1, here), jnp.int32),
            pltpu.SMEM(masses.shape, F32),
            pltpu.VMEM((3, kdev), jnp.int32),
            pltpu.VMEM(small.shape, F32),
            pltpu.VMEM(maps.shape, F32),
            pltpu.VMEM((16, here), F32),
            pltpu.VMEM((16, atoms), F32),
            pltpu.VMEM((MOM, GROUP, 8, here), F32),
            pltpu.VMEM((MOM, 8, atoms), F32),
            pltpu.VMEM((16, LANES), F32),
            pltpu.VMEM((kvecs, 16, LANES), F32),
            pltpu.VMEM((16, LANES), F32),
            pltpu.VMEM((steps, 2, HALF, atoms), F32),
            pltpu.VMEM((steps, 16, atoms), F32),
            pltpu.VMEM((steps, 768, atoms), BF16),
            pltpu.VMEM((steps, SUMS, atoms), BF16),
            pltpu.VMEM((steps, SUMS, atoms), BF16),
            pltpu.VMEM((SUMS, 768), F32),
            pltpu.VMEM((2, 2, points, 2 * LANES), BF16),
            pltpu.VMEM((2 * LANES, atoms), BF16),
            pltpu.VMEM((2 * points, CHUNK), F32),
            pltpu.VMEM((2 * points, CHUNK), F32),
            pltpu.VMEM((3, 8, atoms), F32),
            pltpu.VMEM((6, 8, atoms), F32),
            pltpu.VMEM((8, atoms), F32),
            pltpu.VMEM((3 * GROUP, here), F32),
            pltpu.VMEM((GROUP, 3 * GROUP, here), F32),
            pltpu.VMEM((3 * GROUP, here), F32),
            pltpu.VMEM((GROUP, 4, here), F32),
            pltpu.VMEM((GROUP, 4, here), F32),
            pltpu.SemaphoreType.DMA((9,)),
            pltpu.SemaphoreType.DMA((5, GROUP)),
            pltpu.SemaphoreType.DMA((5, GROUP)),
            pltpu.SemaphoreType.DMA((kvecs,)),
            pltpu.SemaphoreType.DMA((kvecs,)),
        ],
        compiler_params=pltpu.CompilerParams(
            collective_id=0, has_side_effects=True, vmem_limit_bytes=60 << 20
        ),
    )(
        positions.transpose(1, 0, 2),
        moments,
        adj_pos,
        final_momentum_adjoint,
        species.reshape(1, here),
        masses,
        kint.T,
        small,
        maps,
    )
    adj = last[4:7] - time_step * last[0:3]
    return adj, last[8:11] + time_step * adj


def solution(mesh):
    bricks, kvecs = mesh.shape["brick"], mesh.shape["kvec"]
    if bricks != GROUP:
        return plain(mesh)
    placed = (
        P(None, None, "brick"),
        P("brick", None),
        P(None, "brick"),
        P(None, "brick"),
        P("brick"),
        P(),
        P("kvec", None),
    )
    return jax.shard_map(
        functools.partial(fused, kvecs),
        mesh=mesh,
        in_specs=placed,
        out_specs=(P(None, "brick"), P(None, "brick")),
        check_vma=False,
    )
```

```python
import functools
import math

import jax
import jax.numpy as jnp
import numpy as np
from jax import lax
from jax.experimental import pallas as pl
from jax.experimental.pallas import tpu as pltpu
from jax.sharding import PartitionSpec as P

exact = lax.Precision.HIGHEST
wavevector_scale = 0.5
time_step = 0.5
energy_scale = 0.125


def coef_arrays(wavevector_phase):
    kx, ky, kz = (wavevector_phase[:, 0], wavevector_phase[:, 1], wavevector_phase[:, 2])
    ones = jnp.ones_like(kx)
    zeros = jnp.zeros_like(kx)
    acoef = jnp.stack(
        [
            ones,
            zeros,
            zeros,
            zeros,
            -0.5 * kx * kx,
            -0.5 * ky * ky,
            -0.5 * kz * kz,
            -kx * ky,
            -kx * kz,
            -ky * kz,
        ],
        1,
    )
    bcoef = jnp.stack([zeros, kx, ky, kz, zeros, zeros, zeros, zeros, zeros, zeros], 1)
    return (acoef, bcoef)


def moment_sums(cos_w, sin_w, moments, acoef, bcoef):
    channels = moments.shape[1] // 10
    cos_part = jnp.dot(cos_w, moments, precision=exact).reshape(cos_w.shape[0], 10, channels)
    sine_component = jnp.dot(sin_w, moments, precision=exact).reshape(cos_w.shape[0], 10, channels)
    real_sum = jnp.einsum("km,kmc->kc", acoef, cos_part, precision=exact) - jnp.einsum(
        "km,kmc->kc", bcoef, sine_component, precision=exact
    )
    imag_sum = jnp.einsum("km,kmc->kc", acoef, sine_component, precision=exact) + jnp.einsum(
        "km,kmc->kc", bcoef, cos_part, precision=exact
    )
    return (real_sum, imag_sum)


def weave_terms(leading_dimension, trailing, acoef, bcoef):
    woven = (
        leading_dimension[:, None, :] * acoef[:, :, None] + trailing[:, None, :] * bcoef[:, :, None]
    )
    return woven.reshape(leading_dimension.shape[0], -1)


def tangent_force(
    wavevector_phase,
    k_weight,
    acoef,
    bcoef,
    factor,
    tangent,
    cosines,
    sines,
    k_dot_dir,
    moments,
    prefactor,
):
    factor_re, factor_im = factor
    tangent_re, tangent_im = tangent
    stacked = jnp.stack(
        [
            weave_terms(tangent_im, -tangent_re, acoef, bcoef),
            weave_terms(tangent_re, tangent_im, acoef, bcoef),
            weave_terms(factor_re, factor_im, acoef, bcoef),
            weave_terms(factor_im, -factor_re, acoef, bcoef),
        ]
    )
    projected = jnp.einsum("jkf,af->jka", stacked, moments, precision=exact)
    inner_sum = (
        cosines * projected[0]
        - sines * projected[1]
        - k_dot_dir * (cosines * projected[2] + sines * projected[3])
    )
    return jnp.dot((k_weight[:, None] * wavevector_phase).T, inner_sum, precision=exact) * prefactor


def plain_local(positions, moments, adj_pos, final_momentum_adjoint, species, masses, kint):
    wavevector_phase = kint.astype(jnp.float32) * wavevector_scale
    ksq = jnp.sum(wavevector_phase * wavevector_phase, 1)
    k_weight = jnp.exp(-ksq / 4.0) / jnp.maximum(ksq, 1.0)
    acoef, bcoef = coef_arrays(wavevector_phase)
    prefactor = energy_scale / math.sqrt(positions.shape[2] * lax.axis_size("brick"))
    onehot = (species[None, :] == jnp.arange(masses.shape[0], dtype=jnp.int32)[:, None]).astype(
        jnp.float32
    )
    inv_mass = jnp.dot(1.0 / masses, onehot, precision=exact)
    num_steps = positions.shape[0]

    def step_phases(step_index):
        phase = jnp.dot(wavevector_phase, positions[step_index], precision=exact)
        return (jnp.cos(phase), jnp.sin(phase))

    phase_list = [step_phases(step_index) for step_index in range(num_steps)]
    for step_index in reversed(range(num_steps)):
        cosines, sines = phase_list[step_index]
        direction = final_momentum_adjoint * inv_mass
        k_dot_dir = jnp.dot(wavevector_phase, direction, precision=exact)
        tangent_real_part, tan_im = moment_sums(
            k_dot_dir * cosines, k_dot_dir * sines, moments, acoef, bcoef
        )
        fac_re, fac_im = moment_sums(cosines, sines, moments, acoef, bcoef)
        summed_terms = lax.psum((fac_re, fac_im, -tan_im, tangent_real_part), "brick")
        factor = (summed_terms[0], summed_terms[1])
        tangent = (summed_terms[2], summed_terms[3])
        partial_force = tangent_force(
            wavevector_phase,
            k_weight,
            acoef,
            bcoef,
            factor,
            tangent,
            cosines,
            sines,
            k_dot_dir,
            moments,
            prefactor,
        )
        force = lax.psum(partial_force, "kvec")
        adj_pos = adj_pos - time_step * force
        final_momentum_adjoint = final_momentum_adjoint + time_step * adj_pos
    return (adj_pos, final_momentum_adjoint)


def plain(mesh):
    placed = (
        P(None, None, "brick"),
        P("brick", None),
        P(None, "brick"),
        P(None, "brick"),
        P("brick"),
        P(),
        P("kvec", None),
    )
    return jax.shard_map(
        plain_local,
        mesh=mesh,
        in_specs=placed,
        out_specs=(P(None, "brick"), P(None, "brick")),
        check_vma=False,
    )


MESH = pl.DeviceIdType.MESH
GROUP = 8
MOM = 10
LANES = 128
USED = MOM * 8
F32, BF16 = jnp.float32, jnp.bfloat16
two_over_pi = 2.0 / math.pi
half_pi_parts = (1.5703125, 4.837512969970703125e-4, 7.549789948768648e-8)

TOP = 5
PAIRS = [(0, b) for b in range(TOP + 1)] + [
    (a, b) for a in range(1, TOP + 1) for b in range(-TOP, TOP + 1)
]
HALF = 64
SIDE = HALF // 2
ALONG_Z = [0] + [c for top in range(1, TOP + 1) for c in (top, -top)]
SLOTS = len(ALONG_Z)
OPS = 6
SUMS = SLOTS * OPS * 8
CHUNK = 256
PARTS = 2
TURNS = ((0, 3), (3, 6))
HIGH, LOW = (128, 256, 384), (0, 512, 640)


def grid_tables(prefactor):
    scale = wavevector_scale
    a = np.zeros(HALF)
    b = np.zeros(HALF)
    a[: len(PAIRS)] = [pair[0] for pair in PAIRS]
    b[: len(PAIRS)] = [pair[1] for pair in PAIRS]
    kx, ky = scale * a, scale * b
    along = np.broadcast_to(np.stack([kx, ky])[:, :, None], (2, HALF, LANES))
    lane_x, lane_y = np.tile(kx, 2), np.tile(ky, 2)
    sign = np.where(np.arange(LANES) < HALF, -1.0, 1.0)
    lanes = np.zeros((8, LANES))
    lanes[:6] = [
        lane_x,
        lane_y,
        -0.5 * lane_x**2,
        -0.5 * lane_y**2,
        -lane_x * lane_y,
        sign,
    ]
    weights = np.zeros((16, LANES))
    maps = np.zeros((4, SLOTS, HALF, LANES))
    lane = np.arange(LANES)
    room = (LANES - USED) // 8
    one = np.where(lane < USED, lane // 8, (lane - USED) // 8)
    two = np.where(
        lane < USED,
        lane // 8,
        np.where(lane < USED + (MOM - room) * 8, room + (lane - USED) // 8, MOM),
    )
    for slot, c in enumerate(ALONG_Z):
        kz = scale * c + 0.0 * kx
        ksq = kx**2 + ky**2 + kz**2
        weights[slot] = np.tile(np.exp(-ksq / 4.0) / np.maximum(ksq, 1.0), 2) * prefactor
        zero = 0.0 * kx
        acoef = np.stack(
            [zero + 1, zero, zero, zero]
            + [-0.5 * kx**2, -0.5 * ky**2, -0.5 * kz**2, -kx * ky, -kx * kz, -ky * kz]
            + [zero],
            1,
        )
        bcoef = np.stack([zero, kx, ky, kz] + [zero] * 7, 1)
        maps[0, slot], maps[1, slot] = acoef[:, one], bcoef[:, one]
        maps[2, slot], maps[3, slot] = acoef[:, two], bcoef[:, two]
    small = np.concatenate([along.reshape(2 * HALF, LANES), lanes, weights])
    return small.astype(np.float32), maps.reshape(4, SLOTS * HALF, LANES).astype(np.float32)


def sin_cos(phase):
    n = jnp.round(phase * two_over_pi)
    r = phase - n * half_pi_parts[0]
    r = r - n * half_pi_parts[1]
    r = r - n * half_pi_parts[2]
    q = n.astype(jnp.int32)
    z = r * r
    s = r + r * z * (-1.6666654611e-1 + z * (8.3321608736e-3 + z * -1.9515295891e-4))
    c = 1.0 - 0.5 * z + z * z * (
        4.166664568298827e-2 + z * (-1.388731625493765e-3 + z * 2.443315711809948e-5)
    )
    odd = (q & 1) == 1
    sine = jnp.where(odd, c, s)
    cosine = jnp.where(odd, s, c)
    sine = jnp.where((q & 2) == 2, -sine, sine)
    cosine = jnp.where(((q + 1) & 2) == 2, -cosine, cosine)
    return sine, cosine


def split(x):
    high = x.astype(BF16)
    return high, (x - high.astype(F32)).astype(BF16)


def wide(x, copies):
    return jnp.concatenate([x] * copies, axis=1)


def dot_rows(x, y):
    return lax.dot_general(x, y, (((1,), (1,)), ((), ())), preferred_element_type=F32)


def kernel(
    kvecs,
    pos_hbm,
    mom_hbm,
    adj_hbm,
    fma_hbm,
    spec_hbm,
    mass_hbm,
    kint_hbm,
    small_hbm,
    maps_hbm,
    out_ref,
    pos_ref,
    mom_ref,
    adj_ref,
    fma_ref,
    spec_ref,
    mass_ref,
    kint_ref,
    small,
    maps,
    pack,
    rows,
    sent,
    moments,
    counts,
    counted,
    tally,
    xy,
    ztab,
    lmat,
    rhigh,
    rlow,
    sums,
    opr,
    w2,
    proj_a,
    proj_b,
    acc,
    hess,
    dirs,
    gather,
    gathered,
    total,
    part,
    bricks,
    load_sem,
    send_sem,
    recv_sem,
    zsend_sem,
    zrecv_sem,
):
    me = lax.axis_index("brick")
    mev = lax.axis_index("kvec")
    atoms = LANES * GROUP

    def flip(off):
        other = me
        for bit in (1, 2, 4):
            if off & bit:
                other = other + bit - 2 * bit * lax.rem(lax.div(me, bit), 2)
        return other

    barrier = pltpu.get_barrier_semaphore()
    for off in range(1, GROUP):
        pl.semaphore_signal(barrier, inc=1, device_id=(flip(off), mev), device_id_type=MESH)
    leader = me == 0
    beyond = kvecs - 1

    @pl.when(leader)
    def _():
        for over in range(1, kvecs):
            pl.semaphore_signal(
                barrier, inc=1, device_id=(me, lax.rem(mev + over, kvecs)), device_id_type=MESH
            )

    loads = []
    for at, (src, dst) in enumerate(
        (
            (pos_hbm, pos_ref),
            (fma_hbm, fma_ref),
            (adj_hbm, adj_ref),
            (spec_hbm, spec_ref),
            (mass_hbm, mass_ref),
            (mom_hbm, mom_ref),
            (kint_hbm, kint_ref),
            (small_hbm, small),
            (maps_hbm, maps),
        )
    ):
        loads.append(pltpu.make_async_copy(src, dst, load_sem.at[at]))
    for load in loads[:-1]:
        load.start()

    for load in loads[:5]:
        load.wait()
    species = spec_ref[...]
    mass = jnp.ones(species.shape, F32)
    for kind in range(mass_ref.shape[0]):
        mass = jnp.where(species == kind, mass_ref[kind], mass)
    pack[...] = jnp.zeros_like(pack)
    for axis in range(3):
        pack[axis : axis + 1, :] = pos_ref[axis, 0:1]
        pack[3 + axis : 4 + axis, :] = pos_ref[axis, 1:2]
    pack[6:9, :] = fma_ref[...]
    pack[9:12, :] = adj_ref[...]
    pack[12:13, :] = 1.0 / mass
    rows[:, 0:LANES] = pack[...]

    loads[6].wait()
    ka, kb, kc = kint_ref[0:1, :], kint_ref[1:2, :], kint_ref[2:3, :]
    turn = (ka < 0) | ((ka == 0) & (kb < 0))
    ka, kb, kc = (jnp.where(turn, -k, k) for k in (ka, kb, kc))
    pair = jnp.where(ka == 0, kb, (TOP + 1) + (ka - 1) * (2 * TOP + 1) + kb + TOP)
    slot = jnp.where(kc > 0, 2 * kc - 1, -2 * kc)
    here = kint_ref.shape[1]
    pair_row = lax.broadcasted_iota(jnp.int32, (LANES, here), 0)
    pair_row = jnp.where(pair_row < HALF, pair_row, pair_row - HALF)
    slot_row = lax.broadcasted_iota(jnp.int32, (16, here), 0)
    counts[...] = dot_rows(
        (slot_row == slot).astype(F32).astype(BF16), (pair_row == pair).astype(F32).astype(BF16)
    )

    pl.semaphore_wait(barrier, GROUP - 1 + jnp.where(leader, beyond, 0))
    copies = {}
    for off in range(1, GROUP):
        copies[0, off] = pltpu.make_async_remote_copy(
            src_ref=pack,
            dst_ref=rows.at[:, pl.ds(off * LANES, LANES)],
            send_sem=send_sem.at[0, off],
            recv_sem=recv_sem.at[0, off],
            device_id=(flip(off), mev),
            device_id_type=MESH,
        )
        copies[0, off].start()
    def count_copy(over):
        return pltpu.make_async_remote_copy(
            src_ref=counts,
            dst_ref=counted.at[over],
            send_sem=zsend_sem.at[over],
            recv_sem=zrecv_sem.at[over],
            device_id=(me, lax.rem(mev + over, kvecs)),
            device_id_type=MESH,
        )

    def tally_copy(off):
        return pltpu.make_async_remote_copy(
            src_ref=tally,
            dst_ref=tally,
            send_sem=send_sem.at[4, off],
            recv_sem=recv_sem.at[4, 0],
            device_id=(flip(off), mev),
            device_id_type=MESH,
        )

    @pl.when(leader)
    def _():
        for over in range(1, kvecs):
            count_copy(over).start()

    loads[5].wait()
    loads[8].start()
    for piece in range(mom_ref.shape[1] // LANES):
        turned = mom_ref[:, piece * LANES : (piece + 1) * LANES].T
        sent[2 * piece : 2 * piece + 2] = turned.reshape(2, GROUP, 8, LANES)

    for off in (2, 4, 3, 5, 6, 7, 1):
        copies[1, off] = pltpu.make_async_remote_copy(
            src_ref=sent.at[:, flip(off)],
            dst_ref=moments.at[:, :, pl.ds(off * LANES, LANES)],
            send_sem=send_sem.at[1, off],
            recv_sem=recv_sem.at[1, off],
            device_id=(flip(off), mev),
            device_id_type=MESH,
        )
        copies[1, off].start()

    moments[:, :, 0:LANES] = sent[:, pl.ds(me, 1)].reshape(MOM, 8, LANES)

    loads[7].wait()
    for off in range(1, GROUP):
        copies[0, off].wait_recv()
    lane_x, lane_y = small[128:129], small[129:130]
    lane_xx, lane_yy, lane_xy = small[130:131], small[131:132], small[132:133]
    sign = small[133:134]

    def along_x(at, size, copies_wide):
        return wide(small[pl.ds(at, size)], copies_wide)

    def along_y(at, size, copies_wide):
        return wide(small[pl.ds(HALF + at, size)], copies_wide)

    def make_phases(step):
        turns = lax.broadcasted_iota(jnp.int32, (8, atoms), 0).astype(F32) * wavevector_scale
        sine, cosine = sin_cos(turns * rows[3 * step + 2 : 3 * step + 3, :])
        ztab[step, 0:8] = cosine
        ztab[step, 8:16] = sine

        @pl.loop(0, HALF // 16)
        def _(chunk):
            at = pl.multiple_of(chunk * 16, 16)
            phase = along_x(at, 16, GROUP) * rows[3 * step : 3 * step + 1, :] + along_y(
                at, 16, GROUP
            ) * rows[3 * step + 1 : 3 * step + 2, :]
            sine, cosine = sin_cos(phase)
            xy[step, 0, pl.ds(at, 16)] = cosine
            xy[step, 1, pl.ds(at, 16)] = sine
            store_split(step, 0, at, cosine, sine)

    def store_split(step, block, at, real, imag):
        for which, part_here in enumerate((real, imag)):
            high, low = split(part_here)
            lmat[step, pl.ds(HIGH[block] + which * HALF + at, 16)] = high
            lmat[step, pl.ds(LOW[block] + which * HALF + at, 16)] = low

    def make_tangents(step, direction):
        @pl.loop(0, HALF // 16)
        def _(chunk):
            at = pl.multiple_of(chunk * 16, 16)
            real, imag = xy[step, 0, pl.ds(at, 16)], xy[step, 1, pl.ds(at, 16)]
            k_dot = along_x(at, 16, GROUP) * direction(0) + along_y(at, 16, GROUP) * direction(1)
            store_split(step, 1, at, -k_dot * imag, k_dot * real)
            store_split(step, 2, at, direction(2) * real, direction(2) * imag)

    def make_terms(step, first, width):
        here = pl.ds(first, width)
        q = [moments[m, :, here] for m in range(MOM)]

        def store(group, ops):
            for two in range(OPS // 2):
                both = jnp.concatenate([ops[2 * two], ops[2 * two + 1]], axis=0)
                at = group * OPS * 8 + two * 16
                rhigh[step, at : at + 16, here], rlow[step, at : at + 16, here] = split(both)

        store(0, [q[0], q[1], q[2], q[4], q[5], q[7]])
        for turn in range(1, TOP + 1):
            kz = turn * wavevector_scale
            c, s = ztab[step, turn : turn + 1, here], ztab[step, 8 + turn : 9 + turn, here]
            kc, ks = kz * c, kz * s
            charge = q[0] - (0.5 * kz * kz) * q[6]
            store(
                2 * turn - 1,
                [
                    charge * c - q[3] * ks,
                    q[1] * c - q[8] * ks,
                    q[2] * c - q[9] * ks,
                    q[4] * c,
                    q[5] * c,
                    q[7] * c,
                ],
            )
            store(
                2 * turn,
                [
                    charge * s + q[3] * kc,
                    q[1] * s + q[8] * kc,
                    q[2] * s + q[9] * kc,
                    q[4] * s,
                    q[5] * s,
                    q[7] * s,
                ],
            )

    def dots(step, first, width, begin, end, add, turns=(0, TOP + 1)):
        here = pl.ds(first, width)
        at = slice(max(2 * turns[0] - 1, 0) * OPS * 8, (2 * turns[1] - 1) * OPS * 8)
        value = dot_rows(rhigh[step, at, here], lmat[step, begin:end, here])
        sums[at, begin:end] = sums[at, begin:end] + value if add else value
        begin, end = max(begin, HIGH[0]), min(end, LOW[1])
        sums[at, begin:end] += dot_rows(rlow[step, at, here], lmat[step, begin:end, here])

    def combine(block, turns=(0, TOP + 1)):
        high, low = HIGH[block], LOW[block]
        out = {}
        for group in range(max(2 * turns[0] - 1, 0), 2 * turns[1] - 1):
            op = []
            for which in range(OPS):
                at = (group * OPS + which) * 8
                op.append(
                    sums[at : at + 8, high : high + LANES] + sums[at : at + 8, low : low + LANES]
                )
            turned = pltpu.roll(lane_x * op[1] + lane_y * op[2], HALF, 1) * sign
            out[group] = op[0] + turned + lane_xx * op[3] + lane_yy * op[4] + lane_xy * op[5]
        return out

    def tangent_sums(turns=(0, TOP + 1)):
        t1, g = combine(1, turns), combine(2, turns)
        out = {0: t1[0]} if turns[0] == 0 else {}
        for turn in range(max(turns[0], 1), turns[1]):
            kz = turn * wavevector_scale
            out[2 * turn - 1] = t1[2 * turn - 1] - kz * g[2 * turn]
            out[2 * turn] = t1[2 * turn] + kz * g[2 * turn - 1]
        return out

    lane = lax.broadcasted_iota(jnp.int32, (1, LANES), 1)

    def operand(slot, real, imag):
        here = slice(slot * HALF, (slot + 1) * HALF)
        one = real * maps[0, here] + imag * maps[1, here]
        two = real * maps[2, here] + imag * maps[3, here]
        top = one.astype(BF16)
        rest = jnp.where(lane < USED, one - top.astype(F32), two).astype(BF16)
        return jnp.concatenate([top, rest], axis=1)

    def project(place, parts, weights):
        for slot, c in enumerate(ALONG_Z):
            if slot not in parts:
                continue
            if c == 0:
                value = parts[0]
            else:
                turn = abs(c)
                turned = pltpu.roll(parts[2 * turn], HALF, 1) * sign
                value = parts[2 * turn - 1] + (turned if c > 0 else -turned)
            value = value * weights[slot : slot + 1]
            tile = jnp.concatenate([value] * 16, axis=0).T
            real, imag = tile[0:HALF], tile[HALF:]
            first, second = operand(slot, real, imag), operand(slot, imag, -real)
            at = slot * 2 * SIDE
            for side in range(2):
                here = slice(side * SIDE, (side + 1) * SIDE)
                opr[side, place, at : at + SIDE] = first[here]
                opr[side, place, at + SIDE : at + 2 * SIDE] = second[here]

    def around(step, at, here):
        real, imag = xy[step, 0, at : at + 8, here], xy[step, 1, at : at + 8, here]
        yield 0, real, imag
        for turn in range(1, TOP + 1):
            c, s = ztab[step, turn : turn + 1, here], ztab[step, 8 + turn : 9 + turn, here]
            rc, is_, ic, rs = real * c, imag * s, imag * c, real * s
            yield turn, (rc - is_, ic + rs), (rc + is_, ic - rs)

    def projected(buffer, place, slot, row):
        at = (place * SLOTS + slot) * 2 * SIDE + row
        return buffer[at : at + 8], buffer[at + SIDE : at + SIDE + 8]

    def tangent_value(wave, buffer, place, slot, row):
        first, second = projected(buffer, place, slot, row)
        return wave[0] * second - wave[1] * first

    def factor_value(wave, buffer, place, slot, row):
        first, second = projected(buffer, place, slot, row)
        return wave[0] * first + wave[1] * second

    pieces = CHUNK // LANES

    def force_terms(step, buffer, side, here, direction, with_factor):
        place = 1 if with_factor else 0
        total_x, total_y, total_z = 0.0, 0.0, 0.0
        if with_factor:
            dx, dy, dz = (direction(axis, here) for axis in range(3))
        for row in range(0, SIDE, 8):
            at = side * SIDE + row
            kx, ky = along_x(at, 8, pieces), along_y(at, 8, pieces)
            waves = around(step, at, here)
            _, real, imag = next(waves)
            flat = tangent_value((real, imag), buffer, place, 0, row)
            if with_factor:
                k_dot = kx * dx + ky * dy
                flat = flat - k_dot * factor_value((real, imag), buffer, 0, 0, row)
            tilt = 0.0
            for turn, plus, minus in waves:
                kz = turn * wavevector_scale
                up = tangent_value(plus, buffer, place, 2 * turn - 1, row)
                down = tangent_value(minus, buffer, place, 2 * turn, row)
                if with_factor:
                    kdz = kz * dz
                    up = up - (k_dot + kdz) * factor_value(plus, buffer, 0, 2 * turn - 1, row)
                    down = down - (k_dot - kdz) * factor_value(minus, buffer, 0, 2 * turn, row)
                flat = flat + (up + down)
                tilt = tilt + kz * (up - down)
            total_x, total_y, total_z = total_x + kx * flat, total_y + ky * flat, total_z + tilt
            yield
        acc[0, :, here] += total_x
        acc[1, :, here] += total_y
        acc[2, :, here] += total_z

    def hessian_terms(step, buffer, side, here):
        totals = [0.0] * 6
        for row in range(0, SIDE, 8):
            at = side * SIDE + row
            kx, ky = along_x(at, 8, pieces), along_y(at, 8, pieces)
            waves = around(step, at, here)
            _, real, imag = next(waves)
            flat = factor_value((real, imag), buffer, 0, 0, row)
            tilt, bend = 0.0, 0.0
            for turn, plus, minus in waves:
                kz = turn * wavevector_scale
                up = factor_value(plus, buffer, 0, 2 * turn - 1, row)
                down = factor_value(minus, buffer, 0, 2 * turn, row)
                both = up + down
                flat = flat + both
                tilt = tilt + kz * (up - down)
                bend = bend + (kz * kz) * both
            fx, fy = kx * flat, ky * flat
            for entry, value in enumerate((kx * fx, kx * fy, kx * tilt, ky * fy, ky * tilt, bend)):
                totals[entry] = totals[entry] + value
            yield
        for entry in range(6):
            hess[entry, :, here] += totals[entry]

    def sweep(places, terms):
        count = len(places) * SLOTS * 2 * SIDE
        buffers = (proj_a.at[0:count], proj_b.at[0:count])

        def fill(side, first):
            for begin in range(0, count, count // PARTS):
                rows_here = slice(begin, begin + count // PARTS)
                left = opr[side, places[0] : places[-1] + 1].reshape(count, 2 * LANES)[rows_here]
                buffers[side][rows_here] = jnp.dot(
                    left, w2[:, pl.ds(first, CHUNK)], preferred_element_type=F32
                )
                yield

        def beside(*works):
            works = list(works)
            while works:
                for work in list(works):
                    if next(work, works) is works:
                        works.remove(work)

        beside(fill(0, 0))

        @pl.loop(0, atoms // CHUNK)
        def _(index):
            first = pl.multiple_of(index * CHUNK, CHUNK)
            after = pl.multiple_of(lax.rem(index + 1, atoms // CHUNK) * CHUNK, CHUNK)
            here = pl.ds(first, CHUNK)
            beside(fill(1, first), terms(buffers[0], 0, here))
            beside(fill(0, after), terms(buffers[1], 1, here))

    def sums_to_operands(step, place, begin, end, parts):
        waiting = None
        for turns in TURNS:
            dots(step, 0, atoms, begin, end, False, turns)
            if waiting is not None:
                project(place, parts(waiting), weights)
            waiting = turns
        project(place, parts(waiting), weights)

    last = 1
    inv_mass = rows[12:13, :]
    dirs[0:3, :] = rows[6:9, :] * inv_mass
    make_phases(last)
    make_tangents(last, lambda axis: dirs[axis : axis + 1, :])

    order = (0, 2, 4, 6)
    for place, (off, many) in enumerate(((0, 2), (2, 4), (6, 2))):
        if place == 1:
            make_phases(0)
        if place == 1:

            @pl.when(leader)
            def _():
                count = counts[...]
                for over in range(1, kvecs):
                    count_copy(over).wait_recv()
                    count = count + counted[over]
                tally[...] = count
                for other in range(1, GROUP):
                    tally_copy(other).start()

        for one in range(off, off + many):
            if one > 0:
                copies[1, one].wait_recv()
        make_terms(last, off * LANES, many * LANES)
        dots(last, off * LANES, many * LANES, 0, 768, place > 0)
        here = pl.ds(off * LANES, many * LANES)
        q_high, q_low = split(moments[:, :, here].reshape(USED, many * LANES))
        fits = LANES - USED
        w2[0:USED, here] = q_high
        w2[USED:LANES, here] = q_low[0:fits]
        w2[LANES : LANES + USED, here] = q_high
        w2[LANES + USED : LANES + 2 * USED - fits, here] = q_low[fits:]
        w2[LANES + 2 * USED - fits :, here] = jnp.zeros((16, many * LANES), BF16)

    @pl.when(me != 0)
    def _():
        tally_copy(1).wait_recv()

    loads[8].wait()
    weights = tally[...] * small[136:152]

    project(0, combine(0), weights)
    project(1, tangent_sums(), weights)
    acc[...] = jnp.zeros_like(acc)
    sweep(
        (0, 1),
        lambda buffer, side, here: force_terms(
            last, buffer, side, here, lambda axis, here: dirs[axis : axis + 1, here], True
        ),
    )

    for axis in range(3):
        out = jnp.sum(acc[axis], axis=0, keepdims=True)
        for off in range(GROUP):
            gather[pl.ds(axis * GROUP + flip(off), 1), :] = out[:, off * LANES : (off + 1) * LANES]
    for off in range(1, GROUP):
        copies[2, off] = pltpu.make_async_remote_copy(
            src_ref=gather,
            dst_ref=gathered.at[off],
            send_sem=send_sem.at[2, off],
            recv_sem=recv_sem.at[2, off],
            device_id=(flip(off), mev),
            device_id_type=MESH,
        )
        copies[2, off].start()

    for off in order:
        make_terms(0, off * LANES, 2 * LANES)
    sums_to_operands(0, 0, 0, 256, lambda turns: combine(0, turns))
    hess[...] = jnp.zeros_like(hess)
    sweep((0,), lambda buffer, side, here: hessian_terms(0, buffer, side, here))
    second = [jnp.sum(hess[row], axis=0, keepdims=True) for row in range(6)]

    out = gather[...]
    for off in range(1, GROUP):
        copies[2, off].wait_recv()
        out = out + gathered[off]
    total[...] = out
    forces = []
    for axis in range(3):
        forces.append(
            jnp.concatenate(
                [total[pl.ds(axis * GROUP + flip(off), 1), :] for off in range(GROUP)], axis=1
            )
        )
    adj = [rows[9 + axis : 10 + axis, :] - time_step * forces[axis] for axis in range(3)]
    fma = [rows[6 + axis : 7 + axis, :] + time_step * adj[axis] for axis in range(3)]
    for axis in range(3):
        dirs[axis : axis + 1, :] = fma[axis] * inv_mass

    make_tangents(0, lambda axis: dirs[axis : axis + 1, :])
    sums_to_operands(0, 1, 256, 768, tangent_sums)
    acc[...] = jnp.zeros_like(acc)
    sweep((1,), lambda buffer, side, here: force_terms(0, buffer, side, here, None, False))
    direction = [dirs[axis : axis + 1, :] for axis in range(3)]
    places = ((0, 1, 2), (1, 3, 4), (2, 4, 5))
    part[...] = jnp.zeros_like(part)
    for axis in range(3):
        out = jnp.sum(acc[axis], axis=0, keepdims=True)
        for other in range(3):
            out = out - second[places[axis][other]] * direction[other]
        for off in range(GROUP):
            part[off, axis : axis + 1, :] = out[:, off * LANES : (off + 1) * LANES]
    for off in range(1, GROUP):
        copies[3, off] = pltpu.make_async_remote_copy(
            src_ref=part.at[off],
            dst_ref=bricks.at[off],
            send_sem=send_sem.at[3, off],
            recv_sem=recv_sem.at[3, off],
            device_id=(flip(off), mev),
            device_id_type=MESH,
        )
        copies[3, off].start()
    out = part[0]
    for off in range(1, GROUP):
        copies[3, off].wait_recv()
        out = out + bricks[off]
    out_ref[0:4, :] = out
    for axis in range(3):
        out_ref[4 + axis : 5 + axis, :] = adj[axis][:, 0:LANES]
        out_ref[8 + axis : 9 + axis, :] = fma[axis][:, 0:LANES]
    for copy in copies.values():
        copy.wait_send()

    @pl.when(leader)
    def _():
        for over in range(1, kvecs):
            count_copy(over).wait_send()
        for off in range(1, GROUP):
            tally_copy(off).wait_send()


def fused(kvecs, positions, moments, adj_pos, final_momentum_adjoint, species, masses, kint):
    steps, _, here = positions.shape
    kdev = kint.shape[0]
    atoms = here * GROUP
    small, maps = grid_tables(energy_scale / math.sqrt(atoms))
    vmem = pl.BlockSpec(memory_space=pltpu.VMEM)
    hbm = pl.BlockSpec(memory_space=pltpu.HBM)
    points = SLOTS * HALF
    last = pl.pallas_call(
        functools.partial(kernel, kvecs),
        out_shape=pltpu.VMEM((16, here), F32),
        in_specs=[hbm] * 9,
        out_specs=vmem,
        scratch_shapes=[
            pltpu.VMEM((3, steps, here), F32),
            pltpu.VMEM(moments.shape, F32),
            pltpu.VMEM((3, here), F32),
            pltpu.VMEM((3, here), F32),
            pltpu.VMEM((1, here), jnp.int32),
            pltpu.SMEM(masses.shape, F32),
            pltpu.VMEM((3, kdev), jnp.int32),
            pltpu.VMEM(small.shape, F32),
            pltpu.VMEM(maps.shape, F32),
            pltpu.VMEM((16, here), F32),
            pltpu.VMEM((16, atoms), F32),
            pltpu.VMEM((MOM, GROUP, 8, here), F32),
            pltpu.VMEM((MOM, 8, atoms), F32),
            pltpu.VMEM((16, LANES), F32),
            pltpu.VMEM((kvecs, 16, LANES), F32),
            pltpu.VMEM((16, LANES), F32),
            pltpu.VMEM((steps, 2, HALF, atoms), F32),
            pltpu.VMEM((steps, 16, atoms), F32),
            pltpu.VMEM((steps, 768, atoms), BF16),
            pltpu.VMEM((steps, SUMS, atoms), BF16),
            pltpu.VMEM((steps, SUMS, atoms), BF16),
            pltpu.VMEM((SUMS, 768), F32),
            pltpu.VMEM((2, 2, points, 2 * LANES), BF16),
            pltpu.VMEM((2 * LANES, atoms), BF16),
            pltpu.VMEM((2 * points, CHUNK), F32),
            pltpu.VMEM((2 * points, CHUNK), F32),
            pltpu.VMEM((3, 8, atoms), F32),
            pltpu.VMEM((6, 8, atoms), F32),
            pltpu.VMEM((8, atoms), F32),
            pltpu.VMEM((3 * GROUP, here), F32),
            pltpu.VMEM((GROUP, 3 * GROUP, here), F32),
            pltpu.VMEM((3 * GROUP, here), F32),
            pltpu.VMEM((GROUP, 4, here), F32),
            pltpu.VMEM((GROUP, 4, here), F32),
            pltpu.SemaphoreType.DMA((9,)),
            pltpu.SemaphoreType.DMA((5, GROUP)),
            pltpu.SemaphoreType.DMA((5, GROUP)),
            pltpu.SemaphoreType.DMA((kvecs,)),
            pltpu.SemaphoreType.DMA((kvecs,)),
        ],
        compiler_params=pltpu.CompilerParams(
            collective_id=0, has_side_effects=True, vmem_limit_bytes=60 << 20
        ),
    )(
        positions.transpose(1, 0, 2),
        moments,
        adj_pos,
        final_momentum_adjoint,
        species.reshape(1, here),
        masses,
        kint.T,
        small,
        maps,
    )
    adj = last[4:7] - time_step * last[0:3]
    return adj, last[8:11] + time_step * adj


def solution(mesh):
    bricks, kvecs = mesh.shape["brick"], mesh.shape["kvec"]
    if bricks != GROUP:
        return plain(mesh)
    placed = (
        P(None, None, "brick"),
        P("brick", None),
        P(None, "brick"),
        P(None, "brick"),
        P("brick"),
        P(),
        P("kvec", None),
    )
    return jax.shard_map(
        functools.partial(fused, kvecs),
        mesh=mesh,
        in_specs=placed,
        out_specs=(P(None, "brick"), P(None, "brick")),
        check_vma=False,
    )
```

```python
import functools
import math

import jax
import jax.numpy as jnp
import numpy as np
from jax import lax
from jax.experimental import pallas as pl
from jax.experimental.pallas import tpu as pltpu
from jax.sharding import PartitionSpec as P

exact = lax.Precision.HIGHEST
wavevector_scale = 0.5
time_step = 0.5
energy_scale = 0.125


def coef_arrays(wavevector_phase):
    kx, ky, kz = (wavevector_phase[:, 0], wavevector_phase[:, 1], wavevector_phase[:, 2])
    ones = jnp.ones_like(kx)
    zeros = jnp.zeros_like(kx)
    acoef = jnp.stack(
        [
            ones,
            zeros,
            zeros,
            zeros,
            -0.5 * kx * kx,
            -0.5 * ky * ky,
            -0.5 * kz * kz,
            -kx * ky,
            -kx * kz,
            -ky * kz,
        ],
        1,
    )
    bcoef = jnp.stack([zeros, kx, ky, kz, zeros, zeros, zeros, zeros, zeros, zeros], 1)
    return (acoef, bcoef)


def moment_sums(cos_w, sin_w, moments, acoef, bcoef):
    channels = moments.shape[1] // 10
    cos_part = jnp.dot(cos_w, moments, precision=exact).reshape(cos_w.shape[0], 10, channels)
    sine_component = jnp.dot(sin_w, moments, precision=exact).reshape(cos_w.shape[0], 10, channels)
    real_sum = jnp.einsum("km,kmc->kc", acoef, cos_part, precision=exact) - jnp.einsum(
        "km,kmc->kc", bcoef, sine_component, precision=exact
    )
    imag_sum = jnp.einsum("km,kmc->kc", acoef, sine_component, precision=exact) + jnp.einsum(
        "km,kmc->kc", bcoef, cos_part, precision=exact
    )
    return (real_sum, imag_sum)


def weave_terms(leading_dimension, trailing, acoef, bcoef):
    woven = (
        leading_dimension[:, None, :] * acoef[:, :, None] + trailing[:, None, :] * bcoef[:, :, None]
    )
    return woven.reshape(leading_dimension.shape[0], -1)


def tangent_force(
    wavevector_phase,
    k_weight,
    acoef,
    bcoef,
    factor,
    tangent,
    cosines,
    sines,
    k_dot_dir,
    moments,
    prefactor,
):
    factor_re, factor_im = factor
    tangent_re, tangent_im = tangent
    stacked = jnp.stack(
        [
            weave_terms(tangent_im, -tangent_re, acoef, bcoef),
            weave_terms(tangent_re, tangent_im, acoef, bcoef),
            weave_terms(factor_re, factor_im, acoef, bcoef),
            weave_terms(factor_im, -factor_re, acoef, bcoef),
        ]
    )
    projected = jnp.einsum("jkf,af->jka", stacked, moments, precision=exact)
    inner_sum = (
        cosines * projected[0]
        - sines * projected[1]
        - k_dot_dir * (cosines * projected[2] + sines * projected[3])
    )
    return jnp.dot((k_weight[:, None] * wavevector_phase).T, inner_sum, precision=exact) * prefactor


def plain_local(positions, moments, adj_pos, final_momentum_adjoint, species, masses, kint):
    wavevector_phase = kint.astype(jnp.float32) * wavevector_scale
    ksq = jnp.sum(wavevector_phase * wavevector_phase, 1)
    k_weight = jnp.exp(-ksq / 4.0) / jnp.maximum(ksq, 1.0)
    acoef, bcoef = coef_arrays(wavevector_phase)
    prefactor = energy_scale / math.sqrt(positions.shape[2] * lax.axis_size("brick"))
    onehot = (species[None, :] == jnp.arange(masses.shape[0], dtype=jnp.int32)[:, None]).astype(
        jnp.float32
    )
    inv_mass = jnp.dot(1.0 / masses, onehot, precision=exact)
    num_steps = positions.shape[0]

    def step_phases(step_index):
        phase = jnp.dot(wavevector_phase, positions[step_index], precision=exact)
        return (jnp.cos(phase), jnp.sin(phase))

    phase_list = [step_phases(step_index) for step_index in range(num_steps)]
    for step_index in reversed(range(num_steps)):
        cosines, sines = phase_list[step_index]
        direction = final_momentum_adjoint * inv_mass
        k_dot_dir = jnp.dot(wavevector_phase, direction, precision=exact)
        tangent_real_part, tan_im = moment_sums(
            k_dot_dir * cosines, k_dot_dir * sines, moments, acoef, bcoef
        )
        fac_re, fac_im = moment_sums(cosines, sines, moments, acoef, bcoef)
        summed_terms = lax.psum((fac_re, fac_im, -tan_im, tangent_real_part), "brick")
        factor = (summed_terms[0], summed_terms[1])
        tangent = (summed_terms[2], summed_terms[3])
        partial_force = tangent_force(
            wavevector_phase,
            k_weight,
            acoef,
            bcoef,
            factor,
            tangent,
            cosines,
            sines,
            k_dot_dir,
            moments,
            prefactor,
        )
        force = lax.psum(partial_force, "kvec")
        adj_pos = adj_pos - time_step * force
        final_momentum_adjoint = final_momentum_adjoint + time_step * adj_pos
    return (adj_pos, final_momentum_adjoint)


def plain(mesh):
    placed = (
        P(None, None, "brick"),
        P("brick", None),
        P(None, "brick"),
        P(None, "brick"),
        P("brick"),
        P(),
        P("kvec", None),
    )
    return jax.shard_map(
        plain_local,
        mesh=mesh,
        in_specs=placed,
        out_specs=(P(None, "brick"), P(None, "brick")),
        check_vma=False,
    )


MESH = pl.DeviceIdType.MESH
GROUP = 8
MOM = 10
LANES = 128
USED = MOM * 8
F32, BF16 = jnp.float32, jnp.bfloat16
two_over_pi = 2.0 / math.pi
half_pi_parts = (1.5703125, 4.837512969970703125e-4, 7.549789948768648e-8)

TOP = 5
PAIRS = [(0, b) for b in range(TOP + 1)] + [
    (a, b) for a in range(1, TOP + 1) for b in range(-TOP, TOP + 1)
]
HALF = 64
SIDE = HALF // 2
ALONG_Z = [0] + [c for top in range(1, TOP + 1) for c in (top, -top)]
SLOTS = len(ALONG_Z)
OPS = 6
SUMS = SLOTS * OPS * 8
CHUNK = 256
PARTS = 2
FAR_FIRST = (6, 7, 2, 3, 4, 5, 1)
TURNS = ((0, 3), (3, 6))
HIGH, LOW = (128, 256, 384), (0, 512, 640)


def grid_tables(prefactor):
    scale = wavevector_scale
    a = np.zeros(HALF)
    b = np.zeros(HALF)
    a[: len(PAIRS)] = [pair[0] for pair in PAIRS]
    b[: len(PAIRS)] = [pair[1] for pair in PAIRS]
    kx, ky = scale * a, scale * b
    along = np.broadcast_to(np.stack([kx, ky])[:, :, None], (2, HALF, LANES))
    lane_x, lane_y = np.tile(kx, 2), np.tile(ky, 2)
    sign = np.where(np.arange(LANES) < HALF, -1.0, 1.0)
    lanes = np.zeros((8, LANES))
    lanes[:6] = [
        lane_x,
        lane_y,
        -0.5 * lane_x**2,
        -0.5 * lane_y**2,
        -lane_x * lane_y,
        sign,
    ]
    weights = np.zeros((16, LANES))
    maps = np.zeros((4, SLOTS, HALF, LANES))
    lane = np.arange(LANES)
    room = (LANES - USED) // 8
    one = np.where(lane < USED, lane // 8, (lane - USED) // 8)
    two = np.where(
        lane < USED,
        lane // 8,
        np.where(lane < USED + (MOM - room) * 8, room + (lane - USED) // 8, MOM),
    )
    for slot, c in enumerate(ALONG_Z):
        kz = scale * c + 0.0 * kx
        ksq = kx**2 + ky**2 + kz**2
        weights[slot] = np.tile(np.exp(-ksq / 4.0) / np.maximum(ksq, 1.0), 2) * prefactor
        zero = 0.0 * kx
        acoef = np.stack(
            [zero + 1, zero, zero, zero]
            + [-0.5 * kx**2, -0.5 * ky**2, -0.5 * kz**2, -kx * ky, -kx * kz, -ky * kz]
            + [zero],
            1,
        )
        bcoef = np.stack([zero, kx, ky, kz] + [zero] * 7, 1)
        maps[0, slot], maps[1, slot] = acoef[:, one], bcoef[:, one]
        maps[2, slot], maps[3, slot] = acoef[:, two], bcoef[:, two]
    small = np.concatenate([along.reshape(2 * HALF, LANES), lanes, weights])
    return small.astype(np.float32), maps.reshape(4, SLOTS * HALF, LANES).astype(np.float32)


def sin_cos(phase):
    n = jnp.round(phase * two_over_pi)
    r = phase - n * half_pi_parts[0]
    r = r - n * half_pi_parts[1]
    r = r - n * half_pi_parts[2]
    q = n.astype(jnp.int32)
    z = r * r
    s = r + r * z * (-1.6666654611e-1 + z * (8.3321608736e-3 + z * -1.9515295891e-4))
    c = 1.0 - 0.5 * z + z * z * (
        4.166664568298827e-2 + z * (-1.388731625493765e-3 + z * 2.443315711809948e-5)
    )
    odd = (q & 1) == 1
    sine = jnp.where(odd, c, s)
    cosine = jnp.where(odd, s, c)
    sine = jnp.where((q & 2) == 2, -sine, sine)
    cosine = jnp.where(((q + 1) & 2) == 2, -cosine, cosine)
    return sine, cosine


def split(x):
    high = x.astype(BF16)
    return high, (x - high.astype(F32)).astype(BF16)


def wide(x, copies):
    return jnp.concatenate([x] * copies, axis=1)


def dot_rows(x, y):
    return lax.dot_general(x, y, (((1,), (1,)), ((), ())), preferred_element_type=F32)


def kernel(
    kvecs,
    pos_hbm,
    mom_hbm,
    adj_hbm,
    fma_hbm,
    spec_hbm,
    mass_hbm,
    kint_hbm,
    small_hbm,
    maps_hbm,
    out_ref,
    pos_ref,
    mom_ref,
    adj_ref,
    fma_ref,
    spec_ref,
    mass_ref,
    kint_ref,
    small,
    maps,
    pack,
    rows,
    sent,
    moments,
    counts,
    counted,
    tally,
    xy,
    ztab,
    lmat,
    rhigh,
    rlow,
    sums,
    opr,
    w2,
    proj_a,
    proj_b,
    acc,
    hess,
    second,
    dirs,
    gather,
    gathered,
    total,
    part,
    bricks,
    load_sem,
    send_sem,
    recv_sem,
    zsend_sem,
    zrecv_sem,
):
    me = lax.axis_index("brick")
    mev = lax.axis_index("kvec")
    atoms = LANES * GROUP

    def flip(off):
        other = me
        for bit in (1, 2, 4):
            if off & bit:
                other = other + bit - 2 * bit * lax.rem(lax.div(me, bit), 2)
        return other

    barrier = pltpu.get_barrier_semaphore()
    for off in range(1, GROUP):
        pl.semaphore_signal(barrier, inc=1, device_id=(flip(off), mev), device_id_type=MESH)
    leader = me == 0
    beyond = kvecs - 1

    @pl.when(leader)
    def _():
        for over in range(1, kvecs):
            pl.semaphore_signal(
                barrier, inc=1, device_id=(me, lax.rem(mev + over, kvecs)), device_id_type=MESH
            )

    loads = []
    for at, (src, dst) in enumerate(
        (
            (pos_hbm, pos_ref),
            (fma_hbm, fma_ref),
            (adj_hbm, adj_ref),
            (spec_hbm, spec_ref),
            (mass_hbm, mass_ref),
            (mom_hbm, mom_ref),
            (kint_hbm, kint_ref),
            (small_hbm, small),
            (maps_hbm, maps),
        )
    ):
        loads.append(pltpu.make_async_copy(src, dst, load_sem.at[at]))
    for load in loads[:-1]:
        load.start()

    for load in loads[:5]:
        load.wait()
    species = spec_ref[...]
    mass = jnp.ones(species.shape, F32)
    for kind in range(mass_ref.shape[0]):
        mass = jnp.where(species == kind, mass_ref[kind], mass)
    pack[...] = jnp.zeros_like(pack)
    for axis in range(3):
        pack[axis : axis + 1, :] = pos_ref[axis, 0:1]
        pack[3 + axis : 4 + axis, :] = pos_ref[axis, 1:2]
    pack[6:9, :] = fma_ref[...]
    pack[9:12, :] = adj_ref[...]
    pack[12:13, :] = 1.0 / mass
    rows[:, 0:LANES] = pack[...]

    loads[6].wait()
    ka, kb, kc = kint_ref[0:1, :], kint_ref[1:2, :], kint_ref[2:3, :]
    turn = (ka < 0) | ((ka == 0) & (kb < 0))
    ka, kb, kc = (jnp.where(turn, -k, k) for k in (ka, kb, kc))
    pair = jnp.where(ka == 0, kb, (TOP + 1) + (ka - 1) * (2 * TOP + 1) + kb + TOP)
    slot = jnp.where(kc > 0, 2 * kc - 1, -2 * kc)
    here = kint_ref.shape[1]
    pair_row = lax.broadcasted_iota(jnp.int32, (LANES, here), 0)
    pair_row = jnp.where(pair_row < HALF, pair_row, pair_row - HALF)
    slot_row = lax.broadcasted_iota(jnp.int32, (16, here), 0)
    counts[...] = dot_rows(
        (slot_row == slot).astype(F32).astype(BF16), (pair_row == pair).astype(F32).astype(BF16)
    )

    pl.semaphore_wait(barrier, GROUP - 1 + jnp.where(leader, beyond, 0))
    copies = {}
    for off in FAR_FIRST:
        copies[0, off] = pltpu.make_async_remote_copy(
            src_ref=pack,
            dst_ref=rows.at[:, pl.ds(off * LANES, LANES)],
            send_sem=send_sem.at[0, off],
            recv_sem=recv_sem.at[0, off],
            device_id=(flip(off), mev),
            device_id_type=MESH,
        )
        copies[0, off].start()
    def count_copy(over):
        return pltpu.make_async_remote_copy(
            src_ref=counts,
            dst_ref=counted.at[over],
            send_sem=zsend_sem.at[over],
            recv_sem=zrecv_sem.at[over],
            device_id=(me, lax.rem(mev + over, kvecs)),
            device_id_type=MESH,
        )

    def tally_copy(off):
        return pltpu.make_async_remote_copy(
            src_ref=tally,
            dst_ref=tally,
            send_sem=send_sem.at[4, off],
            recv_sem=recv_sem.at[4, 0],
            device_id=(flip(off), mev),
            device_id_type=MESH,
        )

    @pl.when(leader)
    def _():
        for over in range(1, kvecs):
            count_copy(over).start()

    loads[5].wait()
    loads[8].start()
    for piece in range(mom_ref.shape[1] // LANES):
        turned = mom_ref[:, piece * LANES : (piece + 1) * LANES].T
        sent[2 * piece : 2 * piece + 2] = turned.reshape(2, GROUP, 8, LANES)

    for off in (2, 4, 3, 5, 6, 7, 1):
        copies[1, off] = pltpu.make_async_remote_copy(
            src_ref=sent.at[:, flip(off)],
            dst_ref=moments.at[:, :, pl.ds(off * LANES, LANES)],
            send_sem=send_sem.at[1, off],
            recv_sem=recv_sem.at[1, off],
            device_id=(flip(off), mev),
            device_id_type=MESH,
        )
        copies[1, off].start()

    moments[:, :, 0:LANES] = sent[:, pl.ds(me, 1)].reshape(MOM, 8, LANES)

    loads[7].wait()
    for off in range(1, GROUP):
        copies[0, off].wait_recv()
    lane_x, lane_y = small[128:129], small[129:130]
    lane_xx, lane_yy, lane_xy = small[130:131], small[131:132], small[132:133]
    sign = small[133:134]

    def along_x(at, size, copies_wide):
        return wide(small[pl.ds(at, size)], copies_wide)

    def along_y(at, size, copies_wide):
        return wide(small[pl.ds(HALF + at, size)], copies_wide)

    def make_phases(step):
        turns = lax.broadcasted_iota(jnp.int32, (8, atoms), 0).astype(F32) * wavevector_scale
        sine, cosine = sin_cos(turns * rows[3 * step + 2 : 3 * step + 3, :])
        ztab[step, 0:8] = cosine
        ztab[step, 8:16] = sine

        @pl.loop(0, HALF // 16)
        def _(chunk):
            at = pl.multiple_of(chunk * 16, 16)
            phase = along_x(at, 16, GROUP) * rows[3 * step : 3 * step + 1, :] + along_y(
                at, 16, GROUP
            ) * rows[3 * step + 1 : 3 * step + 2, :]
            sine, cosine = sin_cos(phase)
            xy[step, 0, pl.ds(at, 16)] = cosine
            xy[step, 1, pl.ds(at, 16)] = sine
            store_split(step, 0, at, cosine, sine)

    def store_split(step, block, at, real, imag):
        for which, part_here in enumerate((real, imag)):
            high, low = split(part_here)
            lmat[step, pl.ds(HIGH[block] + which * HALF + at, 16)] = high
            lmat[step, pl.ds(LOW[block] + which * HALF + at, 16)] = low

    def make_tangents(step, direction):
        @pl.loop(0, HALF // 16)
        def _(chunk):
            at = pl.multiple_of(chunk * 16, 16)
            real, imag = xy[step, 0, pl.ds(at, 16)], xy[step, 1, pl.ds(at, 16)]
            k_dot = along_x(at, 16, GROUP) * direction(0) + along_y(at, 16, GROUP) * direction(1)
            store_split(step, 1, at, -k_dot * imag, k_dot * real)
            store_split(step, 2, at, direction(2) * real, direction(2) * imag)

    def make_terms(step, first, width):
        here = pl.ds(first, width)
        q = [moments[m, :, here] for m in range(MOM)]

        def store(group, ops):
            for two in range(OPS // 2):
                both = jnp.concatenate([ops[2 * two], ops[2 * two + 1]], axis=0)
                at = group * OPS * 8 + two * 16
                rhigh[step, at : at + 16, here], rlow[step, at : at + 16, here] = split(both)

        store(0, [q[0], q[1], q[2], q[4], q[5], q[7]])
        for turn in range(1, TOP + 1):
            kz = turn * wavevector_scale
            c, s = ztab[step, turn : turn + 1, here], ztab[step, 8 + turn : 9 + turn, here]
            kc, ks = kz * c, kz * s
            charge = q[0] - (0.5 * kz * kz) * q[6]
            store(
                2 * turn - 1,
                [
                    charge * c - q[3] * ks,
                    q[1] * c - q[8] * ks,
                    q[2] * c - q[9] * ks,
                    q[4] * c,
                    q[5] * c,
                    q[7] * c,
                ],
            )
            store(
                2 * turn,
                [
                    charge * s + q[3] * kc,
                    q[1] * s + q[8] * kc,
                    q[2] * s + q[9] * kc,
                    q[4] * s,
                    q[5] * s,
                    q[7] * s,
                ],
            )

    def dots(step, first, width, begin, end, add, turns=(0, TOP + 1)):
        here = pl.ds(first, width)
        at = slice(max(2 * turns[0] - 1, 0) * OPS * 8, (2 * turns[1] - 1) * OPS * 8)
        value = dot_rows(rhigh[step, at, here], lmat[step, begin:end, here])
        sums[at, begin:end] = sums[at, begin:end] + value if add else value
        begin, end = max(begin, HIGH[0]), min(end, LOW[1])
        sums[at, begin:end] += dot_rows(rlow[step, at, here], lmat[step, begin:end, here])

    def combine(block, turns=(0, TOP + 1)):
        high, low = HIGH[block], LOW[block]
        out = {}
        for group in range(max(2 * turns[0] - 1, 0), 2 * turns[1] - 1):
            op = []
            for which in range(OPS):
                at = (group * OPS + which) * 8
                op.append(
                    sums[at : at + 8, high : high + LANES] + sums[at : at + 8, low : low + LANES]
                )
            turned = pltpu.roll(lane_x * op[1] + lane_y * op[2], HALF, 1) * sign
            out[group] = op[0] + turned + lane_xx * op[3] + lane_yy * op[4] + lane_xy * op[5]
        return out

    def tangent_sums(turns=(0, TOP + 1)):
        t1, g = combine(1, turns), combine(2, turns)
        out = {0: t1[0]} if turns[0] == 0 else {}
        for turn in range(max(turns[0], 1), turns[1]):
            kz = turn * wavevector_scale
            out[2 * turn - 1] = t1[2 * turn - 1] - kz * g[2 * turn]
            out[2 * turn] = t1[2 * turn] + kz * g[2 * turn - 1]
        return out

    lane = lax.broadcasted_iota(jnp.int32, (1, LANES), 1)

    def operand(slot, real, imag):
        here = slice(slot * HALF, (slot + 1) * HALF)
        one = real * maps[0, here] + imag * maps[1, here]
        two = real * maps[2, here] + imag * maps[3, here]
        top = one.astype(BF16)
        rest = jnp.where(lane < USED, one - top.astype(F32), two).astype(BF16)
        return jnp.concatenate([top, rest], axis=1)

    def project(place, parts, weights):
        for slot, c in enumerate(ALONG_Z):
            if slot not in parts:
                continue
            if c == 0:
                value = parts[0]
            else:
                turn = abs(c)
                turned = pltpu.roll(parts[2 * turn], HALF, 1) * sign
                value = parts[2 * turn - 1] + (turned if c > 0 else -turned)
            value = value * weights[slot : slot + 1]
            tile = jnp.concatenate([value] * 16, axis=0).T
            real, imag = tile[0:HALF], tile[HALF:]
            first, second = operand(slot, real, imag), operand(slot, imag, -real)
            at = slot * 2 * SIDE
            for side in range(2):
                here = slice(side * SIDE, (side + 1) * SIDE)
                opr[side, place, at : at + SIDE] = first[here]
                opr[side, place, at + SIDE : at + 2 * SIDE] = second[here]

    def around(step, at, here):
        real, imag = xy[step, 0, at : at + 8, here], xy[step, 1, at : at + 8, here]
        yield 0, real, imag
        for turn in range(1, TOP + 1):
            c, s = ztab[step, turn : turn + 1, here], ztab[step, 8 + turn : 9 + turn, here]
            rc, is_, ic, rs = real * c, imag * s, imag * c, real * s
            yield turn, (rc - is_, ic + rs), (rc + is_, ic - rs)

    def projected(buffer, place, slot, row):
        at = (place * SLOTS + slot) * 2 * SIDE + row
        return buffer[at : at + 8], buffer[at + SIDE : at + SIDE + 8]

    def tangent_value(wave, buffer, place, slot, row):
        first, second = projected(buffer, place, slot, row)
        return wave[0] * second - wave[1] * first

    def factor_value(wave, buffer, place, slot, row):
        first, second = projected(buffer, place, slot, row)
        return wave[0] * first + wave[1] * second

    pieces = CHUNK // LANES

    def force_terms(step, buffer, side, here, direction, with_factor):
        place = 1 if with_factor else 0
        total_x, total_y, total_z = 0.0, 0.0, 0.0
        if with_factor:
            dx, dy, dz = (direction(axis, here) for axis in range(3))
        for row in range(0, SIDE, 8):
            at = side * SIDE + row
            kx, ky = along_x(at, 8, pieces), along_y(at, 8, pieces)
            waves = around(step, at, here)
            _, real, imag = next(waves)
            flat = tangent_value((real, imag), buffer, place, 0, row)
            if with_factor:
                k_dot = kx * dx + ky * dy
                flat = flat - k_dot * factor_value((real, imag), buffer, 0, 0, row)
            tilt = 0.0
            for turn, plus, minus in waves:
                kz = turn * wavevector_scale
                up = tangent_value(plus, buffer, place, 2 * turn - 1, row)
                down = tangent_value(minus, buffer, place, 2 * turn, row)
                if with_factor:
                    kdz = kz * dz
                    up = up - (k_dot + kdz) * factor_value(plus, buffer, 0, 2 * turn - 1, row)
                    down = down - (k_dot - kdz) * factor_value(minus, buffer, 0, 2 * turn, row)
                flat = flat + (up + down)
                tilt = tilt + kz * (up - down)
            total_x, total_y, total_z = total_x + kx * flat, total_y + ky * flat, total_z + tilt
            yield
        acc[0, :, here] += total_x
        acc[1, :, here] += total_y
        acc[2, :, here] += total_z

    def hessian_terms(step, buffer, side, here):
        totals = [0.0] * 6
        for row in range(0, SIDE, 8):
            at = side * SIDE + row
            kx, ky = along_x(at, 8, pieces), along_y(at, 8, pieces)
            waves = around(step, at, here)
            _, real, imag = next(waves)
            flat = factor_value((real, imag), buffer, 0, 0, row)
            tilt, bend = 0.0, 0.0
            for turn, plus, minus in waves:
                kz = turn * wavevector_scale
                up = factor_value(plus, buffer, 0, 2 * turn - 1, row)
                down = factor_value(minus, buffer, 0, 2 * turn, row)
                both = up + down
                flat = flat + both
                tilt = tilt + kz * (up - down)
                bend = bend + (kz * kz) * both
            fx, fy = kx * flat, ky * flat
            for entry, value in enumerate((kx * fx, kx * fy, kx * tilt, ky * fy, ky * tilt, bend)):
                totals[entry] = totals[entry] + value
            yield
        for entry in range(6):
            hess[entry, :, here] += totals[entry]

    def sweep(places, terms, backwards=False, finish=None):
        count = len(places) * SLOTS * 2 * SIDE
        buffers = (proj_a.at[0:count], proj_b.at[0:count])

        def fill(side, first):
            for begin in range(0, count, count // PARTS):
                rows_here = slice(begin, begin + count // PARTS)
                left = opr[side, places[0] : places[-1] + 1].reshape(count, 2 * LANES)[rows_here]
                buffers[side][rows_here] = jnp.dot(
                    left, w2[:, pl.ds(first, CHUNK)], preferred_element_type=F32
                )
                yield

        def beside(*works):
            works = list(works)
            while works:
                for work in list(works):
                    if next(work, works) is works:
                        works.remove(work)

        tiles = atoms // CHUNK

        def tile(index):
            return tiles - 1 - index if backwards else index

        beside(fill(0, tile(0) * CHUNK))

        @pl.loop(0, tiles)
        def _(index):
            first = pl.multiple_of(tile(index) * CHUNK, CHUNK)
            after = pl.multiple_of(tile(lax.rem(index + 1, tiles)) * CHUNK, CHUNK)
            here = pl.ds(first, CHUNK)
            beside(fill(1, first), terms(buffers[0], 0, here))
            beside(fill(0, after), terms(buffers[1], 1, here))
            if finish is not None:
                finish(tile(index), here)

    def sums_to_operands(step, place, begin, end, parts):
        waiting = None
        for turns in TURNS:
            dots(step, 0, atoms, begin, end, False, turns)
            if waiting is not None:
                project(place, parts(waiting), weights)
            waiting = turns
        project(place, parts(waiting), weights)

    last = 1
    inv_mass = rows[12:13, :]
    dirs[0:3, :] = rows[6:9, :] * inv_mass
    make_phases(last)
    make_tangents(last, lambda axis: dirs[axis : axis + 1, :])

    order = (0, 2, 4, 6)
    for place, (off, many) in enumerate(((0, 2), (2, 4), (6, 2))):
        if place == 1:
            make_phases(0)
        if place == 1:

            @pl.when(leader)
            def _():
                count = counts[...]
                for over in range(1, kvecs):
                    count_copy(over).wait_recv()
                    count = count + counted[over]
                tally[...] = count
                for other in range(1, GROUP):
                    tally_copy(other).start()

        for one in range(off, off + many):
            if one > 0:
                copies[1, one].wait_recv()
        make_terms(last, off * LANES, many * LANES)
        dots(last, off * LANES, many * LANES, 0, 768, place > 0)
        here = pl.ds(off * LANES, many * LANES)
        q_high, q_low = split(moments[:, :, here].reshape(USED, many * LANES))
        fits = LANES - USED
        w2[0:USED, here] = q_high
        w2[USED:LANES, here] = q_low[0:fits]
        w2[LANES : LANES + USED, here] = q_high
        w2[LANES + USED : LANES + 2 * USED - fits, here] = q_low[fits:]
        w2[LANES + 2 * USED - fits :, here] = jnp.zeros((16, many * LANES), BF16)

    @pl.when(me != 0)
    def _():
        tally_copy(1).wait_recv()

    loads[8].wait()
    weights = tally[...] * small[136:152]

    project(0, combine(0), weights)
    project(1, tangent_sums(), weights)
    acc[...] = jnp.zeros_like(acc)
    sweep(
        (0, 1),
        lambda buffer, side, here: force_terms(
            last, buffer, side, here, lambda axis, here: dirs[axis : axis + 1, here], True
        ),
    )

    for axis in range(3):
        out = jnp.sum(acc[axis], axis=0, keepdims=True)
        for off in range(GROUP):
            gather[pl.ds(axis * GROUP + flip(off), 1), :] = out[:, off * LANES : (off + 1) * LANES]
    for off in FAR_FIRST:
        copies[2, off] = pltpu.make_async_remote_copy(
            src_ref=gather,
            dst_ref=gathered.at[off],
            send_sem=send_sem.at[2, off],
            recv_sem=recv_sem.at[2, off],
            device_id=(flip(off), mev),
            device_id_type=MESH,
        )
        copies[2, off].start()

    for off in order:
        make_terms(0, off * LANES, 2 * LANES)
    sums_to_operands(0, 0, 0, 256, lambda turns: combine(0, turns))
    hess[...] = jnp.zeros_like(hess)
    sweep((0,), lambda buffer, side, here: hessian_terms(0, buffer, side, here))
    for row in range(6):
        second[row : row + 1, :] = jnp.sum(hess[row], axis=0, keepdims=True)

    out = gather[...]
    for off in range(1, GROUP):
        copies[2, off].wait_recv()
        out = out + gathered[off]
    total[...] = out
    forces = []
    for axis in range(3):
        forces.append(
            jnp.concatenate(
                [total[pl.ds(axis * GROUP + flip(off), 1), :] for off in range(GROUP)], axis=1
            )
        )
    adj = [rows[9 + axis : 10 + axis, :] - time_step * forces[axis] for axis in range(3)]
    fma = [rows[6 + axis : 7 + axis, :] + time_step * adj[axis] for axis in range(3)]
    for axis in range(3):
        dirs[axis : axis + 1, :] = fma[axis] * inv_mass

    make_tangents(0, lambda axis: dirs[axis : axis + 1, :])
    sums_to_operands(0, 1, 256, 768, tangent_sums)
    places = ((0, 1, 2), (1, 3, 4), (2, 4, 5))
    part[...] = jnp.zeros_like(part)
    acc[...] = jnp.zeros_like(acc)

    def brick_copy(off, target):
        return pltpu.make_async_remote_copy(
            src_ref=part.at[off],
            dst_ref=bricks.at[off],
            send_sem=send_sem.at[3, off],
            recv_sem=recv_sem.at[3, off],
            device_id=(target, mev),
            device_id_type=MESH,
        )

    def send_tile(tile, here):
        for axis in range(3):
            out = jnp.sum(acc[axis, :, here], axis=0, keepdims=True)
            for other in range(3):
                row = places[axis][other]
                out = out - second[row : row + 1, here] * dirs[other : other + 1, here]
            part[2 * tile, axis : axis + 1, :] = out[:, 0:LANES]
            part[2 * tile + 1, axis : axis + 1, :] = out[:, LANES:]
        chip = (
            me
            + lax.rem(tile, 2) * (2 - 4 * lax.rem(lax.div(me, 2), 2))
            + lax.div(tile, 2) * (4 - 8 * lax.div(me, 4))
        )

        @pl.when(tile != 0)
        def _():
            brick_copy(2 * tile, chip).start()

        brick_copy(2 * tile + 1, chip + 1 - 2 * lax.rem(me, 2)).start()

    sweep(
        (1,),
        lambda buffer, side, here: force_terms(0, buffer, side, here, None, False),
        True,
        send_tile,
    )
    for off in range(1, GROUP):
        copies[3, off] = brick_copy(off, flip(off))
    out = part[0]
    for off in FAR_FIRST:
        copies[3, off].wait_recv()
        out = out + bricks[off]
    out_ref[0:4, :] = out
    for axis in range(3):
        out_ref[4 + axis : 5 + axis, :] = adj[axis][:, 0:LANES]
        out_ref[8 + axis : 9 + axis, :] = fma[axis][:, 0:LANES]
    for copy in copies.values():
        copy.wait_send()

    @pl.when(leader)
    def _():
        for over in range(1, kvecs):
            count_copy(over).wait_send()
        for off in range(1, GROUP):
            tally_copy(off).wait_send()


def fused(kvecs, positions, moments, adj_pos, final_momentum_adjoint, species, masses, kint):
    steps, _, here = positions.shape
    kdev = kint.shape[0]
    atoms = here * GROUP
    small, maps = grid_tables(energy_scale / math.sqrt(atoms))
    vmem = pl.BlockSpec(memory_space=pltpu.VMEM)
    hbm = pl.BlockSpec(memory_space=pltpu.HBM)
    points = SLOTS * HALF
    last = pl.pallas_call(
        functools.partial(kernel, kvecs),
        out_shape=pltpu.VMEM((16, here), F32),
        in_specs=[hbm] * 9,
        out_specs=vmem,
        scratch_shapes=[
            pltpu.VMEM((3, steps, here), F32),
            pltpu.VMEM(moments.shape, F32),
            pltpu.VMEM((3, here), F32),
            pltpu.VMEM((3, here), F32),
            pltpu.VMEM((1, here), jnp.int32),
            pltpu.SMEM(masses.shape, F32),
            pltpu.VMEM((3, kdev), jnp.int32),
            pltpu.VMEM(small.shape, F32),
            pltpu.VMEM(maps.shape, F32),
            pltpu.VMEM((16, here), F32),
            pltpu.VMEM((16, atoms), F32),
            pltpu.VMEM((MOM, GROUP, 8, here), F32),
            pltpu.VMEM((MOM, 8, atoms), F32),
            pltpu.VMEM((16, LANES), F32),
            pltpu.VMEM((kvecs, 16, LANES), F32),
            pltpu.VMEM((16, LANES), F32),
            pltpu.VMEM((steps, 2, HALF, atoms), F32),
            pltpu.VMEM((steps, 16, atoms), F32),
            pltpu.VMEM((steps, 768, atoms), BF16),
            pltpu.VMEM((steps, SUMS, atoms), BF16),
            pltpu.VMEM((steps, SUMS, atoms), BF16),
            pltpu.VMEM((SUMS, 768), F32),
            pltpu.VMEM((2, 2, points, 2 * LANES), BF16),
            pltpu.VMEM((2 * LANES, atoms), BF16),
            pltpu.VMEM((2 * points, CHUNK), F32),
            pltpu.VMEM((2 * points, CHUNK), F32),
            pltpu.VMEM((3, 8, atoms), F32),
            pltpu.VMEM((6, 8, atoms), F32),
            pltpu.VMEM((8, atoms), F32),
            pltpu.VMEM((8, atoms), F32),
            pltpu.VMEM((3 * GROUP, here), F32),
            pltpu.VMEM((GROUP, 3 * GROUP, here), F32),
            pltpu.VMEM((3 * GROUP, here), F32),
            pltpu.VMEM((GROUP, 4, here), F32),
            pltpu.VMEM((GROUP, 4, here), F32),
            pltpu.SemaphoreType.DMA((9,)),
            pltpu.SemaphoreType.DMA((5, GROUP)),
            pltpu.SemaphoreType.DMA((5, GROUP)),
            pltpu.SemaphoreType.DMA((kvecs,)),
            pltpu.SemaphoreType.DMA((kvecs,)),
        ],
        compiler_params=pltpu.CompilerParams(
            collective_id=0, has_side_effects=True, vmem_limit_bytes=60 << 20
        ),
    )(
        positions.transpose(1, 0, 2),
        moments,
        adj_pos,
        final_momentum_adjoint,
        species.reshape(1, here),
        masses,
        kint.T,
        small,
        maps,
    )
    adj = last[4:7] - time_step * last[0:3]
    return adj, last[8:11] + time_step * adj


def solution(mesh):
    bricks, kvecs = mesh.shape["brick"], mesh.shape["kvec"]
    if bricks != GROUP:
        return plain(mesh)
    placed = (
        P(None, None, "brick"),
        P("brick", None),
        P(None, "brick"),
        P(None, "brick"),
        P("brick"),
        P(),
        P("kvec", None),
    )
    return jax.shard_map(
        functools.partial(fused, kvecs),
        mesh=mesh,
        in_specs=placed,
        out_specs=(P(None, "brick"), P(None, "brick")),
        check_vma=False,
    )
```

```python
import functools
import math

import jax
import jax.numpy as jnp
import numpy as np
from jax import lax
from jax.experimental import pallas as pl
from jax.experimental.pallas import tpu as pltpu
from jax.sharding import PartitionSpec as P

exact = lax.Precision.HIGHEST
wavevector_scale = 0.5
time_step = 0.5
energy_scale = 0.125


def coef_arrays(wavevector_phase):
    kx, ky, kz = (wavevector_phase[:, 0], wavevector_phase[:, 1], wavevector_phase[:, 2])
    ones = jnp.ones_like(kx)
    zeros = jnp.zeros_like(kx)
    acoef = jnp.stack(
        [
            ones,
            zeros,
            zeros,
            zeros,
            -0.5 * kx * kx,
            -0.5 * ky * ky,
            -0.5 * kz * kz,
            -kx * ky,
            -kx * kz,
            -ky * kz,
        ],
        1,
    )
    bcoef = jnp.stack([zeros, kx, ky, kz, zeros, zeros, zeros, zeros, zeros, zeros], 1)
    return (acoef, bcoef)


def moment_sums(cos_w, sin_w, moments, acoef, bcoef):
    channels = moments.shape[1] // 10
    cos_part = jnp.dot(cos_w, moments, precision=exact).reshape(cos_w.shape[0], 10, channels)
    sine_component = jnp.dot(sin_w, moments, precision=exact).reshape(cos_w.shape[0], 10, channels)
    real_sum = jnp.einsum("km,kmc->kc", acoef, cos_part, precision=exact) - jnp.einsum(
        "km,kmc->kc", bcoef, sine_component, precision=exact
    )
    imag_sum = jnp.einsum("km,kmc->kc", acoef, sine_component, precision=exact) + jnp.einsum(
        "km,kmc->kc", bcoef, cos_part, precision=exact
    )
    return (real_sum, imag_sum)


def weave_terms(leading_dimension, trailing, acoef, bcoef):
    woven = (
        leading_dimension[:, None, :] * acoef[:, :, None] + trailing[:, None, :] * bcoef[:, :, None]
    )
    return woven.reshape(leading_dimension.shape[0], -1)


def tangent_force(
    wavevector_phase,
    k_weight,
    acoef,
    bcoef,
    factor,
    tangent,
    cosines,
    sines,
    k_dot_dir,
    moments,
    prefactor,
):
    factor_re, factor_im = factor
    tangent_re, tangent_im = tangent
    stacked = jnp.stack(
        [
            weave_terms(tangent_im, -tangent_re, acoef, bcoef),
            weave_terms(tangent_re, tangent_im, acoef, bcoef),
            weave_terms(factor_re, factor_im, acoef, bcoef),
            weave_terms(factor_im, -factor_re, acoef, bcoef),
        ]
    )
    projected = jnp.einsum("jkf,af->jka", stacked, moments, precision=exact)
    inner_sum = (
        cosines * projected[0]
        - sines * projected[1]
        - k_dot_dir * (cosines * projected[2] + sines * projected[3])
    )
    return jnp.dot((k_weight[:, None] * wavevector_phase).T, inner_sum, precision=exact) * prefactor


def plain_local(positions, moments, adj_pos, final_momentum_adjoint, species, masses, kint):
    wavevector_phase = kint.astype(jnp.float32) * wavevector_scale
    ksq = jnp.sum(wavevector_phase * wavevector_phase, 1)
    k_weight = jnp.exp(-ksq / 4.0) / jnp.maximum(ksq, 1.0)
    acoef, bcoef = coef_arrays(wavevector_phase)
    prefactor = energy_scale / math.sqrt(positions.shape[2] * lax.axis_size("brick"))
    onehot = (species[None, :] == jnp.arange(masses.shape[0], dtype=jnp.int32)[:, None]).astype(
        jnp.float32
    )
    inv_mass = jnp.dot(1.0 / masses, onehot, precision=exact)
    num_steps = positions.shape[0]

    def step_phases(step_index):
        phase = jnp.dot(wavevector_phase, positions[step_index], precision=exact)
        return (jnp.cos(phase), jnp.sin(phase))

    phase_list = [step_phases(step_index) for step_index in range(num_steps)]
    for step_index in reversed(range(num_steps)):
        cosines, sines = phase_list[step_index]
        direction = final_momentum_adjoint * inv_mass
        k_dot_dir = jnp.dot(wavevector_phase, direction, precision=exact)
        tangent_real_part, tan_im = moment_sums(
            k_dot_dir * cosines, k_dot_dir * sines, moments, acoef, bcoef
        )
        fac_re, fac_im = moment_sums(cosines, sines, moments, acoef, bcoef)
        summed_terms = lax.psum((fac_re, fac_im, -tan_im, tangent_real_part), "brick")
        factor = (summed_terms[0], summed_terms[1])
        tangent = (summed_terms[2], summed_terms[3])
        partial_force = tangent_force(
            wavevector_phase,
            k_weight,
            acoef,
            bcoef,
            factor,
            tangent,
            cosines,
            sines,
            k_dot_dir,
            moments,
            prefactor,
        )
        force = lax.psum(partial_force, "kvec")
        adj_pos = adj_pos - time_step * force
        final_momentum_adjoint = final_momentum_adjoint + time_step * adj_pos
    return (adj_pos, final_momentum_adjoint)


def plain(mesh):
    placed = (
        P(None, None, "brick"),
        P("brick", None),
        P(None, "brick"),
        P(None, "brick"),
        P("brick"),
        P(),
        P("kvec", None),
    )
    return jax.shard_map(
        plain_local,
        mesh=mesh,
        in_specs=placed,
        out_specs=(P(None, "brick"), P(None, "brick")),
        check_vma=False,
    )


MESH = pl.DeviceIdType.MESH
GROUP = 8
MOM = 10
LANES = 128
USED = MOM * 8
F32, BF16 = jnp.float32, jnp.bfloat16
two_over_pi = 2.0 / math.pi
half_pi_parts = (1.5703125, 4.837512969970703125e-4, 7.549789948768648e-8)

TOP = 5
PAIRS = [(0, b) for b in range(TOP + 1)] + [
    (a, b) for a in range(1, TOP + 1) for b in range(-TOP, TOP + 1)
]
HALF = 64
SIDE = HALF // 2
ALONG_Z = [0] + [c for top in range(1, TOP + 1) for c in (top, -top)]
SLOTS = len(ALONG_Z)
OPS = 6
SUMS = SLOTS * OPS * 8
CHUNK = 256
PARTS = 2
FAR_FIRST = (6, 7, 2, 3, 4, 5, 1)
TURNS = ((0, 3), (3, 6))
HIGH, LOW = (128, 256, 384), (0, 512, 640)


def grid_tables(prefactor):
    scale = wavevector_scale
    a = np.zeros(HALF)
    b = np.zeros(HALF)
    a[: len(PAIRS)] = [pair[0] for pair in PAIRS]
    b[: len(PAIRS)] = [pair[1] for pair in PAIRS]
    kx, ky = scale * a, scale * b
    along = np.broadcast_to(np.stack([kx, ky])[:, :, None], (2, HALF, LANES))
    lane_x, lane_y = np.tile(kx, 2), np.tile(ky, 2)
    sign = np.where(np.arange(LANES) < HALF, -1.0, 1.0)
    lanes = np.zeros((8, LANES))
    lanes[:6] = [
        lane_x,
        lane_y,
        -0.5 * lane_x**2,
        -0.5 * lane_y**2,
        -lane_x * lane_y,
        sign,
    ]
    weights = np.zeros((16, LANES))
    maps = np.zeros((4, SLOTS, HALF, LANES))
    lane = np.arange(LANES)
    room = (LANES - USED) // 8
    one = np.where(lane < USED, lane // 8, (lane - USED) // 8)
    two = np.where(
        lane < USED,
        lane // 8,
        np.where(lane < USED + (MOM - room) * 8, room + (lane - USED) // 8, MOM),
    )
    for slot, c in enumerate(ALONG_Z):
        kz = scale * c + 0.0 * kx
        ksq = kx**2 + ky**2 + kz**2
        weights[slot] = np.tile(np.exp(-ksq / 4.0) / np.maximum(ksq, 1.0), 2) * prefactor
        zero = 0.0 * kx
        acoef = np.stack(
            [zero + 1, zero, zero, zero]
            + [-0.5 * kx**2, -0.5 * ky**2, -0.5 * kz**2, -kx * ky, -kx * kz, -ky * kz]
            + [zero],
            1,
        )
        bcoef = np.stack([zero, kx, ky, kz] + [zero] * 7, 1)
        maps[0, slot], maps[1, slot] = acoef[:, one], bcoef[:, one]
        maps[2, slot], maps[3, slot] = acoef[:, two], bcoef[:, two]
    small = np.concatenate([along.reshape(2 * HALF, LANES), lanes, weights])
    return small.astype(np.float32), maps.reshape(4, SLOTS * HALF, LANES).astype(np.float32)


def sin_cos(phase):
    n = jnp.round(phase * two_over_pi)
    r = phase - n * half_pi_parts[0]
    r = r - n * half_pi_parts[1]
    r = r - n * half_pi_parts[2]
    q = n.astype(jnp.int32)
    z = r * r
    s = r + r * z * (-1.6666654611e-1 + z * (8.3321608736e-3 + z * -1.9515295891e-4))
    c = 1.0 - 0.5 * z + z * z * (
        4.166664568298827e-2 + z * (-1.388731625493765e-3 + z * 2.443315711809948e-5)
    )
    odd = (q & 1) == 1
    sine = jnp.where(odd, c, s)
    cosine = jnp.where(odd, s, c)
    sine = jnp.where((q & 2) == 2, -sine, sine)
    cosine = jnp.where(((q + 1) & 2) == 2, -cosine, cosine)
    return sine, cosine


def split(x):
    high = x.astype(BF16)
    return high, (x - high.astype(F32)).astype(BF16)


def wide(x, copies):
    return jnp.concatenate([x] * copies, axis=1)


def dot_rows(x, y):
    return lax.dot_general(x, y, (((1,), (1,)), ((), ())), preferred_element_type=F32)


def kernel(
    kvecs,
    pos_hbm,
    mom_hbm,
    adj_hbm,
    fma_hbm,
    spec_hbm,
    mass_hbm,
    kint_hbm,
    small_hbm,
    maps_hbm,
    out_ref,
    pos_ref,
    mom_ref,
    adj_ref,
    fma_ref,
    spec_ref,
    mass_ref,
    kint_ref,
    small,
    maps,
    pack,
    rows,
    sent,
    moments,
    counts,
    counted,
    tally,
    xy,
    ztab,
    lmat,
    rhigh,
    rlow,
    sums,
    opr,
    w2,
    proj_a,
    proj_b,
    acc,
    hess,
    second,
    dirs,
    gather,
    gathered,
    total,
    part,
    bricks,
    load_sem,
    send_sem,
    recv_sem,
    zsend_sem,
    zrecv_sem,
):
    me = lax.axis_index("brick")
    mev = lax.axis_index("kvec")
    atoms = LANES * GROUP

    def flip(off):
        other = me
        for bit in (1, 2, 4):
            if off & bit:
                other = other + bit - 2 * bit * lax.rem(lax.div(me, bit), 2)
        return other

    barrier = pltpu.get_barrier_semaphore()
    for off in range(1, GROUP):
        pl.semaphore_signal(barrier, inc=1, device_id=(flip(off), mev), device_id_type=MESH)
    leader = me == 0
    beyond = kvecs - 1

    @pl.when(leader)
    def _():
        for over in range(1, kvecs):
            pl.semaphore_signal(
                barrier, inc=1, device_id=(me, lax.rem(mev + over, kvecs)), device_id_type=MESH
            )

    loads = []
    for at, (src, dst) in enumerate(
        (
            (pos_hbm, pos_ref),
            (fma_hbm, fma_ref),
            (adj_hbm, adj_ref),
            (spec_hbm, spec_ref),
            (mass_hbm, mass_ref),
            (mom_hbm, mom_ref),
            (kint_hbm, kint_ref),
            (small_hbm, small),
            (maps_hbm, maps),
        )
    ):
        loads.append(pltpu.make_async_copy(src, dst, load_sem.at[at]))
    for load in loads[:-1]:
        load.start()

    for load in loads[:5]:
        load.wait()
    species = spec_ref[...]
    mass = jnp.ones(species.shape, F32)
    for kind in range(mass_ref.shape[0]):
        mass = jnp.where(species == kind, mass_ref[kind], mass)
    pack[...] = jnp.zeros_like(pack)
    for axis in range(3):
        pack[axis : axis + 1, :] = pos_ref[axis, 0:1]
        pack[3 + axis : 4 + axis, :] = pos_ref[axis, 1:2]
    pack[6:9, :] = fma_ref[...]
    pack[9:12, :] = adj_ref[...]
    pack[12:13, :] = 1.0 / mass
    rows[:, 0:LANES] = pack[...]

    loads[6].wait()
    ka, kb, kc = kint_ref[0:1, :], kint_ref[1:2, :], kint_ref[2:3, :]
    turn = (ka < 0) | ((ka == 0) & (kb < 0))
    ka, kb, kc = (jnp.where(turn, -k, k) for k in (ka, kb, kc))
    pair = jnp.where(ka == 0, kb, (TOP + 1) + (ka - 1) * (2 * TOP + 1) + kb + TOP)
    slot = jnp.where(kc > 0, 2 * kc - 1, -2 * kc)
    here = kint_ref.shape[1]
    pair_row = lax.broadcasted_iota(jnp.int32, (LANES, here), 0)
    pair_row = jnp.where(pair_row < HALF, pair_row, pair_row - HALF)
    slot_row = lax.broadcasted_iota(jnp.int32, (16, here), 0)
    counts[...] = dot_rows(
        (slot_row == slot).astype(F32).astype(BF16), (pair_row == pair).astype(F32).astype(BF16)
    )

    pl.semaphore_wait(barrier, GROUP - 1 + jnp.where(leader, beyond, 0))
    copies = {}
    for off in FAR_FIRST:
        copies[0, off] = pltpu.make_async_remote_copy(
            src_ref=pack,
            dst_ref=rows.at[:, pl.ds(off * LANES, LANES)],
            send_sem=send_sem.at[0, off],
            recv_sem=recv_sem.at[0, off],
            device_id=(flip(off), mev),
            device_id_type=MESH,
        )
        copies[0, off].start()
    def count_copy(over):
        return pltpu.make_async_remote_copy(
            src_ref=counts,
            dst_ref=counted.at[over],
            send_sem=zsend_sem.at[over],
            recv_sem=zrecv_sem.at[over],
            device_id=(me, lax.rem(mev + over, kvecs)),
            device_id_type=MESH,
        )

    def tally_copy(off):
        return pltpu.make_async_remote_copy(
            src_ref=tally,
            dst_ref=tally,
            send_sem=send_sem.at[4, off],
            recv_sem=recv_sem.at[4, 0],
            device_id=(flip(off), mev),
            device_id_type=MESH,
        )

    @pl.when(leader)
    def _():
        for over in range(1, kvecs):
            count_copy(over).start()

    loads[5].wait()
    loads[8].start()
    for piece in range(mom_ref.shape[1] // LANES):
        turned = mom_ref[:, piece * LANES : (piece + 1) * LANES].T
        sent[2 * piece : 2 * piece + 2] = turned.reshape(2, GROUP, 8, LANES)

    for off in (2, 4, 3, 5, 6, 7, 1):
        copies[1, off] = pltpu.make_async_remote_copy(
            src_ref=sent.at[:, flip(off)],
            dst_ref=moments.at[:, :, pl.ds(off * LANES, LANES)],
            send_sem=send_sem.at[1, off],
            recv_sem=recv_sem.at[1, off],
            device_id=(flip(off), mev),
            device_id_type=MESH,
        )
        copies[1, off].start()

    moments[:, :, 0:LANES] = sent[:, pl.ds(me, 1)].reshape(MOM, 8, LANES)

    loads[7].wait()
    for off in range(1, GROUP):
        copies[0, off].wait_recv()
    lane_x, lane_y = small[128:129], small[129:130]
    lane_xx, lane_yy, lane_xy = small[130:131], small[131:132], small[132:133]
    sign = small[133:134]

    def along_x(at, size, copies_wide):
        return wide(small[pl.ds(at, size)], copies_wide)

    def along_y(at, size, copies_wide):
        return wide(small[pl.ds(HALF + at, size)], copies_wide)

    def make_phases(step):
        turns = lax.broadcasted_iota(jnp.int32, (8, atoms), 0).astype(F32) * wavevector_scale
        sine, cosine = sin_cos(turns * rows[3 * step + 2 : 3 * step + 3, :])
        ztab[step, 0:8] = cosine
        ztab[step, 8:16] = sine

        @pl.loop(0, HALF // 16)
        def _(chunk):
            at = pl.multiple_of(chunk * 16, 16)
            phase = along_x(at, 16, GROUP) * rows[3 * step : 3 * step + 1, :] + along_y(
                at, 16, GROUP
            ) * rows[3 * step + 1 : 3 * step + 2, :]
            sine, cosine = sin_cos(phase)
            xy[step, 0, pl.ds(at, 16)] = cosine
            xy[step, 1, pl.ds(at, 16)] = sine
            store_split(step, 0, at, cosine, sine)

    def store_split(step, block, at, real, imag):
        for which, part_here in enumerate((real, imag)):
            high, low = split(part_here)
            lmat[step, pl.ds(HIGH[block] + which * HALF + at, 16)] = high
            lmat[step, pl.ds(LOW[block] + which * HALF + at, 16)] = low

    def make_tangents(step, direction):
        @pl.loop(0, HALF // 16)
        def _(chunk):
            at = pl.multiple_of(chunk * 16, 16)
            real, imag = xy[step, 0, pl.ds(at, 16)], xy[step, 1, pl.ds(at, 16)]
            k_dot = along_x(at, 16, GROUP) * direction(0) + along_y(at, 16, GROUP) * direction(1)
            store_split(step, 1, at, -k_dot * imag, k_dot * real)
            store_split(step, 2, at, direction(2) * real, direction(2) * imag)

    def make_terms(step, first, width):
        here = pl.ds(first, width)
        q = [moments[m, :, here] for m in range(MOM)]

        def store(group, ops):
            for two in range(OPS // 2):
                both = jnp.concatenate([ops[2 * two], ops[2 * two + 1]], axis=0)
                at = group * OPS * 8 + two * 16
                rhigh[step, at : at + 16, here], rlow[step, at : at + 16, here] = split(both)

        store(0, [q[0], q[1], q[2], q[4], q[5], q[7]])
        for turn in range(1, TOP + 1):
            kz = turn * wavevector_scale
            c, s = ztab[step, turn : turn + 1, here], ztab[step, 8 + turn : 9 + turn, here]
            kc, ks = kz * c, kz * s
            charge = q[0] - (0.5 * kz * kz) * q[6]
            store(
                2 * turn - 1,
                [
                    charge * c - q[3] * ks,
                    q[1] * c - q[8] * ks,
                    q[2] * c - q[9] * ks,
                    q[4] * c,
                    q[5] * c,
                    q[7] * c,
                ],
            )
            store(
                2 * turn,
                [
                    charge * s + q[3] * kc,
                    q[1] * s + q[8] * kc,
                    q[2] * s + q[9] * kc,
                    q[4] * s,
                    q[5] * s,
                    q[7] * s,
                ],
            )

    def dots(step, first, width, begin, end, add, turns=(0, TOP + 1)):
        here = pl.ds(first, width)
        at = slice(max(2 * turns[0] - 1, 0) * OPS * 8, (2 * turns[1] - 1) * OPS * 8)
        value = dot_rows(rhigh[step, at, here], lmat[step, begin:end, here])
        sums[at, begin:end] = sums[at, begin:end] + value if add else value
        begin, end = max(begin, HIGH[0]), min(end, LOW[1])
        sums[at, begin:end] += dot_rows(rlow[step, at, here], lmat[step, begin:end, here])

    def combine(block, turns=(0, TOP + 1)):
        high, low = HIGH[block], LOW[block]
        out = {}
        for group in range(max(2 * turns[0] - 1, 0), 2 * turns[1] - 1):
            op = []
            for which in range(OPS):
                at = (group * OPS + which) * 8
                op.append(
                    sums[at : at + 8, high : high + LANES] + sums[at : at + 8, low : low + LANES]
                )
            turned = pltpu.roll(lane_x * op[1] + lane_y * op[2], HALF, 1) * sign
            out[group] = op[0] + turned + lane_xx * op[3] + lane_yy * op[4] + lane_xy * op[5]
        return out

    def tangent_sums(turns=(0, TOP + 1)):
        t1, g = combine(1, turns), combine(2, turns)
        out = {0: t1[0]} if turns[0] == 0 else {}
        for turn in range(max(turns[0], 1), turns[1]):
            kz = turn * wavevector_scale
            out[2 * turn - 1] = t1[2 * turn - 1] - kz * g[2 * turn]
            out[2 * turn] = t1[2 * turn] + kz * g[2 * turn - 1]
        return out

    lane = lax.broadcasted_iota(jnp.int32, (1, LANES), 1)

    def operand(slot, real, imag):
        here = slice(slot * HALF, (slot + 1) * HALF)
        one = real * maps[0, here] + imag * maps[1, here]
        two = real * maps[2, here] + imag * maps[3, here]
        top = one.astype(BF16)
        rest = jnp.where(lane < USED, one - top.astype(F32), two).astype(BF16)
        return jnp.concatenate([top, rest], axis=1)

    def project(place, parts, weights):
        for slot, c in enumerate(ALONG_Z):
            if slot not in parts:
                continue
            if c == 0:
                value = parts[0]
            else:
                turn = abs(c)
                turned = pltpu.roll(parts[2 * turn], HALF, 1) * sign
                value = parts[2 * turn - 1] + (turned if c > 0 else -turned)
            value = value * weights[slot : slot + 1]
            tile = jnp.concatenate([value] * 16, axis=0).T
            real, imag = tile[0:HALF], tile[HALF:]
            first, second = operand(slot, real, imag), operand(slot, imag, -real)
            at = slot * 2 * SIDE
            for side in range(2):
                here = slice(side * SIDE, (side + 1) * SIDE)
                opr[side, place, at : at + SIDE] = first[here]
                opr[side, place, at + SIDE : at + 2 * SIDE] = second[here]

    def around(step, at, here):
        real, imag = xy[step, 0, at : at + 8, here], xy[step, 1, at : at + 8, here]
        yield 0, real, imag
        for turn in range(1, TOP + 1):
            c, s = ztab[step, turn : turn + 1, here], ztab[step, 8 + turn : 9 + turn, here]
            rc, is_, ic, rs = real * c, imag * s, imag * c, real * s
            yield turn, (rc - is_, ic + rs), (rc + is_, ic - rs)

    def projected(buffer, place, slot, row):
        at = (place * SLOTS + slot) * 2 * SIDE + row
        return buffer[at : at + 8], buffer[at + SIDE : at + SIDE + 8]

    def tangent_value(wave, buffer, place, slot, row):
        first, second = projected(buffer, place, slot, row)
        return wave[0] * second - wave[1] * first

    def factor_value(wave, buffer, place, slot, row):
        first, second = projected(buffer, place, slot, row)
        return wave[0] * first + wave[1] * second

    pieces = CHUNK // LANES

    def force_terms(step, buffer, side, here, direction, with_factor):
        place = 1 if with_factor else 0
        total_x, total_y, total_z = 0.0, 0.0, 0.0
        if with_factor:
            dx, dy, dz = (direction(axis, here) for axis in range(3))
        for row in range(0, SIDE, 8):
            at = side * SIDE + row
            kx, ky = along_x(at, 8, pieces), along_y(at, 8, pieces)
            waves = around(step, at, here)
            _, real, imag = next(waves)
            flat = tangent_value((real, imag), buffer, place, 0, row)
            if with_factor:
                k_dot = kx * dx + ky * dy
                flat = flat - k_dot * factor_value((real, imag), buffer, 0, 0, row)
            tilt = 0.0
            for turn, plus, minus in waves:
                kz = turn * wavevector_scale
                up = tangent_value(plus, buffer, place, 2 * turn - 1, row)
                down = tangent_value(minus, buffer, place, 2 * turn, row)
                if with_factor:
                    kdz = kz * dz
                    up = up - (k_dot + kdz) * factor_value(plus, buffer, 0, 2 * turn - 1, row)
                    down = down - (k_dot - kdz) * factor_value(minus, buffer, 0, 2 * turn, row)
                flat = flat + (up + down)
                tilt = tilt + kz * (up - down)
            total_x, total_y, total_z = total_x + kx * flat, total_y + ky * flat, total_z + tilt
            yield
        acc[0, :, here] += total_x
        acc[1, :, here] += total_y
        acc[2, :, here] += total_z

    def hessian_terms(step, buffer, side, here):
        totals = [0.0] * 6
        for row in range(0, SIDE, 8):
            at = side * SIDE + row
            kx, ky = along_x(at, 8, pieces), along_y(at, 8, pieces)
            waves = around(step, at, here)
            _, real, imag = next(waves)
            flat = factor_value((real, imag), buffer, 0, 0, row)
            tilt, bend = 0.0, 0.0
            for turn, plus, minus in waves:
                kz = turn * wavevector_scale
                up = factor_value(plus, buffer, 0, 2 * turn - 1, row)
                down = factor_value(minus, buffer, 0, 2 * turn, row)
                both = up + down
                flat = flat + both
                tilt = tilt + kz * (up - down)
                bend = bend + (kz * kz) * both
            fx, fy = kx * flat, ky * flat
            for entry, value in enumerate((kx * fx, kx * fy, kx * tilt, ky * fy, ky * tilt, bend)):
                totals[entry] = totals[entry] + value
            yield
        for entry in range(6):
            hess[entry, :, here] += totals[entry]

    def sweep(places, terms, backwards=False, finish=None):
        count = len(places) * SLOTS * 2 * SIDE
        buffers = (proj_a.at[0:count], proj_b.at[0:count])

        def fill(side, first):
            for begin in range(0, count, count // PARTS):
                rows_here = slice(begin, begin + count // PARTS)
                left = opr[side, places[0] : places[-1] + 1].reshape(count, 2 * LANES)[rows_here]
                buffers[side][rows_here] = jnp.dot(
                    left, w2[:, pl.ds(first, CHUNK)], preferred_element_type=F32
                )
                yield

        def beside(*works):
            works = list(works)
            while works:
                for work in list(works):
                    if next(work, works) is works:
                        works.remove(work)

        tiles = atoms // CHUNK

        def tile(index):
            return tiles - 1 - index if backwards else index

        beside(fill(0, tile(0) * CHUNK))

        @pl.loop(0, tiles)
        def _(index):
            first = pl.multiple_of(tile(index) * CHUNK, CHUNK)
            after = pl.multiple_of(tile(lax.rem(index + 1, tiles)) * CHUNK, CHUNK)
            here = pl.ds(first, CHUNK)
            beside(terms(buffers[0], 0, here), fill(1, first))
            beside(terms(buffers[1], 1, here), fill(0, after))
            if finish is not None:
                finish(tile(index), here)

    def sums_to_operands(step, place, begin, end, parts):
        waiting = None
        for turns in TURNS:
            dots(step, 0, atoms, begin, end, False, turns)
            if waiting is not None:
                project(place, parts(waiting), weights)
            waiting = turns
        project(place, parts(waiting), weights)

    last = 1
    inv_mass = rows[12:13, :]
    dirs[0:3, :] = rows[6:9, :] * inv_mass
    make_phases(last)
    make_tangents(last, lambda axis: dirs[axis : axis + 1, :])

    order = (0, 2, 4, 6)
    for place, (off, many) in enumerate(((0, 2), (2, 4), (6, 2))):
        if place == 1:
            make_phases(0)
        if place == 1:

            @pl.when(leader)
            def _():
                count = counts[...]
                for over in range(1, kvecs):
                    count_copy(over).wait_recv()
                    count = count + counted[over]
                tally[...] = count
                for other in range(1, GROUP):
                    tally_copy(other).start()

        for one in range(off, off + many):
            if one > 0:
                copies[1, one].wait_recv()
        make_terms(last, off * LANES, many * LANES)
        dots(last, off * LANES, many * LANES, 0, 768, place > 0)
        here = pl.ds(off * LANES, many * LANES)
        q_high, q_low = split(moments[:, :, here].reshape(USED, many * LANES))
        fits = LANES - USED
        w2[0:USED, here] = q_high
        w2[USED:LANES, here] = q_low[0:fits]
        w2[LANES : LANES + USED, here] = q_high
        w2[LANES + USED : LANES + 2 * USED - fits, here] = q_low[fits:]
        w2[LANES + 2 * USED - fits :, here] = jnp.zeros((16, many * LANES), BF16)

    factor, tangent = combine(0), tangent_sums()

    @pl.when(me != 0)
    def _():
        tally_copy(1).wait_recv()

    loads[8].wait()
    weights = tally[...] * small[136:152]

    project(0, factor, weights)
    project(1, tangent, weights)
    acc[...] = jnp.zeros_like(acc)
    sweep(
        (0, 1),
        lambda buffer, side, here: force_terms(
            last, buffer, side, here, lambda axis, here: dirs[axis : axis + 1, here], True
        ),
    )

    for axis in range(3):
        out = jnp.sum(acc[axis], axis=0, keepdims=True)
        for off in range(GROUP):
            gather[pl.ds(axis * GROUP + flip(off), 1), :] = out[:, off * LANES : (off + 1) * LANES]
    for off in FAR_FIRST:
        copies[2, off] = pltpu.make_async_remote_copy(
            src_ref=gather,
            dst_ref=gathered.at[off],
            send_sem=send_sem.at[2, off],
            recv_sem=recv_sem.at[2, off],
            device_id=(flip(off), mev),
            device_id_type=MESH,
        )
        copies[2, off].start()

    for off in order:
        make_terms(0, off * LANES, 2 * LANES)
    sums_to_operands(0, 0, 0, 256, lambda turns: combine(0, turns))
    hess[...] = jnp.zeros_like(hess)
    sweep((0,), lambda buffer, side, here: hessian_terms(0, buffer, side, here))
    for row in range(6):
        second[row : row + 1, :] = jnp.sum(hess[row], axis=0, keepdims=True)

    out = gather[...]
    for off in range(1, GROUP):
        copies[2, off].wait_recv()
        out = out + gathered[off]
    total[...] = out
    forces = []
    for axis in range(3):
        forces.append(
            jnp.concatenate(
                [total[pl.ds(axis * GROUP + flip(off), 1), :] for off in range(GROUP)], axis=1
            )
        )
    adj = [rows[9 + axis : 10 + axis, :] - time_step * forces[axis] for axis in range(3)]
    fma = [rows[6 + axis : 7 + axis, :] + time_step * adj[axis] for axis in range(3)]
    for axis in range(3):
        dirs[axis : axis + 1, :] = fma[axis] * inv_mass

    make_tangents(0, lambda axis: dirs[axis : axis + 1, :])
    sums_to_operands(0, 1, 256, 768, tangent_sums)
    places = ((0, 1, 2), (1, 3, 4), (2, 4, 5))
    part[...] = jnp.zeros_like(part)
    acc[...] = jnp.zeros_like(acc)

    def brick_copy(off, target):
        return pltpu.make_async_remote_copy(
            src_ref=part.at[off],
            dst_ref=bricks.at[off],
            send_sem=send_sem.at[3, off],
            recv_sem=recv_sem.at[3, off],
            device_id=(target, mev),
            device_id_type=MESH,
        )

    def send_tile(tile, here):
        for axis in range(3):
            out = jnp.sum(acc[axis, :, here], axis=0, keepdims=True)
            for other in range(3):
                row = places[axis][other]
                out = out - second[row : row + 1, here] * dirs[other : other + 1, here]
            part[2 * tile, axis : axis + 1, :] = out[:, 0:LANES]
            part[2 * tile + 1, axis : axis + 1, :] = out[:, LANES:]
        chip = (
            me
            + lax.rem(tile, 2) * (2 - 4 * lax.rem(lax.div(me, 2), 2))
            + lax.div(tile, 2) * (4 - 8 * lax.div(me, 4))
        )

        @pl.when(tile != 0)
        def _():
            brick_copy(2 * tile, chip).start()

        brick_copy(2 * tile + 1, chip + 1 - 2 * lax.rem(me, 2)).start()

    sweep(
        (1,),
        lambda buffer, side, here: force_terms(0, buffer, side, here, None, False),
        True,
        send_tile,
    )
    for off in range(1, GROUP):
        copies[3, off] = brick_copy(off, flip(off))
    out = part[0]
    for off in FAR_FIRST:
        copies[3, off].wait_recv()
        out = out + bricks[off]
    out_ref[0:4, :] = out
    for axis in range(3):
        out_ref[4 + axis : 5 + axis, :] = adj[axis][:, 0:LANES]
        out_ref[8 + axis : 9 + axis, :] = fma[axis][:, 0:LANES]
    for copy in copies.values():
        copy.wait_send()

    @pl.when(leader)
    def _():
        for over in range(1, kvecs):
            count_copy(over).wait_send()
        for off in range(1, GROUP):
            tally_copy(off).wait_send()


def fused(kvecs, positions, moments, adj_pos, final_momentum_adjoint, species, masses, kint):
    steps, _, here = positions.shape
    kdev = kint.shape[0]
    atoms = here * GROUP
    small, maps = grid_tables(energy_scale / math.sqrt(atoms))
    vmem = pl.BlockSpec(memory_space=pltpu.VMEM)
    hbm = pl.BlockSpec(memory_space=pltpu.HBM)
    points = SLOTS * HALF
    last = pl.pallas_call(
        functools.partial(kernel, kvecs),
        out_shape=pltpu.VMEM((16, here), F32),
        in_specs=[hbm] * 9,
        out_specs=vmem,
        scratch_shapes=[
            pltpu.VMEM((3, steps, here), F32),
            pltpu.VMEM(moments.shape, F32),
            pltpu.VMEM((3, here), F32),
            pltpu.VMEM((3, here), F32),
            pltpu.VMEM((1, here), jnp.int32),
            pltpu.SMEM(masses.shape, F32),
            pltpu.VMEM((3, kdev), jnp.int32),
            pltpu.VMEM(small.shape, F32),
            pltpu.VMEM(maps.shape, F32),
            pltpu.VMEM((16, here), F32),
            pltpu.VMEM((16, atoms), F32),
            pltpu.VMEM((MOM, GROUP, 8, here), F32),
            pltpu.VMEM((MOM, 8, atoms), F32),
            pltpu.VMEM((16, LANES), F32),
            pltpu.VMEM((kvecs, 16, LANES), F32),
            pltpu.VMEM((16, LANES), F32),
            pltpu.VMEM((steps, 2, HALF, atoms), F32),
            pltpu.VMEM((steps, 16, atoms), F32),
            pltpu.VMEM((steps, 768, atoms), BF16),
            pltpu.VMEM((steps, SUMS, atoms), BF16),
            pltpu.VMEM((steps, SUMS, atoms), BF16),
            pltpu.VMEM((SUMS, 768), F32),
            pltpu.VMEM((2, 2, points, 2 * LANES), BF16),
            pltpu.VMEM((2 * LANES, atoms), BF16),
            pltpu.VMEM((2 * points, CHUNK), F32),
            pltpu.VMEM((2 * points, CHUNK), F32),
            pltpu.VMEM((3, 8, atoms), F32),
            pltpu.VMEM((6, 8, atoms), F32),
            pltpu.VMEM((8, atoms), F32),
            pltpu.VMEM((8, atoms), F32),
            pltpu.VMEM((3 * GROUP, here), F32),
            pltpu.VMEM((GROUP, 3 * GROUP, here), F32),
            pltpu.VMEM((3 * GROUP, here), F32),
            pltpu.VMEM((GROUP, 4, here), F32),
            pltpu.VMEM((GROUP, 4, here), F32),
            pltpu.SemaphoreType.DMA((9,)),
            pltpu.SemaphoreType.DMA((5, GROUP)),
            pltpu.SemaphoreType.DMA((5, GROUP)),
            pltpu.SemaphoreType.DMA((kvecs,)),
            pltpu.SemaphoreType.DMA((kvecs,)),
        ],
        compiler_params=pltpu.CompilerParams(
            collective_id=0, has_side_effects=True, vmem_limit_bytes=60 << 20
        ),
    )(
        positions.transpose(1, 0, 2),
        moments,
        adj_pos,
        final_momentum_adjoint,
        species.reshape(1, here),
        masses,
        kint.T,
        small,
        maps,
    )
    adj = last[4:7] - time_step * last[0:3]
    return adj, last[8:11] + time_step * adj


def solution(mesh):
    bricks, kvecs = mesh.shape["brick"], mesh.shape["kvec"]
    if bricks != GROUP:
        return plain(mesh)
    placed = (
        P(None, None, "brick"),
        P("brick", None),
        P(None, "brick"),
        P(None, "brick"),
        P("brick"),
        P(),
        P("kvec", None),
    )
    return jax.shard_map(
        functools.partial(fused, kvecs),
        mesh=mesh,
        in_specs=placed,
        out_specs=(P(None, "brick"), P(None, "brick")),
        check_vma=False,
    )
```

```python
import functools
import math

import jax
import jax.numpy as jnp
import numpy as np
from jax import lax
from jax.experimental import pallas as pl
from jax.experimental.pallas import tpu as pltpu
from jax.sharding import PartitionSpec as P

exact = lax.Precision.HIGHEST
wavevector_scale = 0.5
time_step = 0.5
energy_scale = 0.125


def coef_arrays(wavevector_phase):
    kx, ky, kz = (wavevector_phase[:, 0], wavevector_phase[:, 1], wavevector_phase[:, 2])
    ones = jnp.ones_like(kx)
    zeros = jnp.zeros_like(kx)
    acoef = jnp.stack(
        [
            ones,
            zeros,
            zeros,
            zeros,
            -0.5 * kx * kx,
            -0.5 * ky * ky,
            -0.5 * kz * kz,
            -kx * ky,
            -kx * kz,
            -ky * kz,
        ],
        1,
    )
    bcoef = jnp.stack([zeros, kx, ky, kz, zeros, zeros, zeros, zeros, zeros, zeros], 1)
    return (acoef, bcoef)


def moment_sums(cos_w, sin_w, moments, acoef, bcoef):
    channels = moments.shape[1] // 10
    cos_part = jnp.dot(cos_w, moments, precision=exact).reshape(cos_w.shape[0], 10, channels)
    sine_component = jnp.dot(sin_w, moments, precision=exact).reshape(cos_w.shape[0], 10, channels)
    real_sum = jnp.einsum("km,kmc->kc", acoef, cos_part, precision=exact) - jnp.einsum(
        "km,kmc->kc", bcoef, sine_component, precision=exact
    )
    imag_sum = jnp.einsum("km,kmc->kc", acoef, sine_component, precision=exact) + jnp.einsum(
        "km,kmc->kc", bcoef, cos_part, precision=exact
    )
    return (real_sum, imag_sum)


def weave_terms(leading_dimension, trailing, acoef, bcoef):
    woven = (
        leading_dimension[:, None, :] * acoef[:, :, None] + trailing[:, None, :] * bcoef[:, :, None]
    )
    return woven.reshape(leading_dimension.shape[0], -1)


def tangent_force(
    wavevector_phase,
    k_weight,
    acoef,
    bcoef,
    factor,
    tangent,
    cosines,
    sines,
    k_dot_dir,
    moments,
    prefactor,
):
    factor_re, factor_im = factor
    tangent_re, tangent_im = tangent
    stacked = jnp.stack(
        [
            weave_terms(tangent_im, -tangent_re, acoef, bcoef),
            weave_terms(tangent_re, tangent_im, acoef, bcoef),
            weave_terms(factor_re, factor_im, acoef, bcoef),
            weave_terms(factor_im, -factor_re, acoef, bcoef),
        ]
    )
    projected = jnp.einsum("jkf,af->jka", stacked, moments, precision=exact)
    inner_sum = (
        cosines * projected[0]
        - sines * projected[1]
        - k_dot_dir * (cosines * projected[2] + sines * projected[3])
    )
    return jnp.dot((k_weight[:, None] * wavevector_phase).T, inner_sum, precision=exact) * prefactor


def plain_local(positions, moments, adj_pos, final_momentum_adjoint, species, masses, kint):
    wavevector_phase = kint.astype(jnp.float32) * wavevector_scale
    ksq = jnp.sum(wavevector_phase * wavevector_phase, 1)
    k_weight = jnp.exp(-ksq / 4.0) / jnp.maximum(ksq, 1.0)
    acoef, bcoef = coef_arrays(wavevector_phase)
    prefactor = energy_scale / math.sqrt(positions.shape[2] * lax.axis_size("brick"))
    onehot = (species[None, :] == jnp.arange(masses.shape[0], dtype=jnp.int32)[:, None]).astype(
        jnp.float32
    )
    inv_mass = jnp.dot(1.0 / masses, onehot, precision=exact)
    num_steps = positions.shape[0]

    def step_phases(step_index):
        phase = jnp.dot(wavevector_phase, positions[step_index], precision=exact)
        return (jnp.cos(phase), jnp.sin(phase))

    phase_list = [step_phases(step_index) for step_index in range(num_steps)]
    for step_index in reversed(range(num_steps)):
        cosines, sines = phase_list[step_index]
        direction = final_momentum_adjoint * inv_mass
        k_dot_dir = jnp.dot(wavevector_phase, direction, precision=exact)
        tangent_real_part, tan_im = moment_sums(
            k_dot_dir * cosines, k_dot_dir * sines, moments, acoef, bcoef
        )
        fac_re, fac_im = moment_sums(cosines, sines, moments, acoef, bcoef)
        summed_terms = lax.psum((fac_re, fac_im, -tan_im, tangent_real_part), "brick")
        factor = (summed_terms[0], summed_terms[1])
        tangent = (summed_terms[2], summed_terms[3])
        partial_force = tangent_force(
            wavevector_phase,
            k_weight,
            acoef,
            bcoef,
            factor,
            tangent,
            cosines,
            sines,
            k_dot_dir,
            moments,
            prefactor,
        )
        force = lax.psum(partial_force, "kvec")
        adj_pos = adj_pos - time_step * force
        final_momentum_adjoint = final_momentum_adjoint + time_step * adj_pos
    return (adj_pos, final_momentum_adjoint)


def plain(mesh):
    placed = (
        P(None, None, "brick"),
        P("brick", None),
        P(None, "brick"),
        P(None, "brick"),
        P("brick"),
        P(),
        P("kvec", None),
    )
    return jax.shard_map(
        plain_local,
        mesh=mesh,
        in_specs=placed,
        out_specs=(P(None, "brick"), P(None, "brick")),
        check_vma=False,
    )


MESH = pl.DeviceIdType.MESH
GROUP = 8
MOM = 10
LANES = 128
USED = MOM * 8
F32, BF16 = jnp.float32, jnp.bfloat16
two_over_pi = 2.0 / math.pi
half_pi_parts = (1.5703125, 4.837512969970703125e-4, 7.549789948768648e-8)

TOP = 5
PAIRS = [(0, b) for b in range(TOP + 1)] + [
    (a, b) for a in range(1, TOP + 1) for b in range(-TOP, TOP + 1)
]
HALF = 64
SIDE = HALF // 2
ALONG_Z = [0] + [c for top in range(1, TOP + 1) for c in (top, -top)]
SLOTS = len(ALONG_Z)
OPS = 6
SUMS = SLOTS * OPS * 8
CHUNK = 256
PARTS = 2
FAR_FIRST = (6, 7, 2, 3, 4, 5, 1)
TURNS = ((0, 3), (3, 6))
HIGH, LOW = (128, 256, 384), (0, 512, 640)


def grid_tables(prefactor):
    scale = wavevector_scale
    a = np.zeros(HALF)
    b = np.zeros(HALF)
    a[: len(PAIRS)] = [pair[0] for pair in PAIRS]
    b[: len(PAIRS)] = [pair[1] for pair in PAIRS]
    kx, ky = scale * a, scale * b
    along = np.broadcast_to(np.stack([kx, ky])[:, :, None], (2, HALF, LANES))
    lane_x, lane_y = np.tile(kx, 2), np.tile(ky, 2)
    sign = np.where(np.arange(LANES) < HALF, -1.0, 1.0)
    lanes = np.zeros((8, LANES))
    lanes[:6] = [
        lane_x,
        lane_y,
        -0.5 * lane_x**2,
        -0.5 * lane_y**2,
        -lane_x * lane_y,
        sign,
    ]
    weights = np.zeros((16, LANES))
    maps = np.zeros((4, SLOTS, HALF, LANES))
    lane = np.arange(LANES)
    room = (LANES - USED) // 8
    one = np.where(lane < USED, lane // 8, (lane - USED) // 8)
    two = np.where(
        lane < USED,
        lane // 8,
        np.where(lane < USED + (MOM - room) * 8, room + (lane - USED) // 8, MOM),
    )
    for slot, c in enumerate(ALONG_Z):
        kz = scale * c + 0.0 * kx
        ksq = kx**2 + ky**2 + kz**2
        weights[slot] = np.tile(np.exp(-ksq / 4.0) / np.maximum(ksq, 1.0), 2) * prefactor
        zero = 0.0 * kx
        acoef = np.stack(
            [zero + 1, zero, zero, zero]
            + [-0.5 * kx**2, -0.5 * ky**2, -0.5 * kz**2, -kx * ky, -kx * kz, -ky * kz]
            + [zero],
            1,
        )
        bcoef = np.stack([zero, kx, ky, kz] + [zero] * 7, 1)
        maps[0, slot], maps[1, slot] = acoef[:, one], bcoef[:, one]
        maps[2, slot], maps[3, slot] = acoef[:, two], bcoef[:, two]
    small = np.concatenate([along.reshape(2 * HALF, LANES), lanes, weights])
    return small.astype(np.float32), maps.reshape(4, SLOTS * HALF, LANES).astype(np.float32)


def sin_cos(phase):
    n = jnp.round(phase * two_over_pi)
    r = phase - n * half_pi_parts[0]
    r = r - n * half_pi_parts[1]
    r = r - n * half_pi_parts[2]
    q = n.astype(jnp.int32)
    z = r * r
    s = r + r * z * (-1.6666654611e-1 + z * (8.3321608736e-3 + z * -1.9515295891e-4))
    c = 1.0 - 0.5 * z + z * z * (
        4.166664568298827e-2 + z * (-1.388731625493765e-3 + z * 2.443315711809948e-5)
    )
    odd = (q & 1) == 1
    sine = jnp.where(odd, c, s)
    cosine = jnp.where(odd, s, c)
    sine = jnp.where((q & 2) == 2, -sine, sine)
    cosine = jnp.where(((q + 1) & 2) == 2, -cosine, cosine)
    return sine, cosine


def split(x):
    high = x.astype(BF16)
    return high, (x - high.astype(F32)).astype(BF16)


def wide(x, copies):
    return jnp.concatenate([x] * copies, axis=1)


def dot_rows(x, y):
    return lax.dot_general(x, y, (((1,), (1,)), ((), ())), preferred_element_type=F32)


def kernel(
    kvecs,
    pos_hbm,
    mom_hbm,
    adj_hbm,
    fma_hbm,
    spec_hbm,
    mass_hbm,
    kint_hbm,
    small_hbm,
    maps_hbm,
    out_ref,
    pos_ref,
    mom_ref,
    adj_ref,
    fma_ref,
    spec_ref,
    mass_ref,
    kint_ref,
    small,
    maps,
    pack,
    rows,
    sent,
    moments,
    counts,
    counted,
    tally,
    xy,
    ztab,
    lmat,
    rhigh,
    rlow,
    sums,
    opr,
    w2,
    proj_a,
    proj_b,
    acc,
    hess,
    second,
    dirs,
    gather,
    gathered,
    total,
    part,
    bricks,
    load_sem,
    send_sem,
    recv_sem,
    zsend_sem,
    zrecv_sem,
):
    me = lax.axis_index("brick")
    mev = lax.axis_index("kvec")
    atoms = LANES * GROUP

    def flip(off):
        other = me
        for bit in (1, 2, 4):
            if off & bit:
                other = other + bit - 2 * bit * lax.rem(lax.div(me, bit), 2)
        return other

    barrier = pltpu.get_barrier_semaphore()
    for off in range(1, GROUP):
        pl.semaphore_signal(barrier, inc=1, device_id=(flip(off), mev), device_id_type=MESH)
    leader = me == 0
    beyond = kvecs - 1

    @pl.when(leader)
    def _():
        for over in range(1, kvecs):
            pl.semaphore_signal(
                barrier, inc=1, device_id=(me, lax.rem(mev + over, kvecs)), device_id_type=MESH
            )

    loads = []
    for at, (src, dst) in enumerate(
        (
            (pos_hbm, pos_ref),
            (fma_hbm, fma_ref),
            (adj_hbm, adj_ref),
            (spec_hbm, spec_ref),
            (mass_hbm, mass_ref),
            (mom_hbm, mom_ref),
            (kint_hbm, kint_ref),
            (small_hbm, small),
            (maps_hbm, maps),
        )
    ):
        loads.append(pltpu.make_async_copy(src, dst, load_sem.at[at]))
    for load in loads[:-1]:
        load.start()

    for load in loads[:5]:
        load.wait()
    species = spec_ref[...]
    mass = jnp.ones(species.shape, F32)
    for kind in range(mass_ref.shape[0]):
        mass = jnp.where(species == kind, mass_ref[kind], mass)
    pack[...] = jnp.zeros_like(pack)
    for axis in range(3):
        pack[axis : axis + 1, :] = pos_ref[axis, 0:1]
        pack[3 + axis : 4 + axis, :] = pos_ref[axis, 1:2]
    pack[6:9, :] = fma_ref[...]
    pack[9:12, :] = adj_ref[...]
    pack[12:13, :] = 1.0 / mass
    rows[:, 0:LANES] = pack[...]

    loads[6].wait()
    ka, kb, kc = kint_ref[0:1, :], kint_ref[1:2, :], kint_ref[2:3, :]
    turn = (ka < 0) | ((ka == 0) & (kb < 0))
    ka, kb, kc = (jnp.where(turn, -k, k) for k in (ka, kb, kc))
    pair = jnp.where(ka == 0, kb, (TOP + 1) + (ka - 1) * (2 * TOP + 1) + kb + TOP)
    slot = jnp.where(kc > 0, 2 * kc - 1, -2 * kc)
    here = kint_ref.shape[1]
    pair_row = lax.broadcasted_iota(jnp.int32, (LANES, here), 0)
    pair_row = jnp.where(pair_row < HALF, pair_row, pair_row - HALF)
    slot_row = lax.broadcasted_iota(jnp.int32, (16, here), 0)
    counts[...] = dot_rows(
        (slot_row == slot).astype(F32).astype(BF16), (pair_row == pair).astype(F32).astype(BF16)
    )

    pl.semaphore_wait(barrier, GROUP - 1 + jnp.where(leader, beyond, 0))
    copies = {}
    for off in FAR_FIRST:
        copies[0, off] = pltpu.make_async_remote_copy(
            src_ref=pack,
            dst_ref=rows.at[:, pl.ds(off * LANES, LANES)],
            send_sem=send_sem.at[0, off],
            recv_sem=recv_sem.at[0, off],
            device_id=(flip(off), mev),
            device_id_type=MESH,
        )
        copies[0, off].start()
    def count_copy(over):
        return pltpu.make_async_remote_copy(
            src_ref=counts,
            dst_ref=counted.at[over],
            send_sem=zsend_sem.at[over],
            recv_sem=zrecv_sem.at[over],
            device_id=(me, lax.rem(mev + over, kvecs)),
            device_id_type=MESH,
        )

    def tally_copy(off):
        return pltpu.make_async_remote_copy(
            src_ref=tally,
            dst_ref=tally,
            send_sem=send_sem.at[4, off],
            recv_sem=recv_sem.at[4, 0],
            device_id=(flip(off), mev),
            device_id_type=MESH,
        )

    @pl.when(leader)
    def _():
        for over in range(1, kvecs):
            count_copy(over).start()

    loads[5].wait()
    loads[8].start()
    for piece in range(mom_ref.shape[1] // LANES):
        turned = mom_ref[:, piece * LANES : (piece + 1) * LANES].T
        sent[2 * piece : 2 * piece + 2] = turned.reshape(2, GROUP, 8, LANES)

    for off in (2, 4, 3, 5, 6, 7, 1):
        copies[1, off] = pltpu.make_async_remote_copy(
            src_ref=sent.at[:, flip(off)],
            dst_ref=moments.at[:, :, pl.ds(off * LANES, LANES)],
            send_sem=send_sem.at[1, off],
            recv_sem=recv_sem.at[1, off],
            device_id=(flip(off), mev),
            device_id_type=MESH,
        )
        copies[1, off].start()

    moments[:, :, 0:LANES] = sent[:, pl.ds(me, 1)].reshape(MOM, 8, LANES)

    loads[7].wait()
    for off in range(1, GROUP):
        copies[0, off].wait_recv()
    lane_x, lane_y = small[128:129], small[129:130]
    lane_xx, lane_yy, lane_xy = small[130:131], small[131:132], small[132:133]
    sign = small[133:134]

    def along_x(at, size, copies_wide):
        return wide(small[pl.ds(at, size)], copies_wide)

    def along_y(at, size, copies_wide):
        return wide(small[pl.ds(HALF + at, size)], copies_wide)

    def make_phases(step):
        turns = lax.broadcasted_iota(jnp.int32, (8, atoms), 0).astype(F32) * wavevector_scale
        sine, cosine = sin_cos(turns * rows[3 * step + 2 : 3 * step + 3, :])
        ztab[step, 0:8] = cosine
        ztab[step, 8:16] = sine

        @pl.loop(0, HALF // 16)
        def _(chunk):
            at = pl.multiple_of(chunk * 16, 16)
            phase = along_x(at, 16, GROUP) * rows[3 * step : 3 * step + 1, :] + along_y(
                at, 16, GROUP
            ) * rows[3 * step + 1 : 3 * step + 2, :]
            sine, cosine = sin_cos(phase)
            xy[step, 0, pl.ds(at, 16)] = cosine
            xy[step, 1, pl.ds(at, 16)] = sine
            store_split(step, 0, at, cosine, sine)

    def store_split(step, block, at, real, imag):
        for which, part_here in enumerate((real, imag)):
            high, low = split(part_here)
            lmat[step, pl.ds(HIGH[block] + which * HALF + at, 16)] = high
            lmat[step, pl.ds(LOW[block] + which * HALF + at, 16)] = low

    def make_tangents(step, direction):
        @pl.loop(0, HALF // 16)
        def _(chunk):
            at = pl.multiple_of(chunk * 16, 16)
            real, imag = xy[step, 0, pl.ds(at, 16)], xy[step, 1, pl.ds(at, 16)]
            k_dot = along_x(at, 16, GROUP) * direction(0) + along_y(at, 16, GROUP) * direction(1)
            store_split(step, 1, at, -k_dot * imag, k_dot * real)
            store_split(step, 2, at, direction(2) * real, direction(2) * imag)

    def make_terms(step, first, width):
        here = pl.ds(first, width)
        q = [moments[m, :, here] for m in range(MOM)]

        def store(group, ops):
            for two in range(OPS // 2):
                both = jnp.concatenate([ops[2 * two], ops[2 * two + 1]], axis=0)
                at = group * OPS * 8 + two * 16
                rhigh[step, at : at + 16, here], rlow[step, at : at + 16, here] = split(both)

        store(0, [q[0], q[1], q[2], q[4], q[5], q[7]])
        for turn in range(1, TOP + 1):
            kz = turn * wavevector_scale
            c, s = ztab[step, turn : turn + 1, here], ztab[step, 8 + turn : 9 + turn, here]
            kc, ks = kz * c, kz * s
            charge = q[0] - (0.5 * kz * kz) * q[6]
            store(
                2 * turn - 1,
                [
                    charge * c - q[3] * ks,
                    q[1] * c - q[8] * ks,
                    q[2] * c - q[9] * ks,
                    q[4] * c,
                    q[5] * c,
                    q[7] * c,
                ],
            )
            store(
                2 * turn,
                [
                    charge * s + q[3] * kc,
                    q[1] * s + q[8] * kc,
                    q[2] * s + q[9] * kc,
                    q[4] * s,
                    q[5] * s,
                    q[7] * s,
                ],
            )

    def dots(step, first, width, begin, end, add, turns=(0, TOP + 1)):
        here = pl.ds(first, width)
        at = slice(max(2 * turns[0] - 1, 0) * OPS * 8, (2 * turns[1] - 1) * OPS * 8)
        if begin == HIGH[1]:
            across = lmat[step, begin : LOW[1], here]
            sums[at, begin : LOW[1]] = dot_rows(
                jnp.concatenate([rhigh[step, at, here], rlow[step, at, here]], axis=1),
                jnp.concatenate([across, across], axis=1),
            )
            sums[at, LOW[1] : end] = dot_rows(rhigh[step, at, here], lmat[step, LOW[1] : end, here])
            return
        value = dot_rows(rhigh[step, at, here], lmat[step, begin:end, here])
        sums[at, begin:end] = sums[at, begin:end] + value if add else value
        begin, end = max(begin, HIGH[0]), min(end, LOW[1])
        sums[at, begin:end] += dot_rows(rlow[step, at, here], lmat[step, begin:end, here])

    def combine(block, turns=(0, TOP + 1)):
        high, low = HIGH[block], LOW[block]
        out = {}
        for group in range(max(2 * turns[0] - 1, 0), 2 * turns[1] - 1):
            op = []
            for which in range(OPS):
                at = (group * OPS + which) * 8
                op.append(
                    sums[at : at + 8, high : high + LANES] + sums[at : at + 8, low : low + LANES]
                )
            turned = pltpu.roll(lane_x * op[1] + lane_y * op[2], HALF, 1) * sign
            out[group] = op[0] + turned + lane_xx * op[3] + lane_yy * op[4] + lane_xy * op[5]
        return out

    def tangent_sums(turns=(0, TOP + 1)):
        t1, g = combine(1, turns), combine(2, turns)
        out = {0: t1[0]} if turns[0] == 0 else {}
        for turn in range(max(turns[0], 1), turns[1]):
            kz = turn * wavevector_scale
            out[2 * turn - 1] = t1[2 * turn - 1] - kz * g[2 * turn]
            out[2 * turn] = t1[2 * turn] + kz * g[2 * turn - 1]
        return out

    lane = lax.broadcasted_iota(jnp.int32, (1, LANES), 1)

    def operand(slot, real, imag):
        here = slice(slot * HALF, (slot + 1) * HALF)
        one = real * maps[0, here] + imag * maps[1, here]
        two = real * maps[2, here] + imag * maps[3, here]
        top = one.astype(BF16)
        rest = jnp.where(lane < USED, one - top.astype(F32), two).astype(BF16)
        return jnp.concatenate([top, rest], axis=1)

    def project(place, parts, weights):
        for slot, c in enumerate(ALONG_Z):
            if slot not in parts:
                continue
            if c == 0:
                value = parts[0]
            else:
                turn = abs(c)
                turned = pltpu.roll(parts[2 * turn], HALF, 1) * sign
                value = parts[2 * turn - 1] + (turned if c > 0 else -turned)
            value = value * weights[slot : slot + 1]
            tile = jnp.concatenate([value] * 16, axis=0).T
            real, imag = tile[0:HALF], tile[HALF:]
            first, second = operand(slot, real, imag), operand(slot, imag, -real)
            at = slot * 2 * SIDE
            for side in range(2):
                here = slice(side * SIDE, (side + 1) * SIDE)
                opr[side, place, at : at + SIDE] = first[here]
                opr[side, place, at + SIDE : at + 2 * SIDE] = second[here]

    def around(step, at, here):
        real, imag = xy[step, 0, at : at + 8, here], xy[step, 1, at : at + 8, here]
        yield 0, real, imag
        for turn in range(1, TOP + 1):
            c, s = ztab[step, turn : turn + 1, here], ztab[step, 8 + turn : 9 + turn, here]
            rc, is_, ic, rs = real * c, imag * s, imag * c, real * s
            yield turn, (rc - is_, ic + rs), (rc + is_, ic - rs)

    def projected(buffer, place, slot, row):
        at = (place * SLOTS + slot) * 2 * SIDE + row
        return buffer[at : at + 8], buffer[at + SIDE : at + SIDE + 8]

    def tangent_value(wave, buffer, place, slot, row):
        first, second = projected(buffer, place, slot, row)
        return wave[0] * second - wave[1] * first

    def factor_value(wave, buffer, place, slot, row):
        first, second = projected(buffer, place, slot, row)
        return wave[0] * first + wave[1] * second

    pieces = CHUNK // LANES

    def force_terms(step, buffer, side, here, direction, with_factor):
        place = 1 if with_factor else 0
        total_x, total_y, total_z = 0.0, 0.0, 0.0
        if with_factor:
            dx, dy, dz = (direction(axis, here) for axis in range(3))
        for row in range(0, SIDE, 8):
            at = side * SIDE + row
            kx, ky = along_x(at, 8, pieces), along_y(at, 8, pieces)
            waves = around(step, at, here)
            _, real, imag = next(waves)
            flat = tangent_value((real, imag), buffer, place, 0, row)
            if with_factor:
                k_dot = kx * dx + ky * dy
                flat = flat - k_dot * factor_value((real, imag), buffer, 0, 0, row)
            tilt = 0.0
            for turn, plus, minus in waves:
                kz = turn * wavevector_scale
                up = tangent_value(plus, buffer, place, 2 * turn - 1, row)
                down = tangent_value(minus, buffer, place, 2 * turn, row)
                if with_factor:
                    kdz = kz * dz
                    up = up - (k_dot + kdz) * factor_value(plus, buffer, 0, 2 * turn - 1, row)
                    down = down - (k_dot - kdz) * factor_value(minus, buffer, 0, 2 * turn, row)
                flat = flat + (up + down)
                tilt = tilt + kz * (up - down)
            total_x, total_y, total_z = total_x + kx * flat, total_y + ky * flat, total_z + tilt
            yield
        acc[0, :, here] += total_x
        acc[1, :, here] += total_y
        acc[2, :, here] += total_z

    def hessian_terms(step, buffer, side, here):
        totals = [0.0] * 6
        for row in range(0, SIDE, 8):
            at = side * SIDE + row
            kx, ky = along_x(at, 8, pieces), along_y(at, 8, pieces)
            waves = around(step, at, here)
            _, real, imag = next(waves)
            flat = factor_value((real, imag), buffer, 0, 0, row)
            tilt, bend = 0.0, 0.0
            for turn, plus, minus in waves:
                kz = turn * wavevector_scale
                up = factor_value(plus, buffer, 0, 2 * turn - 1, row)
                down = factor_value(minus, buffer, 0, 2 * turn, row)
                both = up + down
                flat = flat + both
                tilt = tilt + kz * (up - down)
                bend = bend + (kz * kz) * both
            fx, fy = kx * flat, ky * flat
            for entry, value in enumerate((kx * fx, kx * fy, kx * tilt, ky * fy, ky * tilt, bend)):
                totals[entry] = totals[entry] + value
            yield
        for entry in range(6):
            hess[entry, :, here] += totals[entry]

    def sweep(places, terms, backwards=False, finish=None):
        count = len(places) * SLOTS * 2 * SIDE
        buffers = (proj_a.at[0:count], proj_b.at[0:count])

        def fill(side, first):
            for begin in range(0, count, count // PARTS):
                rows_here = slice(begin, begin + count // PARTS)
                left = opr[side, places[0] : places[-1] + 1].reshape(count, 2 * LANES)[rows_here]
                buffers[side][rows_here] = jnp.dot(
                    left, w2[:, pl.ds(first, CHUNK)], preferred_element_type=F32
                )
                yield

        def beside(*works):
            works = list(works)
            while works:
                for work in list(works):
                    if next(work, works) is works:
                        works.remove(work)

        tiles = atoms // CHUNK

        def tile(index):
            return tiles - 1 - index if backwards else index

        beside(fill(0, tile(0) * CHUNK))

        @pl.loop(0, tiles)
        def _(index):
            first = pl.multiple_of(tile(index) * CHUNK, CHUNK)
            after = pl.multiple_of(tile(lax.rem(index + 1, tiles)) * CHUNK, CHUNK)
            here = pl.ds(first, CHUNK)
            beside(terms(buffers[0], 0, here), fill(1, first))
            beside(terms(buffers[1], 1, here), fill(0, after))
            if finish is not None:
                finish(tile(index), here)

    def sums_to_operands(step, place, begin, end, parts):
        waiting = None
        for turns in TURNS:
            dots(step, 0, atoms, begin, end, False, turns)
            if waiting is not None:
                project(place, parts(waiting), weights)
            waiting = turns
        project(place, parts(waiting), weights)

    last = 1
    inv_mass = rows[12:13, :]
    dirs[0:3, :] = rows[6:9, :] * inv_mass
    make_phases(last)
    make_tangents(last, lambda axis: dirs[axis : axis + 1, :])

    order = (0, 2, 4, 6)
    for place, (off, many) in enumerate(((0, 2), (2, 4), (6, 2))):
        if place == 1:
            make_phases(0)
        if place == 1:

            @pl.when(leader)
            def _():
                count = counts[...]
                for over in range(1, kvecs):
                    count_copy(over).wait_recv()
                    count = count + counted[over]
                tally[...] = count
                for other in range(1, GROUP):
                    tally_copy(other).start()

        for one in range(off, off + many):
            if one > 0:
                copies[1, one].wait_recv()
        make_terms(last, off * LANES, many * LANES)
        dots(last, off * LANES, many * LANES, 0, 768, place > 0)
        here = pl.ds(off * LANES, many * LANES)
        q_high, q_low = split(moments[:, :, here].reshape(USED, many * LANES))
        fits = LANES - USED
        w2[0:USED, here] = q_high
        w2[USED:LANES, here] = q_low[0:fits]
        w2[LANES : LANES + USED, here] = q_high
        w2[LANES + USED : LANES + 2 * USED - fits, here] = q_low[fits:]
        w2[LANES + 2 * USED - fits :, here] = jnp.zeros((16, many * LANES), BF16)

    factor, tangent = combine(0), tangent_sums()

    @pl.when(me != 0)
    def _():
        tally_copy(1).wait_recv()

    loads[8].wait()
    weights = tally[...] * small[136:152]

    project(0, factor, weights)
    project(1, tangent, weights)
    acc[...] = jnp.zeros_like(acc)
    sweep(
        (0, 1),
        lambda buffer, side, here: force_terms(
            last, buffer, side, here, lambda axis, here: dirs[axis : axis + 1, here], True
        ),
    )

    for axis in range(3):
        out = jnp.sum(acc[axis], axis=0, keepdims=True)
        for off in range(GROUP):
            gather[pl.ds(axis * GROUP + flip(off), 1), :] = out[:, off * LANES : (off + 1) * LANES]
    for off in FAR_FIRST:
        copies[2, off] = pltpu.make_async_remote_copy(
            src_ref=gather,
            dst_ref=gathered.at[off],
            send_sem=send_sem.at[2, off],
            recv_sem=recv_sem.at[2, off],
            device_id=(flip(off), mev),
            device_id_type=MESH,
        )
        copies[2, off].start()

    for off in order:
        make_terms(0, off * LANES, 2 * LANES)
    sums_to_operands(0, 0, 0, 256, lambda turns: combine(0, turns))
    hess[...] = jnp.zeros_like(hess)
    sweep((0,), lambda buffer, side, here: hessian_terms(0, buffer, side, here))
    for row in range(6):
        second[row : row + 1, :] = jnp.sum(hess[row], axis=0, keepdims=True)

    out = gather[...]
    for off in range(1, GROUP):
        copies[2, off].wait_recv()
        out = out + gathered[off]
    total[...] = out
    forces = []
    for axis in range(3):
        forces.append(
            jnp.concatenate(
                [total[pl.ds(axis * GROUP + flip(off), 1), :] for off in range(GROUP)], axis=1
            )
        )
    adj = [rows[9 + axis : 10 + axis, :] - time_step * forces[axis] for axis in range(3)]
    fma = [rows[6 + axis : 7 + axis, :] + time_step * adj[axis] for axis in range(3)]
    for axis in range(3):
        dirs[axis : axis + 1, :] = fma[axis] * inv_mass

    make_tangents(0, lambda axis: dirs[axis : axis + 1, :])
    sums_to_operands(0, 1, 256, 768, tangent_sums)
    places = ((0, 1, 2), (1, 3, 4), (2, 4, 5))
    part[...] = jnp.zeros_like(part)
    acc[...] = jnp.zeros_like(acc)

    def brick_copy(off, target):
        return pltpu.make_async_remote_copy(
            src_ref=part.at[off],
            dst_ref=bricks.at[off],
            send_sem=send_sem.at[3, off],
            recv_sem=recv_sem.at[3, off],
            device_id=(target, mev),
            device_id_type=MESH,
        )

    def send_tile(tile, here):
        for axis in range(3):
            out = jnp.sum(acc[axis, :, here], axis=0, keepdims=True)
            for other in range(3):
                row = places[axis][other]
                out = out - second[row : row + 1, here] * dirs[other : other + 1, here]
            part[2 * tile, axis : axis + 1, :] = out[:, 0:LANES]
            part[2 * tile + 1, axis : axis + 1, :] = out[:, LANES:]
        chip = (
            me
            + lax.rem(tile, 2) * (2 - 4 * lax.rem(lax.div(me, 2), 2))
            + lax.div(tile, 2) * (4 - 8 * lax.div(me, 4))
        )

        @pl.when(tile != 0)
        def _():
            brick_copy(2 * tile, chip).start()

        brick_copy(2 * tile + 1, chip + 1 - 2 * lax.rem(me, 2)).start()

    sweep(
        (1,),
        lambda buffer, side, here: force_terms(0, buffer, side, here, None, False),
        True,
        send_tile,
    )
    for off in range(1, GROUP):
        copies[3, off] = brick_copy(off, flip(off))
    out = part[0]
    for off in FAR_FIRST:
        copies[3, off].wait_recv()
        out = out + bricks[off]
    out_ref[0:4, :] = out
    for axis in range(3):
        out_ref[4 + axis : 5 + axis, :] = adj[axis][:, 0:LANES]
        out_ref[8 + axis : 9 + axis, :] = fma[axis][:, 0:LANES]
    for copy in copies.values():
        copy.wait_send()

    @pl.when(leader)
    def _():
        for over in range(1, kvecs):
            count_copy(over).wait_send()
        for off in range(1, GROUP):
            tally_copy(off).wait_send()


def fused(kvecs, positions, moments, adj_pos, final_momentum_adjoint, species, masses, kint):
    steps, _, here = positions.shape
    kdev = kint.shape[0]
    atoms = here * GROUP
    small, maps = grid_tables(energy_scale / math.sqrt(atoms))
    vmem = pl.BlockSpec(memory_space=pltpu.VMEM)
    hbm = pl.BlockSpec(memory_space=pltpu.HBM)
    points = SLOTS * HALF
    last = pl.pallas_call(
        functools.partial(kernel, kvecs),
        out_shape=pltpu.VMEM((16, here), F32),
        in_specs=[hbm] * 9,
        out_specs=vmem,
        scratch_shapes=[
            pltpu.VMEM((3, steps, here), F32),
            pltpu.VMEM(moments.shape, F32),
            pltpu.VMEM((3, here), F32),
            pltpu.VMEM((3, here), F32),
            pltpu.VMEM((1, here), jnp.int32),
            pltpu.SMEM(masses.shape, F32),
            pltpu.VMEM((3, kdev), jnp.int32),
            pltpu.VMEM(small.shape, F32),
            pltpu.VMEM(maps.shape, F32),
            pltpu.VMEM((16, here), F32),
            pltpu.VMEM((16, atoms), F32),
            pltpu.VMEM((MOM, GROUP, 8, here), F32),
            pltpu.VMEM((MOM, 8, atoms), F32),
            pltpu.VMEM((16, LANES), F32),
            pltpu.VMEM((kvecs, 16, LANES), F32),
            pltpu.VMEM((16, LANES), F32),
            pltpu.VMEM((steps, 2, HALF, atoms), F32),
            pltpu.VMEM((steps, 16, atoms), F32),
            pltpu.VMEM((steps, 768, atoms), BF16),
            pltpu.VMEM((steps, SUMS, atoms), BF16),
            pltpu.VMEM((steps, SUMS, atoms), BF16),
            pltpu.VMEM((SUMS, 768), F32),
            pltpu.VMEM((2, 2, points, 2 * LANES), BF16),
            pltpu.VMEM((2 * LANES, atoms), BF16),
            pltpu.VMEM((2 * points, CHUNK), F32),
            pltpu.VMEM((2 * points, CHUNK), F32),
            pltpu.VMEM((3, 8, atoms), F32),
            pltpu.VMEM((6, 8, atoms), F32),
            pltpu.VMEM((8, atoms), F32),
            pltpu.VMEM((8, atoms), F32),
            pltpu.VMEM((3 * GROUP, here), F32),
            pltpu.VMEM((GROUP, 3 * GROUP, here), F32),
            pltpu.VMEM((3 * GROUP, here), F32),
            pltpu.VMEM((GROUP, 4, here), F32),
            pltpu.VMEM((GROUP, 4, here), F32),
            pltpu.SemaphoreType.DMA((9,)),
            pltpu.SemaphoreType.DMA((5, GROUP)),
            pltpu.SemaphoreType.DMA((5, GROUP)),
            pltpu.SemaphoreType.DMA((kvecs,)),
            pltpu.SemaphoreType.DMA((kvecs,)),
        ],
        compiler_params=pltpu.CompilerParams(
            collective_id=0, has_side_effects=True, vmem_limit_bytes=60 << 20
        ),
    )(
        positions.transpose(1, 0, 2),
        moments,
        adj_pos,
        final_momentum_adjoint,
        species.reshape(1, here),
        masses,
        kint.T,
        small,
        maps,
    )
    adj = last[4:7] - time_step * last[0:3]
    return adj, last[8:11] + time_step * adj


def solution(mesh):
    bricks, kvecs = mesh.shape["brick"], mesh.shape["kvec"]
    if bricks != GROUP:
        return plain(mesh)
    placed = (
        P(None, None, "brick"),
        P("brick", None),
        P(None, "brick"),
        P(None, "brick"),
        P("brick"),
        P(),
        P("kvec", None),
    )
    return jax.shard_map(
        functools.partial(fused, kvecs),
        mesh=mesh,
        in_specs=placed,
        out_specs=(P(None, "brick"), P(None, "brick")),
        check_vma=False,
    )
```
